32 devices in a mesh: grp: 2 (over x), seq: 8 (over z, y), tile: 2 (over core).
Axes of the slice: x: 2, y: 2, z: 4, core: 2. Of those that a mesh axis runs over, the one named last changes fastest.
Arguments:
- query_input: bfloat16 [4096, 4096], P(None, ('grp', 'seq', 'tile')), parts along dimension 1, may hold values from -6 to 6
- key_input: bfloat16 [4096, 4096], P(None, ('grp', 'seq', 'tile')), parts along dimension 1, may hold values from -6 to 6
- value_input: bfloat16 [4096, 4096], P(None, ('grp', 'seq', 'tile')), parts along dimension 1, may hold values from -6 to 6
- short_taps: float32 [3, 7, 4096], replicated, may hold values from -2 to 2
- long_filter: float32 [4096, 2048], P(('seq', 'tile')), may hold values from -4 to 4
- skip_gain: float32 [4096], P(('seq', 'tile')), may hold values from -4 to 4
- unembed: bfloat16 [4096, 512], replicated, may hold values from -0.25 to 0.25
- targets: int32 [4096], P(('grp', 'seq', 'tile')), parts along dimension 0, may hold values from 0 to 511
- rankings: int32 [64, 64], P(('grp', 'seq', 'tile')), parts along dimension 0, may hold values from 0 to 63, each once within a row
Outputs:
- hyena_out: bfloat16 [4096, 4096], P(None, ('grp', 'seq', 'tile')), parts along dimension 1
- list_loss: float32 [64], P(('grp', 'seq', 'tile')), parts along dimension 0
The draws below stay inside these ranges and needn't reach their ends.
There are 2 independent parts, one for each index of `grp`. The reference program is written for one: setup_inputs(seed, part) draws one part's arguments, and reference() takes and returns one part's arrays. A program takes and returns all parts, laid end to end along the dimension named above; an argument that names none is the same for every part. Nothing has to cross between parts.
Inputs may be any that keep to these rules, and one draw needn't show every extreme that they name: Each row of rankings holds every number from 0 to 63 once.
All inputs are finite; a program needn't handle non-finite values.
Results may differ from the reference program's by a relative error of at most 0.0058.
Values may be sent and summed in bfloat16 or wider, within the bound.
No kernel may reach another device: no remote copies, remote signals or barrier semaphores. Data moves between devices by JAX's collectives and lax.ppermute only.
A program may use at most 128 MiB of HBM per device.

```python
import math
import jax
import jax.numpy as jnp
from jax import lax

FEATURE_WIDTH = 4096
V = 512
WS = 7
K = 64
SEQUENCE_LENGTH = 2048
NBLK = 32


def draw_long_filter(key, part):
    lookup_matrix = jax.random.split(key, 7)
    lag_offsets = jnp.arange(SEQUENCE_LENGTH, dtype=jnp.float32)[None, :]
    fast_share = 0.5
    fast_mask = jax.random.uniform(lookup_matrix[0], (FEATURE_WIDTH, 1)) < fast_share
    fast_rate = jax.random.uniform(lookup_matrix[1], (FEATURE_WIDTH, 1), minval=1.0 / 50.0, maxval=1.0 / 30.0)
    slow_rate = jax.random.uniform(lookup_matrix[2], (FEATURE_WIDTH, 1), minval=0.1, maxval=1.0) / SEQUENCE_LENGTH
    decay_rate = jnp.where(fast_mask, fast_rate, slow_rate)
    impulse_location = jax.random.uniform(lookup_matrix[3], (FEATURE_WIDTH, 2)) * SEQUENCE_LENGTH
    impulse_kept_share = jax.random.uniform(lookup_matrix[4], (FEATURE_WIDTH, 2), minval=0.6, maxval=0.8)
    head_energy = jnp.expm1(-2.0 * decay_rate * SEQUENCE_LENGTH) / jnp.expm1(-2.0 * decay_rate)
    tail_share = jax.random.uniform(lookup_matrix[6], (FEATURE_WIDTH, 1), minval=0.06, maxval=0.12)
    floor_level = jnp.sqrt(tail_share * head_energy / SEQUENCE_LENGTH)
    fading_profile = jnp.exp(-decay_rate * lag_offsets) + floor_level
    for ordinal_numbers in range(2):
        fading_profile = fading_profile * jnp.where(lag_offsets >= impulse_location[:, ordinal_numbers:ordinal_numbers + 1], impulse_kept_share[:, ordinal_numbers:ordinal_numbers + 1], 1.0)
    energy = head_energy * (1.0 + tail_share)
    roughness = jnp.clip(jax.random.normal(lookup_matrix[5], (FEATURE_WIDTH, SEQUENCE_LENGTH)), -4.0, 4.0)
    return (fading_profile * roughness / jnp.sqrt(energy)).astype(jnp.float32)


def touch_ends(result, rng, low, largest):
    place = [jax.random.randint(jax.random.fold_in(rng, axis), (), 0, length) for axis, length in enumerate(result.shape)]
    widest = result.shape.index(max(result.shape))
    beside = place[:widest] + [(place[widest] + 1) % result.shape[widest]] + place[widest + 1:]
    return result.at[tuple(place)].set(low).at[tuple(beside)].set(largest)


def block_scale(key, dims, shards, smallest, largest):
    gain, own = 1.0, jax.random.fold_in(key, 6)
    for axis_at, parts in shards:
        steps = jnp.exp(jax.random.uniform(jax.random.fold_in(own, axis_at), (parts,), jnp.float32, smallest / len(shards), largest / len(shards)))
        gain = gain * jnp.repeat(steps, dims[axis_at] // parts).reshape([-1 if axis == axis_at else 1 for axis in range(len(dims))])
    return gain


def scatter_about(own_key, extent, spread, limit, cuts=(), kind=jnp.bfloat16):
    loudness = block_scale(own_key, extent, cuts, -0.22, 0.18) if cuts else 1.0
    result = jax.random.normal(own_key, extent, jnp.float32) * spread * loudness
    return jnp.minimum(jnp.maximum(result, -limit), limit).astype(kind)


def setup_inputs(seed: int = 0, part: int = 0) -> dict:
    splits = jax.random.split(jax.random.key(seed), 10)
    own_keys = jax.random.split(jax.random.fold_in(splits[9], part), 10)
    return {
        "query_input": scatter_about(own_keys[0], (FEATURE_WIDTH, SEQUENCE_LENGTH), 1.0, 6.0, ((1, 16),)),
        "key_input": scatter_about(own_keys[1], (FEATURE_WIDTH, SEQUENCE_LENGTH), 1.0, 6.0, ((1, 16),)),
        "value_input": scatter_about(own_keys[2], (FEATURE_WIDTH, SEQUENCE_LENGTH), 1.0, 6.0, ((1, 16),)),
        "short_taps": scatter_about(splits[3], (3, WS, FEATURE_WIDTH), WS ** -0.5, 2.0, (), jnp.float32),
        "long_filter": draw_long_filter(jax.random.fold_in(splits[9], 71), part),
        "skip_gain": scatter_about(splits[5], (FEATURE_WIDTH,), 0.25, 4.0, ((0, 16),), jnp.float32),
        "unembed": scatter_about(splits[6], (FEATURE_WIDTH, V), (FEATURE_WIDTH // 9) ** -0.5, 0.25),
        "targets": touch_ends(jax.random.randint(own_keys[7], (SEQUENCE_LENGTH,), 0, V), jax.random.fold_in(own_keys[7], 1), 0, V - 1).astype(jnp.int32),
        "rankings": jax.vmap(lambda own: jax.random.permutation(own, K))(jax.random.split(own_keys[8], NBLK)).reshape((NBLK, K)).astype(jnp.int32),
    }


soft_cap = 5.0


def short_filter(signal, tap_rows):
    width = tap_rows.shape[0]
    length = signal.shape[1]
    padded = jnp.pad(signal.astype(jnp.float32), ((0, 0), (width - 1, 0)))
    running = jnp.zeros((signal.shape[0], length), jnp.float32)
    for offset in range(width):
        begin = width - 1 - offset
        running = running + tap_rows[offset][:, None] * padded[:, begin:begin + length]
    return running


def long_convolution(gated_wide, long_filter):
    block_size = math.gcd(FEATURE_WIDTH, 256)
    total_len = 2 * SEQUENCE_LENGTH

    def convolve_group(operands):
        signal, taps = operands
        spectrum = jnp.fft.rfft(signal, n=total_len, axis=-1) * jnp.fft.rfft(taps, n=total_len, axis=-1)
        return jnp.fft.irfft(spectrum, n=total_len, axis=-1)[:, :SEQUENCE_LENGTH]

    grouped = lax.map(convolve_group, (gated_wide.reshape(FEATURE_WIDTH // block_size, block_size, SEQUENCE_LENGTH), long_filter.reshape(FEATURE_WIDTH // block_size, block_size, SEQUENCE_LENGTH)))
    return grouped.reshape(FEATURE_WIDTH, SEQUENCE_LENGTH)


def plackett_luce(score, rankings):
    listed = score.reshape(rankings.shape)
    ranked = jnp.take_along_axis(listed, rankings, axis=1)
    weights = jnp.exp(ranked)
    mass = jnp.flip(jnp.cumsum(jnp.flip(weights, 1), axis=1), 1)
    return jnp.mean(jnp.log(mass) - ranked, axis=1)


def reference(query_input, key_input, value_input, short_taps, long_filter, skip_gain, unembed, targets, rankings):
    query_short = short_filter(query_input, short_taps[0])
    key_short = short_filter(key_input, short_taps[1])
    value_short = short_filter(value_input, short_taps[2])
    gated = lax.optimization_barrier((key_short * value_short).astype(jnp.bfloat16))
    gated_wide = gated.astype(jnp.float32)
    history = long_convolution(gated_wide, long_filter)
    carried = lax.optimization_barrier((history + skip_gain[:, None] * gated_wide).astype(jnp.bfloat16))
    hyena_out = (query_short * carried.astype(jnp.float32)).astype(jnp.bfloat16)
    picked = jnp.take(unembed, targets, axis=1)
    logit = jnp.sum(hyena_out.astype(jnp.float32) * picked.astype(jnp.float32), axis=0)
    score = soft_cap * jnp.tanh(logit / soft_cap)
    list_loss = plackett_luce(score, rankings)
    return hyena_out, list_loss
```

```python
import functools
import math

import jax
import jax.numpy as jnp
import numpy as np
from jax import lax
from jax.experimental import pallas as pl
from jax.experimental.pallas import tpu as pltpu
from jax.sharding import PartitionSpec as P

soft_cap = 5.0
token_axes = ("seq", "tile")
bf16 = jnp.bfloat16
f32 = jnp.float32
rim = 8
mebibyte = 1 << 20


def params(limit=48):
    return pltpu.CompilerParams(vmem_limit_bytes=limit * mebibyte)


def cost(flops, size):
    return pl.CostEstimate(flops=flops, bytes_accessed=size, transcendentals=0)


def dot(a, b, over):
    return lax.dot_general(a, b, ((over[0], over[1]), ((), ())), preferred_element_type=f32)


def passed_along(block, axis, distance):
    devices = range(lax.axis_size(axis))
    route = [(i - distance, i) for i in devices if i - distance in devices]
    return lax.ppermute(block, axis, route)


def c_mul(z, angle):
    re, im = z
    turns = angle / (math.pi / 4)
    nearest = round(turns)
    if abs(turns - nearest) < 1e-9:
        eighth = nearest % 8
        if eighth == 0:
            return (re, im)
        if eighth == 2:
            return (-im, re)
        if eighth == 4:
            return (-re, -im)
        if eighth == 6:
            return (im, -re)
        half = math.sqrt(0.5)
        if eighth == 1:
            return ((re - im) * half, (re + im) * half)
        if eighth == 3:
            return ((re + im) * -half, (re - im) * half)
        if eighth == 5:
            return ((im - re) * half, (re + im) * -half)
        return ((re + im) * half, (im - re) * half)
    c, s = math.cos(angle), math.sin(angle)
    return (re * c - im * s, re * s + im * c)


def c_add(a, b):
    return (a[0] + b[0], a[1] + b[1])


def c_sub(a, b):
    return (a[0] - b[0], a[1] - b[1])


def c_dft(z, sign):
    n = len(z)
    if n == 1:
        return list(z)
    even = c_dft(z[0::2], sign)
    odd = c_dft(z[1::2], sign)
    turned = [c_mul(o, sign * 2 * math.pi * p / n) for p, o in enumerate(odd)]
    return [c_add(e, o) for e, o in zip(even, turned)] + [c_sub(e, o) for e, o in zip(even, turned)]


def odd_dft(x):
    n = len(x)
    if n == 1:
        return [(x[0], None)]
    half = n // 2
    z = [c_mul((x[j], -x[j + half]), -math.pi * j / n) for j in range(half)]
    wide = c_dft(z, -1)
    out = []
    for m in range(half):
        if m % 2 == 0:
            out.append(wide[m // 2])
        else:
            re, im = wide[(n - 1 - m) // 2]
            out.append((re, -im))
    return out


def real_dft(x):
    n = len(x)
    if n == 1:
        return [(x[0], None)]
    half = n // 2
    even = real_dft([x[j] + x[j + half] for j in range(half)])
    odd = odd_dft([x[j] - x[j + half] for j in range(half)])
    out = [None] * (half + 1)
    out[0::2] = even if half > 1 else [even[0]]
    out[1::2] = odd
    return out


def padded_real_dft(x):
    n = len(x)
    out = [None] * (n + 1)
    out[0::2] = real_dft(x)
    out[1::2] = odd_dft(x)
    return out


def odd_dft_adjoint(y):
    half = len(y)
    if y[0][1] is None:
        return [y[0][0]]
    n = 2 * half
    wide = []
    for p in range(half):
        if 2 * p < half:
            wide.append(y[2 * p])
        else:
            re, im = y[n - 1 - 2 * p]
            wide.append((re, -im))
    z = c_dft(wide, 1)
    turned = [c_mul(value, math.pi * j / n) for j, value in enumerate(z)]
    return [u[0] for u in turned] + [-u[1] for u in turned]


def real_dft_adjoint(x):
    if len(x) == 1:
        return [x[0][0]]
    even = real_dft_adjoint(x[0::2])
    odd = odd_dft_adjoint(x[1::2])
    return [e + o for e, o in zip(even, odd)] + [e - o for e, o in zip(even, odd)]


def padded_real_dft_adjoint(x):
    even = real_dft_adjoint(x[0::2])
    odd = odd_dft_adjoint(x[1::2])
    return [e + o for e, o in zip(even, odd)]


def rim_picker(lanes):
    row = lax.broadcasted_iota(jnp.int32, (rim, lanes), 0)
    lane = lax.broadcasted_iota(jnp.int32, (rim, lanes), 1)
    return (lane == row + (lanes - rim)).astype(bf16)


def rim_kernel(k_ref, v_ref, q_ref, kv_ref, qo_ref):
    picker = rim_picker(k_ref.shape[1])

    def last(ref):
        return dot(picker, ref[...], ((1,), (1,)))

    kv_ref[...] = jnp.concatenate([last(k_ref), last(v_ref)], axis=0).astype(bf16)
    qo_ref[...] = last(q_ref).astype(bf16)


def rims(key_input, value_input, query_input):
    channels, tokens = key_input.shape
    rows = min(channels, 1024)
    block = pl.BlockSpec((rows, tokens), lambda i: (i, 0))
    return pl.pallas_call(
        rim_kernel,
        grid=(channels // rows,),
        in_specs=[block] * 3,
        out_specs=[
            pl.BlockSpec((2 * rim, rows), lambda i: (0, i)),
            pl.BlockSpec((rim, rows), lambda i: (0, i)),
        ],
        out_shape=[
            jax.ShapeDtypeStruct((2 * rim, channels), bf16),
            jax.ShapeDtypeStruct((rim, channels), bf16),
        ],
        compiler_params=params(),
        cost_estimate=cost(6 * channels * tokens * rim, 6 * channels * tokens),
        name="rims",
    )(key_input, value_input, query_input)


step_rows = 16


def short_conv(x, before, taps):
    rows, lanes = x.shape
    width = taps.shape[0]
    tail = dot(before, rim_picker(lanes), ((0,), (0,)))
    padded = jnp.concatenate([taps, jnp.zeros((8 - width, rows), f32)], axis=0)
    columns = padded.T
    lane = lax.broadcasted_iota(jnp.int32, (step_rows, lanes), 1)
    out = []
    for begin in range(0, rows, step_rows):
        part = slice(begin, begin + step_rows)
        here = x[part].astype(f32)
        there = tail[part]
        total = columns[part, 0:1] * here
        for offset in range(1, width):
            moved = pltpu.roll(jnp.where(lane < lanes - offset, here, there), offset, 1)
            total = total + columns[part, offset : offset + 1] * moved
        out.append(total)
    return out


def gated_kernel(k_ref, v_ref, before_ref, taps_k_ref, taps_v_ref, out_ref):
    before = before_ref[...].astype(f32)
    key_short = short_conv(k_ref[0], before[:rim].astype(bf16), taps_k_ref[0])
    value_short = short_conv(v_ref[0], before[rim:].astype(bf16), taps_v_ref[0])
    for at, (k, v) in enumerate(zip(key_short, value_short)):
        out_ref[0, at * step_rows : (at + 1) * step_rows] = (k * v).astype(bf16)


def gated_features(key_input, value_input, before, short_taps):
    channels, tokens = key_input.shape
    width = short_taps.shape[1]
    rows = min(channels, 256)
    count = channels // rows
    block = pl.BlockSpec((1, rows, tokens), lambda i: (i, 0, 0))
    return pl.pallas_call(
        gated_kernel,
        grid=(count,),
        in_specs=[
            block,
            block,
            pl.BlockSpec((2 * rim, rows), lambda i: (0, i)),
            pl.BlockSpec((1, width, rows), lambda i: (1, 0, i)),
            pl.BlockSpec((1, width, rows), lambda i: (2, 0, i)),
        ],
        out_specs=block,
        out_shape=jax.ShapeDtypeStruct((count, rows, tokens), bf16),
        compiler_params=params(),
        cost_estimate=cost(28 * channels * tokens, 6 * channels * tokens),
        name="gated",
    )(
        key_input.reshape(count, rows, tokens),
        value_input.reshape(count, rows, tokens),
        before,
        short_taps,
        short_taps,
    )


def halves(x):
    high = x.astype(bf16)
    return high, (x - high.astype(f32)).astype(bf16)


def put_spectrum(spectrum, high_ref, low_ref, rows, lanes):
    for at, (re, im) in enumerate(spectrum):
        high, low = halves(re)
        high_ref[at, rows, :lanes] = high
        low_ref[at, rows, :lanes] = low
        if im is None:
            high, low = jnp.zeros_like(high), jnp.zeros_like(low)
        else:
            high, low = halves(im)
        high_ref[at, rows, lanes:] = high
        low_ref[at, rows, lanes:] = low


def three_pass(ah, al, wh, wl, over):
    return dot(ah, wh, over) + (dot(al, wh, over) + dot(ah, wl, over))


def filter_kernel(taps_ref, skip_ref, base_ref, turn_ref, spec_ref, wh_ref, wl_ref, ah, al):
    channels = taps_ref.shape[0]
    lanes = base_ref.shape[1]
    blocks = taps_ref.shape[1] // lanes
    skip = jnp.broadcast_to(skip_ref[...], (8, channels)).T
    lane = lax.broadcasted_iota(jnp.int32, (step_rows, lanes), 1)
    for step in range(channels // step_rows):
        rows = slice(step * step_rows, (step + 1) * step_rows)
        x = [taps_ref[rows, j * lanes : (j + 1) * lanes] for j in range(blocks)]
        x[0] = x[0] + jnp.where(lane == 0, skip[rows, 0:1], 0.0)
        put_spectrum(padded_real_dft(x), ah, al, rows, lanes)

    base_c, base_s = base_ref[0], base_ref[1]

    @pl.loop(0, blocks + 1)
    def _(k):
        turn_c, turn_s = turn_ref[0, k].T[:, 0:1], turn_ref[1, k].T[:, 0:1]
        c = turn_c * base_c - turn_s * base_s
        s = turn_s * base_c + turn_c * base_s
        ch, cl = halves(c)
        sh, sl = halves(s)
        for ref, cc, ss in ((wh_ref, ch, sh), (wl_ref, cl, sl)):
            ref[k, :lanes, :lanes] = cc
            ref[k, :lanes, lanes:] = -ss
            ref[k, lanes:, :lanes] = ss
            ref[k, lanes:, lanes:] = cc
        scale = jnp.where((k == 0) | (k == blocks), 1.0, 2.0) / (2 * blocks * lanes)
        spec_ref[k] = three_pass(ah[k], al[k], wh_ref[k], wl_ref[k], ((1,), (0,))) * scale


def filter_spectrum(long_filter, skip_gain, lanes):
    channels, length = long_filter.shape
    blocks = length // lanes
    count = blocks + 1
    period = 2 * length
    s = np.arange(lanes)
    base = 2 * np.pi * (s[:, None] * s[None, :] % lanes) / lanes
    turn = 2 * np.pi * (np.arange(count)[:, None] * s[None, :] % period) / period
    base = np.stack([np.cos(base), np.sin(base)]).astype(np.float32)
    turn = np.stack([np.cos(turn), np.sin(turn)]).astype(np.float32)
    turn = np.broadcast_to(turn[:, :, None, :], (2, count, 8, lanes))
    whole = pl.BlockSpec(memory_space=pltpu.VMEM)
    return pl.pallas_call(
        filter_kernel,
        in_specs=[whole] * 4,
        out_specs=[whole] * 3,
        out_shape=[
            jax.ShapeDtypeStruct((count, channels, 2 * lanes), f32),
            jax.ShapeDtypeStruct((count, 2 * lanes, 2 * lanes), bf16),
            jax.ShapeDtypeStruct((count, 2 * lanes, 2 * lanes), bf16),
        ],
        scratch_shapes=[
            pltpu.VMEM((count, channels, 2 * lanes), bf16),
            pltpu.VMEM((count, channels, 2 * lanes), bf16),
        ],
        compiler_params=params(),
        cost_estimate=cost(6 * count * channels * 4 * lanes * lanes, 12 * count * channels * lanes),
        name="filter_spectrum",
    )(long_filter, skip_gain.reshape(1, channels), jnp.asarray(base), jnp.asarray(turn))


def long_kernel(x_ref, spec_ref, wh_ref, wl_ref, out_ref, ah, al, back):
    blocks, channels, lanes = x_ref.shape

    @pl.loop(0, channels // step_rows)
    def _(step):
        rows = pl.ds(pl.multiple_of(step * step_rows, step_rows), step_rows)
        x = [x_ref[j, rows].astype(f32) for j in range(blocks)]
        put_spectrum(padded_real_dft(x), ah, al, rows, lanes)

    @pl.loop(0, blocks + 1)
    def _(k):
        x = three_pass(ah[k], al[k], wh_ref[k], wl_ref[k], ((1,), (0,)))
        spec = spec_ref[k]
        xr, xi = x[:, :lanes], x[:, lanes:]
        fr, fi = spec[:, :lanes], spec[:, lanes:]
        product = jnp.concatenate([xr * fr - xi * fi, xr * fi + xi * fr], axis=1)
        high, low = halves(product)
        back[k] = three_pass(high, low, wh_ref[k], wl_ref[k], ((1,), (1,)))

    @pl.loop(0, channels // step_rows)
    def _(step):
        rows = pl.ds(pl.multiple_of(step * step_rows, step_rows), step_rows)
        spectrum = []
        for k in range(blocks + 1):
            im = None if k in (0, blocks) else back[k, rows, lanes:]
            spectrum.append((back[k, rows, :lanes], im))
        for j, y in enumerate(padded_real_dft_adjoint(spectrum)):
            out_ref[j, rows] = y.astype(bf16)


def long_convolution(arrived, spec, wh, wl):
    blocks, channels, lanes = arrived.shape
    count = blocks + 1
    whole = pl.BlockSpec(memory_space=pltpu.VMEM)
    return pl.pallas_call(
        long_kernel,
        in_specs=[whole] * 4,
        out_specs=whole,
        out_shape=jax.ShapeDtypeStruct(arrived.shape, bf16),
        scratch_shapes=[
            pltpu.VMEM((count, channels, 2 * lanes), bf16),
            pltpu.VMEM((count, channels, 2 * lanes), bf16),
            pltpu.VMEM((count, channels, 2 * lanes), f32),
        ],
        compiler_params=params(),
        cost_estimate=cost(12 * count * channels * 4 * lanes * lanes, 12 * count * channels * lanes),
        name="long_convolution",
    )(arrived, spec, wh, wl)


def query_kernel(q_ref, before_ref, taps_ref, unembed_ref, targets_ref, ranks_ref, qs_ref, picked_ref, after_ref):
    parts = short_conv(q_ref[...], before_ref[...], taps_ref[0])
    for at, part in enumerate(parts):
        qs_ref[at * step_rows : (at + 1) * step_rows] = part
    tokens = q_ref.shape[1]
    vocabulary = unembed_ref.shape[1]
    word = lax.broadcasted_iota(jnp.int32, (vocabulary, tokens), 0)
    chosen = (word == targets_ref[...]).astype(bf16)
    picked_ref[...] = dot(unembed_ref[...], chosen, ((1,), (0,))).astype(bf16)

    @pl.when(pl.program_id(0) == 0)
    def _():
        lists, size = ranks_ref.shape
        token = lax.broadcasted_iota(jnp.int32, (size, size), 0)
        rank = lax.broadcasted_iota(jnp.int32, (size, size), 1).astype(f32)
        at = [
            jnp.sum(jnp.where(token == ranks_ref[b : b + 1, :], rank, 0.0), axis=1, keepdims=True)
            for b in range(lists)
        ]
        column = jnp.concatenate(at, axis=0)
        row_of = lax.broadcasted_iota(jnp.int32, (tokens, tokens), 0)
        col_of = lax.broadcasted_iota(jnp.int32, (tokens, tokens), 1)
        row = jnp.sum(jnp.where(row_of == col_of, column, 0.0), axis=0, keepdims=True)
        same = row_of // size == col_of // size
        after_ref[...] = jnp.where(same & (row >= column), 1.0, 0.0)


def query_side(query_input, before, short_taps, unembed, targets, rankings):
    channels, tokens = query_input.shape
    width = short_taps.shape[1]
    vocabulary = unembed.shape[1]
    rows = min(channels, 256)
    block = pl.BlockSpec((rows, tokens), lambda i: (i, 0))
    return pl.pallas_call(
        query_kernel,
        grid=(channels // rows,),
        in_specs=[
            block,
            pl.BlockSpec((rim, rows), lambda i: (0, i)),
            pl.BlockSpec((1, width, rows), lambda i: (0, 0, i)),
            pl.BlockSpec((rows, vocabulary), lambda i: (i, 0)),
            pl.BlockSpec((1, tokens), lambda i: (0, 0)),
            pl.BlockSpec(rankings.shape, lambda i: (0, 0)),
        ],
        out_specs=[block, block, pl.BlockSpec((tokens, tokens), lambda i: (0, 0))],
        out_shape=[
            jax.ShapeDtypeStruct((channels, tokens), f32),
            jax.ShapeDtypeStruct((channels, tokens), bf16),
            jax.ShapeDtypeStruct((tokens, tokens), f32),
        ],
        compiler_params=params(),
        cost_estimate=cost(2 * channels * tokens * (vocabulary + 7), channels * (8 * tokens + 2 * vocabulary)),
        name="query_side",
    )(query_input, before, short_taps, unembed, targets.reshape(1, tokens), rankings)


def result_kernel(size, carried_ref, qs_ref, picked_ref, after_ref, out_ref, loss_ref, total):
    rows, tokens = carried_ref.shape
    out = (qs_ref[...] * carried_ref[...].astype(f32)).astype(bf16)
    out_ref[...] = out
    terms = out.astype(f32) * picked_ref[...].astype(f32)
    terms = jnp.sum(terms.reshape(rows // 8, 8, tokens), axis=0)

    @pl.when(pl.program_id(0) == 0)
    def _():
        total[...] = terms

    @pl.when(pl.program_id(0) > 0)
    def _():
        total[...] += terms

    @pl.when(pl.program_id(0) == pl.num_programs(0) - 1)
    def _():
        logit = jnp.sum(total[...], axis=0, keepdims=True)
        score = soft_cap * jnp.tanh(logit / soft_cap)
        mass = jnp.sum(after_ref[...] * jnp.exp(score), axis=1, keepdims=True)
        level = jnp.log(mass)
        lists = tokens // size
        lane = lax.broadcasted_iota(jnp.int32, (1, lists), 1)
        losses = jnp.zeros((1, lists), f32)
        for b in range(lists):
            part = slice(b * size, (b + 1) * size)
            own = jnp.sum(level[part]) - jnp.sum(score[:, part])
            losses = jnp.where(lane == b, own / size, losses)
        loss_ref[...] = losses


def result(carried, query_short, picked, after, lists):
    channels, tokens = carried.shape
    rows = min(channels, 1024)
    block = pl.BlockSpec((rows, tokens), lambda i: (i, 0))
    return pl.pallas_call(
        functools.partial(result_kernel, tokens // lists),
        grid=(channels // rows,),
        in_specs=[block, block, block, pl.BlockSpec((tokens, tokens), lambda i: (0, 0))],
        out_specs=[block, pl.BlockSpec((1, lists), lambda i: (0, 0))],
        out_shape=[
            jax.ShapeDtypeStruct((channels, tokens), bf16),
            jax.ShapeDtypeStruct((1, lists), f32),
        ],
        scratch_shapes=[pltpu.VMEM((8, tokens), f32)],
        compiler_params=params(),
        cost_estimate=cost(4 * channels * tokens, 10 * channels * tokens),
        name="result",
    )(carried, query_short, picked, after)


def per_device(
    query_input,
    key_input,
    value_input,
    short_taps,
    long_filter,
    skip_gain,
    unembed,
    targets,
    rankings,
):
    channels, tokens = query_input.shape
    owners = lax.axis_size(token_axes)
    local = channels // owners
    rim_kv, rim_q = rims(key_input, value_input, query_input)
    before_kv = passed_along(rim_kv, token_axes, 1)
    before_q = passed_along(rim_q, token_axes, 1)
    gated = gated_features(key_input, value_input, before_kv, short_taps)
    arrived = lax.all_to_all(gated.reshape(owners, local, tokens), token_axes, 0, 0, tiled=True)
    spec, wh, wl = filter_spectrum(long_filter, skip_gain, tokens)
    query_short, picked, after = query_side(
        query_input, before_q, short_taps, unembed, targets, rankings
    )
    carried = long_convolution(arrived, spec, wh, wl)
    returned = lax.all_to_all(carried, token_axes, 0, 0, tiled=True)
    out, losses = result(
        returned.reshape(channels, tokens), query_short, picked, after, rankings.shape[0]
    )
    return out, losses.reshape(rankings.shape[0])


def solution(mesh):
    placed = (
        P(None, ("grp", "seq", "tile")),
        P(None, ("grp", "seq", "tile")),
        P(None, ("grp", "seq", "tile")),
        P(),
        P(("seq", "tile"), None),
        P(("seq", "tile")),
        P(),
        P(("grp", "seq", "tile")),
        P(("grp", "seq", "tile"), None),
    )
    return jax.shard_map(
        per_device,
        mesh=mesh,
        in_specs=placed,
        out_specs=(P(None, ("grp", "seq", "tile")), P(("grp", "seq", "tile"))),
        check_vma=False,
    )
```

```python
import functools
import math

import jax
import jax.numpy as jnp
import ml_dtypes
import numpy as np
from jax import lax
from jax.experimental import pallas as pl
from jax.experimental.pallas import tpu as pltpu
from jax.sharding import PartitionSpec as P

soft_cap = 5.0
token_axes = ("seq", "tile")
bf16 = jnp.bfloat16
f32 = jnp.float32
rim = 8
most_chunks = 1
mebibyte = 1 << 20


whole = pl.BlockSpec(memory_space=pltpu.VMEM)
outside = pl.BlockSpec(memory_space=pltpu.HBM)


def in_hbm(x):
    return pltpu.with_memory_space_constraint(x, pltpu.HBM)


def params(limit=48):
    return pltpu.CompilerParams(vmem_limit_bytes=limit * mebibyte)


def cost(flops, size):
    return pl.CostEstimate(flops=flops, bytes_accessed=size, transcendentals=0)


def dot(a, b, over):
    return lax.dot_general(a, b, ((over[0], over[1]), ((), ())), preferred_element_type=f32)


def passed_along(block, axis, distance):
    devices = range(lax.axis_size(axis))
    route = [(i - distance, i) for i in devices if i - distance in devices]
    return lax.ppermute(block, axis, route)


def c_mul(z, angle):
    re, im = z
    turns = angle / (math.pi / 4)
    nearest = round(turns)
    if abs(turns - nearest) < 1e-9:
        eighth = nearest % 8
        if eighth == 0:
            return (re, im)
        if eighth == 2:
            return (-im, re)
        if eighth == 4:
            return (-re, -im)
        if eighth == 6:
            return (im, -re)
        half = math.sqrt(0.5)
        if eighth == 1:
            return ((re - im) * half, (re + im) * half)
        if eighth == 3:
            return ((re + im) * -half, (re - im) * half)
        if eighth == 5:
            return ((im - re) * half, (re + im) * -half)
        return ((re + im) * half, (im - re) * half)
    c, s = math.cos(angle), math.sin(angle)
    return (re * c - im * s, re * s + im * c)


def c_add(a, b):
    return (a[0] + b[0], a[1] + b[1])


def c_sub(a, b):
    return (a[0] - b[0], a[1] - b[1])


def c_dft(z, sign):
    n = len(z)
    if n == 1:
        return list(z)
    even = c_dft(z[0::2], sign)
    odd = c_dft(z[1::2], sign)
    turned = [c_mul(o, sign * 2 * math.pi * p / n) for p, o in enumerate(odd)]
    return [c_add(e, o) for e, o in zip(even, turned)] + [c_sub(e, o) for e, o in zip(even, turned)]


def odd_dft(x):
    n = len(x)
    if n == 1:
        return [(x[0], None)]
    half = n // 2
    z = [c_mul((x[j], -x[j + half]), -math.pi * j / n) for j in range(half)]
    wide = c_dft(z, -1)
    out = []
    for m in range(half):
        if m % 2 == 0:
            out.append(wide[m // 2])
        else:
            re, im = wide[(n - 1 - m) // 2]
            out.append((re, -im))
    return out


def real_dft(x):
    n = len(x)
    if n == 1:
        return [(x[0], None)]
    half = n // 2
    even = real_dft([x[j] + x[j + half] for j in range(half)])
    odd = odd_dft([x[j] - x[j + half] for j in range(half)])
    out = [None] * (half + 1)
    out[0::2] = even if half > 1 else [even[0]]
    out[1::2] = odd
    return out


def padded_real_dft(x):
    n = len(x)
    out = [None] * (n + 1)
    out[0::2] = real_dft(x)
    out[1::2] = odd_dft(x)
    return out


def odd_dft_adjoint(y):
    half = len(y)
    if y[0][1] is None:
        return [y[0][0]]
    n = 2 * half
    wide = []
    for p in range(half):
        if 2 * p < half:
            wide.append(y[2 * p])
        else:
            re, im = y[n - 1 - 2 * p]
            wide.append((re, -im))
    z = c_dft(wide, 1)
    turned = [c_mul(value, math.pi * j / n) for j, value in enumerate(z)]
    return [u[0] for u in turned] + [-u[1] for u in turned]


def real_dft_adjoint(x):
    if len(x) == 1:
        return [x[0][0]]
    even = real_dft_adjoint(x[0::2])
    odd = odd_dft_adjoint(x[1::2])
    return [e + o for e, o in zip(even, odd)] + [e - o for e, o in zip(even, odd)]


def padded_real_dft_adjoint(x):
    even = real_dft_adjoint(x[0::2])
    odd = odd_dft_adjoint(x[1::2])
    return [e + o for e, o in zip(even, odd)]


tile = 128


def rim_kernel(q_ref, k_ref, v_ref, out_ref, held, sems):
    pieces = sems.shape[1]
    channels, lanes = q_ref.shape
    rows = channels // pieces
    copies = [
        [
            pltpu.make_async_copy(
                ref.at[p * rows : (p + 1) * rows], held.at[a, p * rows : (p + 1) * rows], sems.at[a, p]
            )
            for a, ref in enumerate((q_ref, k_ref, v_ref))
        ]
        for p in range(pieces)
    ]
    for group in copies:
        for copy in group:
            copy.start()
    row = lax.broadcasted_iota(jnp.int32, (rim, lanes), 0)
    lane = lax.broadcasted_iota(jnp.int32, (rim, lanes), 1)
    picker = (lane == row + (lanes - rim)).astype(bf16)
    for p, group in enumerate(copies):
        for copy in group:
            copy.wait()
        part = slice(p * rows, (p + 1) * rows)
        last = [dot(picker, held[a, part], ((1,), (1,))) for a in range(3)]
        out_ref[:, part] = jnp.concatenate(last, axis=0).astype(bf16)


def rims(query_input, key_input, value_input):
    channels, tokens = key_input.shape
    pieces = 2
    return pl.pallas_call(
        rim_kernel,
        in_specs=[outside] * 3,
        out_specs=whole,
        out_shape=jax.ShapeDtypeStruct((3 * rim, channels), bf16),
        scratch_shapes=[
            pltpu.VMEM((3, channels, tokens), bf16),
            pltpu.SemaphoreType.DMA((3, pieces)),
        ],
        compiler_params=params(6),
        cost_estimate=cost(6 * channels * tokens * rim, 6 * channels * tokens),
        name="rims",
    )(in_hbm(query_input), in_hbm(key_input), in_hbm(value_input))


def short_conv(x, before, taps_ref, which, lanes, space):
    tokens = x.shape[1]
    space[:rim] = before
    space[rim:] = x.astype(f32).T
    width = taps_ref.shape[1]
    taps = [
        jnp.broadcast_to(taps_ref[which, offset : offset + 1, lanes], (8, tile)) for offset in range(width)
    ]
    out = []
    for begin in range(0, tokens, 8):
        total = taps[0] * space[rim + begin : rim + begin + 8]
        for offset in range(1, width):
            first = rim + begin - offset
            total = total + taps[offset] * space[first : first + 8]
        out.append(total)
    return out


def aligned(start, size):
    return pl.ds(pl.multiple_of(start, size), size)


def gated_kernel(
    chunk, k_ref, v_ref, before_ref, taps_out, out_ref, held, made, key_space, value_space, taps_ref, sems, taps_sem
):
    owners, per, tokens = made.shape
    local = k_ref.shape[1]
    groups = sems.shape[1]
    size = owners // groups
    first = chunk * per
    loads, stores = [], []
    for g in range(groups):
        part = slice(g * size, (g + 1) * size)
        loads.append(
            [
                pltpu.make_async_copy(ref.at[part, first : first + per], held.at[a, part], sems.at[a, g])
                for a, ref in enumerate((k_ref, v_ref))
            ]
        )
        stores.append(pltpu.make_async_copy(made.at[part], out_ref.at[part], sems.at[2, g]))
    taps_load = pltpu.make_async_copy(taps_out, taps_ref, taps_sem)
    taps_load.start()
    for pair in loads:
        for copy in pair:
            copy.start()
    taps_load.wait()
    tiles = per // tile
    for g in range(groups):
        for copy in loads[g]:
            copy.wait()

        @pl.loop(0, size * tiles, unroll=4)
        def _(at):
            owner = g * size + at // tiles
            row = at % tiles * tile
            rows = aligned(row, tile)
            lanes = aligned(owner * local + first + row, tile)
            before = before_ref[:, lanes].astype(f32)
            key_short = short_conv(
                held[0, owner, rows], before[rim : 2 * rim], taps_ref, 1, lanes, key_space.at[at % 2]
            )
            value_short = short_conv(
                held[1, owner, rows], before[2 * rim :], taps_ref, 2, lanes, value_space.at[at % 2]
            )
            made[owner, rows] = jnp.concatenate([k * v for k, v in zip(key_short, value_short)], 0).T.astype(bf16)

        stores[g].start()
    for copy in stores:
        copy.wait()


def gated_features(chunk, chunks, key_input, value_input, before, short_taps, owners):
    channels, tokens = key_input.shape
    if chunks == 1:
        owners = channels // tile
    local = channels // owners
    per = local // chunks
    groups = math.gcd(owners, 4)
    return pl.pallas_call(
        functools.partial(gated_kernel, chunk),
        in_specs=[outside, outside, whole, outside],
        out_specs=outside,
        out_shape=jax.ShapeDtypeStruct((owners, per, tokens), bf16),
        scratch_shapes=[
            pltpu.VMEM((2, owners, per, tokens), bf16),
            pltpu.VMEM((owners, per, tokens), bf16),
            pltpu.VMEM((2, rim + tokens, tile), f32),
            pltpu.VMEM((2, rim + tokens, tile), f32),
            pltpu.VMEM(short_taps.shape, f32),
            pltpu.SemaphoreType.DMA((3, groups)),
            pltpu.SemaphoreType.DMA,
        ],
        compiler_params=params(8),
        cost_estimate=cost(28 * channels * tokens // chunks, 6 * channels * tokens // chunks),
        name="gated",
    )(
        in_hbm(key_input.reshape(owners, local, tokens)),
        in_hbm(value_input.reshape(owners, local, tokens)),
        before,
        in_hbm(short_taps),
    )


step_rows = 16


def halves(x):
    high = x.astype(bf16)
    return high, (x - high.astype(f32)).astype(bf16)


def put_spectrum(spectrum, turn_ref, high_ref, low_ref, rows, lanes):
    for at, (re, im) in enumerate(spectrum):
        if at == 0:
            im = jnp.zeros_like(re)
        else:
            c, s = turn_ref[0, at : at + 1], turn_ref[1, at : at + 1]
            if im is None:
                re, im = re * c, -(re * s)
            else:
                re, im = re * c + im * s, im * c - re * s
        for value, part in ((re, slice(0, lanes)), (im, slice(lanes, 2 * lanes))):
            high, low = halves(value)
            high_ref[at, rows, part] = high
            low_ref[at, rows, part] = low


def three_pass(ah, al, wh, wl, over):
    return dot(ah, wh, over) + (dot(al, wh, over) + dot(ah, wl, over))


def over_frequencies(count, body):
    if count <= 33:
        for k in range(count):
            body(k)
    else:
        pl.loop(0, count)(body)


def filter_kernel(taps_ref, skip_ref, table_ref, *rest):
    *spec_refs, ah, al, turn_ref = rest
    put_turns(turn_ref)
    channels = taps_ref.shape[0]
    lanes = turn_ref.shape[2]
    blocks = taps_ref.shape[1] // lanes
    skip = jnp.broadcast_to(skip_ref[...], (8, channels)).T
    lane = lax.broadcasted_iota(jnp.int32, (step_rows, lanes), 1)
    for step in range(channels // step_rows):
        rows = slice(step * step_rows, (step + 1) * step_rows)
        x = [taps_ref[rows, j * lanes : (j + 1) * lanes] for j in range(blocks)]
        x[0] = x[0] + jnp.where(lane == 0, skip[rows, 0:1], 0.0)
        put_spectrum(padded_real_dft(x), turn_ref, ah, al, rows, lanes)
    per = channels // len(spec_refs)

    def one(k):
        ends = (k == 0) | (k == blocks)
        scale = jnp.where(ends, 1.0, 2.0) / (2 * blocks * lanes)
        spec = three_pass(ah[k], al[k], table_ref[0], table_ref[1], ((1,), (0,))) * scale
        for at, ref in enumerate(spec_refs):
            ref[k] = spec[at * per : (at + 1) * per]

    over_frequencies(blocks + 1, one)


def put_turns(turn_ref):
    _, count, lanes = turn_ref.shape
    period = 2 * (count - 1) * lanes
    k = lax.broadcasted_iota(jnp.int32, (count, lanes), 0)
    s = lax.broadcasted_iota(jnp.int32, (count, lanes), 1)
    turn = (k * s).astype(f32) * (2 * math.pi / period)
    turn_ref[0] = jnp.cos(turn)
    turn_ref[1] = jnp.sin(turn)


def table(lanes):
    s = np.arange(lanes)
    base = 2 * np.pi * (s[:, None] * s[None, :] % lanes) / lanes
    c, n = np.cos(base), np.sin(base)
    full = np.block([[c, -n], [n, c]]).astype(np.float32)
    high = full.astype(ml_dtypes.bfloat16)
    low = (full - high.astype(np.float32)).astype(ml_dtypes.bfloat16)
    return jnp.asarray(np.stack([high, low]))


def filter_spectrum(long_filter, skip_gain, table, chunks):
    channels, length = long_filter.shape
    lanes = table.shape[2] // 2
    count = length // lanes + 1
    return pl.pallas_call(
        filter_kernel,
        in_specs=[whole] * 3,
        out_specs=[whole] * chunks,
        out_shape=[pltpu.HBM((count, channels // chunks, 2 * lanes), f32)] * chunks,
        scratch_shapes=[pltpu.VMEM((count, channels, 2 * lanes), bf16)] * 2
        + [pltpu.VMEM((2, count, lanes), f32)],
        compiler_params=params(24),
        cost_estimate=cost(6 * count * channels * 4 * lanes * lanes, 12 * count * channels * lanes),
        name="filter_spectrum",
    )(long_filter, skip_gain.reshape(1, channels), table)


def long_kernel(x_ref, spec_out, table_out, out_ref, ah, al, back, spec_ref, table_ref, turn_ref, sems):
    blocks, channels, lanes = x_ref.shape
    pieces = sems.shape[0] - 1
    edges = [(blocks + 1) * p // pieces for p in range(pieces + 1)]
    loads = [
        pltpu.make_async_copy(spec_out.at[low:high], spec_ref.at[low:high], sems.at[p])
        for p, (low, high) in enumerate(zip(edges, edges[1:]))
    ]
    loads.append(pltpu.make_async_copy(table_out, table_ref, sems.at[pieces]))
    for copy in reversed(loads):
        copy.start()
    put_turns(turn_ref)

    @pl.loop(0, channels // step_rows, unroll=2)
    def _(step):
        rows = pl.ds(pl.multiple_of(step * step_rows, step_rows), step_rows)
        x = [x_ref[j, rows].astype(f32) for j in range(blocks)]
        put_spectrum(padded_real_dft(x), turn_ref, ah, al, rows, lanes)

    for copy in loads:
        copy.wait()

    def one(k):
        x = three_pass(ah[k], al[k], table_ref[0], table_ref[1], ((1,), (0,)))
        spec = spec_ref[k]
        xr, xi = x[:, :lanes], x[:, lanes:]
        fr, fi = spec[:, :lanes], spec[:, lanes:]
        product = jnp.concatenate([xr * fr - xi * fi, xr * fi + xi * fr], axis=1)
        high, low = halves(product)
        back[k] = three_pass(high, low, table_ref[0], table_ref[1], ((1,), (1,)))

    over_frequencies(blocks + 1, one)

    @pl.loop(0, channels // step_rows, unroll=2)
    def _(step):
        rows = pl.ds(pl.multiple_of(step * step_rows, step_rows), step_rows)
        spectrum = [(back[0, rows, :lanes], None)]
        for k in range(1, blocks + 1):
            re, im = back[k, rows, :lanes], back[k, rows, lanes:]
            c, s = turn_ref[0, k : k + 1], turn_ref[1, k : k + 1]
            spectrum.append((re * c - im * s, None if k == blocks else re * s + im * c))
        for j, y in enumerate(padded_real_dft_adjoint(spectrum)):
            out_ref[j, rows] = y.astype(bf16)


def long_convolution(arrived, spec, table):
    blocks, channels, lanes = arrived.shape
    count = blocks + 1
    return pl.pallas_call(
        long_kernel,
        in_specs=[whole, outside, outside],
        out_specs=whole,
        out_shape=jax.ShapeDtypeStruct(arrived.shape, bf16),
        scratch_shapes=[
            pltpu.VMEM((count, channels, 2 * lanes), bf16),
            pltpu.VMEM((count, channels, 2 * lanes), bf16),
            pltpu.VMEM((count, channels, 2 * lanes), f32),
            pltpu.VMEM((count, channels, 2 * lanes), f32),
            pltpu.VMEM(table.shape, bf16),
            pltpu.VMEM((2, count, lanes), f32),
            pltpu.SemaphoreType.DMA((5,)),
        ],
        compiler_params=params(24),
        cost_estimate=cost(12 * count * channels * 4 * lanes * lanes, 12 * count * channels * lanes),
        name="long_convolution",
    )(arrived, in_hbm(spec), in_hbm(table))


def query_kernel(q_ref, before_ref, taps_ref, unembed_ref, targets_ref, ranks_ref, qs_ref, picked_ref, after_ref, space):
    rows, tokens = q_ref.shape

    @pl.loop(0, rows // tile, unroll=min(4, rows // tile))
    def _(at):
        part = aligned(at * tile, tile)
        before = before_ref[:, part].astype(f32)
        query_short = short_conv(q_ref[part], before[:rim], taps_ref, 0, part, space.at[at % 2])
        qs_ref[part] = jnp.concatenate(query_short, 0).T

    vocabulary = unembed_ref.shape[1]
    word = lax.broadcasted_iota(jnp.int32, (vocabulary, tokens), 0)
    chosen = (word == targets_ref[...]).astype(bf16)
    picked_ref[...] = dot(unembed_ref[...], chosen, ((1,), (0,))).astype(bf16)

    @pl.when(pl.program_id(0) == 0)
    def _():
        lists, size = ranks_ref.shape
        token = lax.broadcasted_iota(jnp.int32, (size, size), 0)
        rank = lax.broadcasted_iota(jnp.int32, (size, size), 1).astype(f32)
        at = [
            jnp.sum(jnp.where(token == ranks_ref[b : b + 1, :], rank, 0.0), axis=1, keepdims=True)
            for b in range(lists)
        ]
        column = jnp.concatenate(at, axis=0)
        row_of = lax.broadcasted_iota(jnp.int32, (tokens, tokens), 0)
        col_of = lax.broadcasted_iota(jnp.int32, (tokens, tokens), 1)
        row = jnp.sum(jnp.where(row_of == col_of, column, 0.0), axis=0, keepdims=True)
        same = row_of // size == col_of // size
        after_ref[...] = jnp.where(same & (row >= column), 1.0, 0.0)


def query_side(query_input, before, short_taps, unembed, targets, rankings):
    channels, tokens = query_input.shape
    width = short_taps.shape[1]
    vocabulary = unembed.shape[1]
    rows = channels // 4
    block = pl.BlockSpec((rows, tokens), lambda i: (i, 0))
    return pl.pallas_call(
        query_kernel,
        grid=(channels // rows,),
        in_specs=[
            block,
            pl.BlockSpec((3 * rim, rows), lambda i: (0, i)),
            pl.BlockSpec((1, width, rows), lambda i: (0, 0, i)),
            pl.BlockSpec((rows, vocabulary), lambda i: (i, 0)),
            pl.BlockSpec((1, tokens), lambda i: (0, 0)),
            pl.BlockSpec(rankings.shape, lambda i: (0, 0)),
        ],
        out_specs=[block, block, pl.BlockSpec((tokens, tokens), lambda i: (0, 0))],
        out_shape=[
            pltpu.HBM((channels, tokens), f32),
            pltpu.HBM((channels, tokens), bf16),
            pltpu.HBM((tokens, tokens), f32),
        ],
        scratch_shapes=[pltpu.VMEM((2, rim + tokens, tile), f32)],
        compiler_params=params(12),
        cost_estimate=cost(2 * channels * tokens * (vocabulary + 7), channels * (8 * tokens + 2 * vocabulary)),
        name="query_side",
    )(in_hbm(query_input), before, short_taps, in_hbm(unembed), targets.reshape(1, tokens), rankings)


def result_kernel(
    size, last, first, carried_ref, qs_out, picked_out, after_out, total_ref, _, out_hbm, next_ref, loss_ref,
    qs_ref, picked_ref, out_ref, after_ref, sems, after_sem,
):
    owners, per, tokens = carried_ref.shape
    groups = sems.shape[1]
    share = owners // groups
    loads, stores = [], []
    for g in range(groups):
        part = slice(g * share, (g + 1) * share)
        rows = slice(first, first + per)
        loads.append(
            [
                pltpu.make_async_copy(qs_out.at[part, rows], qs_ref.at[part], sems.at[0, g]),
                pltpu.make_async_copy(picked_out.at[part, rows], picked_ref.at[part], sems.at[1, g]),
            ]
        )
        stores.append(pltpu.make_async_copy(out_ref.at[part], out_hbm.at[part, rows], sems.at[2, g]))
    for pair in loads:
        for copy in pair:
            copy.start()
    after_load = pltpu.make_async_copy(after_out, after_ref, after_sem)
    after_load.start()
    total = total_ref[...]
    for g in range(groups):
        for copy in loads[g]:
            copy.wait()
        part = slice(g * share, (g + 1) * share)
        out = (qs_ref[part] * carried_ref[part].astype(f32)).astype(bf16)
        out_ref[part] = out
        stores[g].start()
        terms = out.astype(f32) * picked_ref[part].astype(f32)
        total = total + jnp.sum(terms.reshape(share * per // 8, 8, tokens), axis=0)
    next_ref[...] = total
    after_load.wait()
    if last:
        logit = jnp.sum(total, axis=0, keepdims=True)
        score = soft_cap * jnp.tanh(logit / soft_cap)
        mass = jnp.sum(after_ref[...] * jnp.exp(score), axis=1, keepdims=True)
        level = jnp.log(mass)
        lists = tokens // size
        lane = lax.broadcasted_iota(jnp.int32, (1, lists), 1)
        losses = jnp.zeros((1, lists), f32)
        for b in range(lists):
            part = slice(b * size, (b + 1) * size)
            own = jnp.sum(level[part]) - jnp.sum(score[:, part])
            losses = jnp.where(lane == b, own / size, losses)
        loss_ref[...] = losses
    for copy in stores:
        copy.wait()


def result(chunk, chunks, carried, query_short, picked, after, lists, total, out):
    owners, per, tokens = carried.shape
    local = per * chunks
    groups = math.gcd(owners, 8)
    start = out is None
    if start:
        total, out = jnp.zeros((8, tokens), f32), jnp.zeros((8, tokens), bf16)
    return pl.pallas_call(
        functools.partial(result_kernel, tokens // lists, chunk == chunks - 1, chunk * per),
        in_specs=[whole, outside, outside, outside, whole, outside],
        out_specs=[outside, whole, whole],
        out_shape=[
            jax.ShapeDtypeStruct((owners, local, tokens), bf16),
            jax.ShapeDtypeStruct((8, tokens), f32),
            jax.ShapeDtypeStruct((1, lists), f32),
        ],
        scratch_shapes=[
            pltpu.VMEM((owners, per, tokens), f32),
            pltpu.VMEM((owners, per, tokens), bf16),
            pltpu.VMEM((owners, per, tokens), bf16),
            pltpu.VMEM((tokens, tokens), f32),
            pltpu.SemaphoreType.DMA((3, groups)),
            pltpu.SemaphoreType.DMA,
        ],
        input_output_aliases={} if start else {5: 0},
        compiler_params=params(8),
        cost_estimate=cost(4 * owners * per * tokens, 10 * owners * per * tokens),
        name="result",
    )(
        carried,
        in_hbm(query_short.reshape(owners, local, tokens)),
        in_hbm(picked.reshape(owners, local, tokens)),
        in_hbm(after),
        total,
        out,
    )


def per_device(
    query_input,
    key_input,
    value_input,
    short_taps,
    long_filter,
    skip_gain,
    unembed,
    targets,
    rankings,
):
    channels, tokens = query_input.shape
    owners = lax.axis_size(token_axes)
    local = channels // owners
    lists = rankings.shape[0]
    chunks = most_chunks if local % (most_chunks * tile) == 0 else 1
    before = passed_along(rims(query_input, key_input, value_input), token_axes, 1)
    arrived = []
    for chunk in range(chunks):
        gated = gated_features(chunk, chunks, key_input, value_input, before, short_taps, owners)
        arrived.append(
            lax.all_to_all(gated.reshape(owners, local // chunks, tokens), token_axes, 0, 0, tiled=True)
        )
    transform = table(tokens)
    specs = filter_spectrum(long_filter, skip_gain, transform, chunks)
    query_short, picked, after = query_side(query_input, before, short_taps, unembed, targets, rankings)
    returned = []
    for chunk in range(chunks):
        carried = long_convolution(arrived[chunk], specs[chunk], transform)
        returned.append(lax.all_to_all(carried, token_axes, 0, 0, tiled=True))
    total = out = None
    for chunk in range(chunks):
        out, total, losses = result(
            chunk, chunks, returned[chunk], query_short, picked, after, lists, total, out
        )
    return out.reshape(channels, tokens), losses.reshape(lists)


def solution(mesh):
    placed = (
        P(None, ("grp", "seq", "tile")),
        P(None, ("grp", "seq", "tile")),
        P(None, ("grp", "seq", "tile")),
        P(),
        P(("seq", "tile"), None),
        P(("seq", "tile")),
        P(),
        P(("grp", "seq", "tile")),
        P(("grp", "seq", "tile"), None),
    )
    return jax.shard_map(
        per_device,
        mesh=mesh,
        in_specs=placed,
        out_specs=(P(None, ("grp", "seq", "tile")), P(("grp", "seq", "tile"))),
        check_vma=False,
    )
```

```python
import functools
import math

import jax
import jax.numpy as jnp
import ml_dtypes
import numpy as np
from jax import lax
from jax.experimental import pallas as pl
from jax.experimental.pallas import tpu as pltpu
from jax.sharding import PartitionSpec as P

soft_cap = 5.0
token_axes = ("seq", "tile")
bf16 = jnp.bfloat16
f32 = jnp.float32
rim = 8
most_chunks = 1
mebibyte = 1 << 20


whole = pl.BlockSpec(memory_space=pltpu.VMEM)
outside = pl.BlockSpec(memory_space=pltpu.HBM)


def in_hbm(x):
    return pltpu.with_memory_space_constraint(x, pltpu.HBM)


def params(limit=48):
    return pltpu.CompilerParams(vmem_limit_bytes=limit * mebibyte)


def cost(flops, size):
    return pl.CostEstimate(flops=flops, bytes_accessed=size, transcendentals=0)


def dot(a, b, over):
    return lax.dot_general(a, b, ((over[0], over[1]), ((), ())), preferred_element_type=f32)


def passed_along(block, axis, distance):
    devices = range(lax.axis_size(axis))
    route = [(i - distance, i) for i in devices if i - distance in devices]
    return lax.ppermute(block, axis, route)


def c_mul(z, angle):
    re, im = z
    turns = angle / (math.pi / 4)
    nearest = round(turns)
    if abs(turns - nearest) < 1e-9:
        eighth = nearest % 8
        if eighth == 0:
            return (re, im)
        if eighth == 2:
            return (-im, re)
        if eighth == 4:
            return (-re, -im)
        if eighth == 6:
            return (im, -re)
        half = math.sqrt(0.5)
        if eighth == 1:
            return ((re - im) * half, (re + im) * half)
        if eighth == 3:
            return ((re + im) * -half, (re - im) * half)
        if eighth == 5:
            return ((im - re) * half, (re + im) * -half)
        return ((re + im) * half, (im - re) * half)
    c, s = math.cos(angle), math.sin(angle)
    return (re * c - im * s, re * s + im * c)


def c_add(a, b):
    return (a[0] + b[0], a[1] + b[1])


def c_sub(a, b):
    return (a[0] - b[0], a[1] - b[1])


def c_dft(z, sign):
    n = len(z)
    if n == 1:
        return list(z)
    even = c_dft(z[0::2], sign)
    odd = c_dft(z[1::2], sign)
    turned = [c_mul(o, sign * 2 * math.pi * p / n) for p, o in enumerate(odd)]
    return [c_add(e, o) for e, o in zip(even, turned)] + [c_sub(e, o) for e, o in zip(even, turned)]


def odd_dft(x):
    n = len(x)
    if n == 1:
        return [(x[0], None)]
    half = n // 2
    z = [c_mul((x[j], -x[j + half]), -math.pi * j / n) for j in range(half)]
    wide = c_dft(z, -1)
    out = []
    for m in range(half):
        if m % 2 == 0:
            out.append(wide[m // 2])
        else:
            re, im = wide[(n - 1 - m) // 2]
            out.append((re, -im))
    return out


def real_dft(x):
    n = len(x)
    if n == 1:
        return [(x[0], None)]
    half = n // 2
    even = real_dft([x[j] + x[j + half] for j in range(half)])
    odd = odd_dft([x[j] - x[j + half] for j in range(half)])
    out = [None] * (half + 1)
    out[0::2] = even if half > 1 else [even[0]]
    out[1::2] = odd
    return out


def padded_real_dft(x):
    n = len(x)
    out = [None] * (n + 1)
    out[0::2] = real_dft(x)
    out[1::2] = odd_dft(x)
    return out


def odd_dft_adjoint(y):
    half = len(y)
    if y[0][1] is None:
        return [y[0][0]]
    n = 2 * half
    wide = []
    for p in range(half):
        if 2 * p < half:
            wide.append(y[2 * p])
        else:
            re, im = y[n - 1 - 2 * p]
            wide.append((re, -im))
    z = c_dft(wide, 1)
    turned = [c_mul(value, math.pi * j / n) for j, value in enumerate(z)]
    return [u[0] for u in turned] + [-u[1] for u in turned]


def real_dft_adjoint(x):
    if len(x) == 1:
        return [x[0][0]]
    even = real_dft_adjoint(x[0::2])
    odd = odd_dft_adjoint(x[1::2])
    return [e + o for e, o in zip(even, odd)] + [e - o for e, o in zip(even, odd)]


def padded_real_dft_adjoint(x):
    even = real_dft_adjoint(x[0::2])
    odd = odd_dft_adjoint(x[1::2])
    return [e + o for e, o in zip(even, odd)]


tile = 128


def rim_kernel(q_ref, k_ref, v_ref, out_ref, held_k, held_v, held_q, sems):
    pieces = sems.shape[1]
    channels, lanes = q_ref.shape
    rows = channels // pieces
    pairs = ((q_ref, held_q), (k_ref, held_k), (v_ref, held_v))
    parts = [slice(p * rows, (p + 1) * rows) for p in range(pieces)]
    copies = [
        [pltpu.make_async_copy(ref.at[part], held.at[part], sems.at[a, p]) for a, (ref, held) in enumerate(pairs)]
        for p, part in enumerate(parts)
    ]
    for group in copies:
        for copy in group:
            copy.start()
    row = lax.broadcasted_iota(jnp.int32, (rim, lanes), 0)
    lane = lax.broadcasted_iota(jnp.int32, (rim, lanes), 1)
    picker = (lane == row + (lanes - rim)).astype(bf16)
    for part, group in zip(parts, copies):
        for copy in group:
            copy.wait()
        last = [dot(picker, held[part], ((1,), (1,))) for _, held in pairs]
        out_ref[:, part] = jnp.concatenate(last, axis=0).astype(bf16)


def rims(query_input, key_input, value_input):
    channels, tokens = key_input.shape
    pieces = 2
    return pl.pallas_call(
        rim_kernel,
        in_specs=[outside] * 3,
        out_specs=[whole] * 3,
        out_shape=[jax.ShapeDtypeStruct((3 * rim, channels), bf16)]
        + [pltpu.VMEM((channels, tokens), bf16)] * 2,
        scratch_shapes=[
            pltpu.VMEM((channels, tokens), bf16),
            pltpu.SemaphoreType.DMA((3, pieces)),
        ],
        compiler_params=params(6),
        cost_estimate=cost(6 * channels * tokens * rim, 6 * channels * tokens),
        name="rims",
    )(in_hbm(query_input), in_hbm(key_input), in_hbm(value_input))


def short_conv(x, before, taps_ref, which, lanes, space):
    tokens = x.shape[1]
    space[:rim] = before
    space[rim:] = x.astype(f32).T
    width = taps_ref.shape[1]
    taps = [
        jnp.broadcast_to(taps_ref[which, offset : offset + 1, lanes], (8, tile)) for offset in range(width)
    ]
    out = []
    for begin in range(0, tokens, 8):
        total = taps[0] * space[rim + begin : rim + begin + 8]
        for offset in range(1, width):
            first = rim + begin - offset
            total = total + taps[offset] * space[first : first + 8]
        out.append(total)
    return out


def aligned(start, size):
    return pl.ds(pl.multiple_of(start, size), size)


def gated_kernel(chunk, k_ref, v_ref, before_ref, taps_out, out_ref, made, key_space, value_space, taps_ref, sems, taps_sem):
    owners, per, tokens = made.shape
    local = k_ref.shape[1]
    (groups,) = sems.shape
    size = owners // groups
    first = chunk * per
    taps_load = pltpu.make_async_copy(taps_out, taps_ref, taps_sem)
    taps_load.start()
    parts = [slice(g * size, (g + 1) * size) for g in range(groups)]
    stores = [pltpu.make_async_copy(made.at[part], out_ref.at[part], sems.at[g]) for g, part in enumerate(parts)]
    taps_load.wait()
    tiles = per // tile
    for g in range(groups):

        @pl.loop(0, size * tiles, unroll=gated_unroll)
        def _(at):
            owner = g * size + at // tiles
            row = at % tiles * tile
            rows = aligned(first + row, tile)
            lanes = aligned(owner * local + first + row, tile)
            before = before_ref[:, lanes].astype(f32)
            key_short = short_conv(k_ref[owner, rows], before[rim : 2 * rim], taps_ref, 1, lanes, key_space)
            value_short = short_conv(v_ref[owner, rows], before[2 * rim :], taps_ref, 2, lanes, value_space)
            made[owner, aligned(row, tile)] = (
                jnp.concatenate([k * v for k, v in zip(key_short, value_short)], 0).T.astype(bf16)
            )

        stores[g].start()
    for copy in stores:
        copy.wait()


gated_unroll = 4


def gated_features(chunk, chunks, key_input, value_input, before, short_taps, owners):
    channels, tokens = key_input.shape
    if chunks == 1:
        owners = channels // tile
    local = channels // owners
    per = local // chunks
    groups = math.gcd(owners, 8)
    return pl.pallas_call(
        functools.partial(gated_kernel, chunk),
        in_specs=[whole, whole, whole, outside],
        out_specs=outside,
        out_shape=jax.ShapeDtypeStruct((owners, per, tokens), bf16),
        scratch_shapes=[
            pltpu.VMEM((owners, per, tokens), bf16),
            pltpu.VMEM((rim + tokens, tile), f32),
            pltpu.VMEM((rim + tokens, tile), f32),
            pltpu.VMEM(short_taps.shape, f32),
            pltpu.SemaphoreType.DMA((groups,)),
            pltpu.SemaphoreType.DMA,
        ],
        compiler_params=params(8),
        cost_estimate=cost(28 * channels * tokens // chunks, 6 * channels * tokens // chunks),
        name="gated",
    )(
        key_input.reshape(owners, local, tokens),
        value_input.reshape(owners, local, tokens),
        before,
        in_hbm(short_taps),
    )


step_rows = 16
long_parts = 2


def halves(x):
    high = x.astype(bf16)
    return high, (x - high.astype(f32)).astype(bf16)


def put_spectrum(spectrum, turn_ref, high_ref, low_ref, rows, lanes):
    for at, (re, im) in enumerate(spectrum):
        if at == 0:
            im = jnp.zeros_like(re)
        else:
            c, s = turn_ref[0, at : at + 1], turn_ref[1, at : at + 1]
            if im is None:
                re, im = re * c, -(re * s)
            else:
                re, im = re * c + im * s, im * c - re * s
        for value, part in ((re, slice(0, lanes)), (im, slice(lanes, 2 * lanes))):
            high, low = halves(value)
            high_ref[at, rows, part] = high
            low_ref[at, rows, part] = low


def three_pass(ah, al, wh, wl, over):
    return dot(ah, wh, over) + (dot(al, wh, over) + dot(ah, wl, over))


def over_frequencies(count, body):
    if count <= 33:
        for k in range(count):
            body(k)
    else:
        pl.loop(0, count)(body)


def filter_kernel(taps_ref, skip_ref, table_ref, *rest):
    *spec_refs, ah, al, turn_ref = rest
    put_turns(turn_ref)
    channels = taps_ref.shape[0]
    lanes = turn_ref.shape[2]
    blocks = taps_ref.shape[1] // lanes
    skip = jnp.broadcast_to(skip_ref[...], (8, channels)).T
    lane = lax.broadcasted_iota(jnp.int32, (step_rows, lanes), 1)
    for step in range(channels // step_rows):
        rows = slice(step * step_rows, (step + 1) * step_rows)
        x = [taps_ref[rows, j * lanes : (j + 1) * lanes] for j in range(blocks)]
        x[0] = x[0] + jnp.where(lane == 0, skip[rows, 0:1], 0.0)
        put_spectrum(padded_real_dft(x), turn_ref, ah, al, rows, lanes)
    per = channels // len(spec_refs)

    def one(k):
        ends = (k == 0) | (k == blocks)
        scale = jnp.where(ends, 1.0, 2.0) / (2 * blocks * lanes)
        spec = three_pass(ah[k], al[k], table_ref[0], table_ref[1], ((1,), (0,))) * scale
        for at, ref in enumerate(spec_refs):
            ref[k] = spec[at * per : (at + 1) * per]

    over_frequencies(blocks + 1, one)


def put_turns(turn_ref):
    _, count, lanes = turn_ref.shape
    period = 2 * (count - 1) * lanes
    k = lax.broadcasted_iota(jnp.int32, (count, lanes), 0)
    s = lax.broadcasted_iota(jnp.int32, (count, lanes), 1)
    turn = (k * s).astype(f32) * (2 * math.pi / period)
    turn_ref[0] = jnp.cos(turn)
    turn_ref[1] = jnp.sin(turn)


def table(lanes):
    s = np.arange(lanes)
    base = 2 * np.pi * (s[:, None] * s[None, :] % lanes) / lanes
    c, n = np.cos(base), np.sin(base)
    full = np.block([[c, -n], [n, c]]).astype(np.float32)
    high = full.astype(ml_dtypes.bfloat16)
    low = (full - high.astype(np.float32)).astype(ml_dtypes.bfloat16)
    return jnp.asarray(np.stack([high, low]))


def filter_spectrum(long_filter, skip_gain, table, chunks):
    channels, length = long_filter.shape
    lanes = table.shape[2] // 2
    count = length // lanes + 1
    return pl.pallas_call(
        filter_kernel,
        in_specs=[whole] * 3,
        out_specs=[whole] * chunks,
        out_shape=[pltpu.HBM((count, channels // chunks, 2 * lanes), f32)] * chunks,
        scratch_shapes=[pltpu.VMEM((count, channels, 2 * lanes), bf16)] * 2
        + [pltpu.VMEM((2, count, lanes), f32)],
        compiler_params=params(24),
        cost_estimate=cost(6 * count * channels * 4 * lanes * lanes, 12 * count * channels * lanes),
        name="filter_spectrum",
    )(long_filter, skip_gain.reshape(1, channels), table)


def long_kernel(x_ref, spec_out, table_out, out_hbm, ah, al, back, spec_ref, table_ref, turn_ref, out_ref, sems):
    blocks, channels, lanes = x_ref.shape
    count = blocks + 1
    table_load = pltpu.make_async_copy(table_out, table_ref, sems.at[0])
    split = channels % (long_parts * step_rows) == 0 and count <= 33
    share = channels // long_parts if split else channels
    parts = [slice(first, first + share) for first in range(0, channels, share)]
    loads = [
        pltpu.make_async_copy(spec_out.at[:, part], spec_ref.at[:, part], sems.at[1 + at])
        for at, part in enumerate(parts)
    ]
    table_load.start()
    for copy in loads[:2]:
        copy.start()
    put_turns(turn_ref)

    def forward(rows):
        x = [x_ref[j, rows].astype(f32) for j in range(blocks)]
        put_spectrum(padded_real_dft(x), turn_ref, ah, al, rows, lanes)

    def multiply(first, size, rows):
        def take(ref):
            part = ref[pl.ds(first, size), rows]
            return part.reshape(size * part.shape[1], 2 * lanes)

        x = three_pass(take(ah), take(al), table_ref[0], table_ref[1], ((1,), (0,)))
        spec = take(spec_ref)
        xr, xi = x[:, :lanes], x[:, lanes:]
        fr, fi = spec[:, :lanes], spec[:, lanes:]
        product = jnp.concatenate([xr * fr - xi * fi, xr * fi + xi * fr], axis=1)
        high, low = halves(product)
        y = three_pass(high, low, table_ref[0], table_ref[1], ((1,), (1,)))
        back[pl.ds(first, size), rows] = y.reshape(size, -1, 2 * lanes)

    def backward(rows):
        spectrum = [(back[0, rows, :lanes], None)]
        for k in range(1, count):
            re, im = back[k, rows, :lanes], back[k, rows, lanes:]
            c, s = turn_ref[0, k : k + 1], turn_ref[1, k : k + 1]
            spectrum.append((re * c - im * s, None if k == blocks else re * s + im * c))
        for j, y in enumerate(padded_real_dft_adjoint(spectrum)):
            out_ref[j, rows] = y.astype(bf16)

    def store(part, at):
        return pltpu.make_async_copy(out_ref.at[:, part], out_hbm.at[:, part], sems.at[1 + long_parts + at])

    if split:
        size = max(1, 256 // share)
        steps = [[slice(r, r + step_rows) for r in range(p.start, p.stop, step_rows)] for p in parts]
        groups = [(k, min(size, count - k)) for k in range(0, count, size)]

        def together(part, others):
            done = 0
            for at, (k, many) in enumerate(groups):
                multiply(k, many, part)
                upto = len(others) * (at + 1) // len(groups)
                for body, rows in others[done:upto]:
                    body(rows)
                done = upto

        ahead = 2
        for step in steps[:ahead]:
            for rows in step:
                forward(rows)
        table_load.wait()
        for at, part in enumerate(parts):
            loads[at].wait()
            if at + 2 < len(parts):
                loads[at + 2].start()
            others = [(forward, rows) for rows in (steps[at + ahead] if at + ahead < len(parts) else [])]
            others += [(backward, rows) for rows in (steps[at - 1] if at else [])]
            together(part, others)
            if at:
                store(parts[at - 1], at - 1).start()
        for rows in steps[-1]:
            backward(rows)
        store(parts[-1], len(parts) - 1).start()
        for at, part in enumerate(parts):
            store(part, at).wait()
    else:
        everything = slice(0, channels)

        @pl.loop(0, channels // step_rows)
        def _(step):
            forward(aligned(step * step_rows, step_rows))

        table_load.wait()
        loads[0].wait()
        over_frequencies(count, lambda k: multiply(k, 1, everything))

        @pl.loop(0, channels // step_rows)
        def _(step):
            backward(aligned(step * step_rows, step_rows))

        store(everything, 0).start()
        store(everything, 0).wait()


def long_convolution(arrived, spec, table):
    blocks, channels, lanes = arrived.shape
    count = blocks + 1
    return pl.pallas_call(
        long_kernel,
        in_specs=[whole, outside, outside],
        out_specs=outside,
        out_shape=jax.ShapeDtypeStruct(arrived.shape, bf16),
        scratch_shapes=[
            pltpu.VMEM((count, channels, 2 * lanes), bf16),
            pltpu.VMEM((count, channels, 2 * lanes), bf16),
            pltpu.VMEM((count, channels, 2 * lanes), f32),
            pltpu.VMEM((count, channels, 2 * lanes), f32),
            pltpu.VMEM(table.shape, bf16),
            pltpu.VMEM((2, count, lanes), f32),
            pltpu.VMEM(arrived.shape, bf16),
            pltpu.SemaphoreType.DMA((1 + 2 * long_parts,)),
        ],
        compiler_params=params(24),
        cost_estimate=cost(12 * count * channels * 4 * lanes * lanes, 12 * count * channels * lanes),
        name="long_convolution",
    )(arrived, in_hbm(spec), in_hbm(table))


def query_kernel(q_ref, before_ref, taps_ref, unembed_ref, targets_ref, ranks_ref, qs_ref, picked_ref, after_ref, space):
    rows, tokens = q_ref.shape

    @pl.loop(0, rows // tile, unroll=min(4, rows // tile))
    def _(at):
        part = aligned(at * tile, tile)
        before = before_ref[:, part].astype(f32)
        query_short = short_conv(q_ref[part], before[:rim], taps_ref, 0, part, space.at[at % 2])
        qs_ref[part] = jnp.concatenate(query_short, 0).T

    vocabulary = unembed_ref.shape[1]
    word = lax.broadcasted_iota(jnp.int32, (vocabulary, tokens), 0)
    chosen = (word == targets_ref[...]).astype(bf16)
    picked_ref[...] = dot(unembed_ref[...], chosen, ((1,), (0,))).astype(bf16)

    @pl.when(pl.program_id(0) == 0)
    def _():
        lists, size = ranks_ref.shape
        token = lax.broadcasted_iota(jnp.int32, (size, size), 0)
        rank = lax.broadcasted_iota(jnp.int32, (size, size), 1).astype(f32)
        at = [
            jnp.sum(jnp.where(token == ranks_ref[b : b + 1, :], rank, 0.0), axis=1, keepdims=True)
            for b in range(lists)
        ]
        column = jnp.concatenate(at, axis=0)
        row_of = lax.broadcasted_iota(jnp.int32, (tokens, tokens), 0)
        col_of = lax.broadcasted_iota(jnp.int32, (tokens, tokens), 1)
        row = jnp.sum(jnp.where(row_of == col_of, column, 0.0), axis=0, keepdims=True)
        same = row_of // size == col_of // size
        after_ref[...] = jnp.where(same & (row >= column), 1.0, 0.0)


def query_side(query_input, before, short_taps, unembed, targets, rankings):
    channels, tokens = query_input.shape
    width = short_taps.shape[1]
    vocabulary = unembed.shape[1]
    rows = channels // 4
    block = pl.BlockSpec((rows, tokens), lambda i: (i, 0))
    return pl.pallas_call(
        query_kernel,
        grid=(channels // rows,),
        in_specs=[
            block,
            pl.BlockSpec((3 * rim, rows), lambda i: (0, i)),
            pl.BlockSpec((1, width, rows), lambda i: (0, 0, i)),
            pl.BlockSpec((rows, vocabulary), lambda i: (i, 0)),
            pl.BlockSpec((1, tokens), lambda i: (0, 0)),
            pl.BlockSpec(rankings.shape, lambda i: (0, 0)),
        ],
        out_specs=[block, block, pl.BlockSpec((tokens, tokens), lambda i: (0, 0))],
        out_shape=[
            pltpu.HBM((channels, tokens), f32),
            pltpu.HBM((channels, tokens), bf16),
            pltpu.HBM((tokens, tokens), f32),
        ],
        scratch_shapes=[pltpu.VMEM((2, rim + tokens, tile), f32)],
        compiler_params=params(12),
        cost_estimate=cost(2 * channels * tokens * (vocabulary + 7), channels * (8 * tokens + 2 * vocabulary)),
        name="query_side",
    )(in_hbm(query_input), before, short_taps, in_hbm(unembed), targets.reshape(1, tokens), rankings)


def result_kernel(
    size, last, first, carried_ref, qs_out, picked_out, after_out, total_ref, _, out_hbm, next_ref, loss_ref,
    qs_ref, picked_ref, out_ref, after_ref, sems, after_sem,
):
    owners, per, tokens = carried_ref.shape
    groups = sems.shape[1]
    share = owners // groups
    loads, stores = [], []
    for g in range(groups):
        part = slice(g * share, (g + 1) * share)
        rows = slice(first, first + per)
        loads.append(
            [
                pltpu.make_async_copy(qs_out.at[part, rows], qs_ref.at[part], sems.at[0, g]),
                pltpu.make_async_copy(picked_out.at[part, rows], picked_ref.at[part], sems.at[1, g]),
            ]
        )
        stores.append(pltpu.make_async_copy(out_ref.at[part], out_hbm.at[part, rows], sems.at[2, g]))
    for pair in loads:
        for copy in pair:
            copy.start()
    after_load = pltpu.make_async_copy(after_out, after_ref, after_sem)
    after_load.start()
    total = total_ref[...]
    for g in range(groups):
        for copy in loads[g]:
            copy.wait()
        part = slice(g * share, (g + 1) * share)
        out = (qs_ref[part] * carried_ref[part].astype(f32)).astype(bf16)
        out_ref[part] = out
        stores[g].start()
        terms = out.astype(f32) * picked_ref[part].astype(f32)
        total = total + jnp.sum(terms.reshape(share * per // 8, 8, tokens), axis=0)
    next_ref[...] = total
    after_load.wait()
    if last:
        logit = jnp.sum(total, axis=0, keepdims=True)
        score = soft_cap * jnp.tanh(logit / soft_cap)
        mass = jnp.sum(after_ref[...] * jnp.exp(score), axis=1, keepdims=True)
        level = jnp.log(mass)
        lists = tokens // size
        lane = lax.broadcasted_iota(jnp.int32, (1, lists), 1)
        losses = jnp.zeros((1, lists), f32)
        for b in range(lists):
            part = slice(b * size, (b + 1) * size)
            own = jnp.sum(level[part]) - jnp.sum(score[:, part])
            losses = jnp.where(lane == b, own / size, losses)
        loss_ref[...] = losses
    for copy in stores:
        copy.wait()


def result(chunk, chunks, carried, query_short, picked, after, lists, total, out):
    owners, per, tokens = carried.shape
    local = per * chunks
    groups = math.gcd(owners, 8)
    start = out is None
    if start:
        total, out = jnp.zeros((8, tokens), f32), jnp.zeros((8, tokens), bf16)
    return pl.pallas_call(
        functools.partial(result_kernel, tokens // lists, chunk == chunks - 1, chunk * per),
        in_specs=[whole, outside, outside, outside, whole, outside],
        out_specs=[outside, whole, whole],
        out_shape=[
            jax.ShapeDtypeStruct((owners, local, tokens), bf16),
            jax.ShapeDtypeStruct((8, tokens), f32),
            jax.ShapeDtypeStruct((1, lists), f32),
        ],
        scratch_shapes=[
            pltpu.VMEM((owners, per, tokens), f32),
            pltpu.VMEM((owners, per, tokens), bf16),
            pltpu.VMEM((owners, per, tokens), bf16),
            pltpu.VMEM((tokens, tokens), f32),
            pltpu.SemaphoreType.DMA((3, groups)),
            pltpu.SemaphoreType.DMA,
        ],
        input_output_aliases={} if start else {5: 0},
        compiler_params=params(8),
        cost_estimate=cost(4 * owners * per * tokens, 10 * owners * per * tokens),
        name="result",
    )(
        carried,
        in_hbm(query_short.reshape(owners, local, tokens)),
        in_hbm(picked.reshape(owners, local, tokens)),
        in_hbm(after),
        total,
        out,
    )


def per_device(
    query_input,
    key_input,
    value_input,
    short_taps,
    long_filter,
    skip_gain,
    unembed,
    targets,
    rankings,
):
    channels, tokens = query_input.shape
    owners = lax.axis_size(token_axes)
    local = channels // owners
    lists = rankings.shape[0]
    chunks = most_chunks if local % (most_chunks * tile) == 0 else 1
    last, held_key, held_value = rims(query_input, key_input, value_input)
    before = passed_along(last, token_axes, 1)
    arrived = []
    for chunk in range(chunks):
        gated = gated_features(chunk, chunks, held_key, held_value, before, short_taps, owners)
        arrived.append(
            lax.all_to_all(gated.reshape(owners, local // chunks, tokens), token_axes, 0, 0, tiled=True)
        )
    transform = table(tokens)
    specs = filter_spectrum(long_filter, skip_gain, transform, chunks)
    query_short, picked, after = query_side(query_input, before, short_taps, unembed, targets, rankings)
    returned = []
    for chunk in range(chunks):
        carried = long_convolution(arrived[chunk], specs[chunk], transform)
        returned.append(lax.all_to_all(carried, token_axes, 0, 0, tiled=True))
    total = out = None
    for chunk in range(chunks):
        out, total, losses = result(
            chunk, chunks, returned[chunk], query_short, picked, after, lists, total, out
        )
    return out.reshape(channels, tokens), losses.reshape(lists)


def solution(mesh):
    placed = (
        P(None, ("grp", "seq", "tile")),
        P(None, ("grp", "seq", "tile")),
        P(None, ("grp", "seq", "tile")),
        P(),
        P(("seq", "tile"), None),
        P(("seq", "tile")),
        P(),
        P(("grp", "seq", "tile")),
        P(("grp", "seq", "tile"), None),
    )
    return jax.shard_map(
        per_device,
        mesh=mesh,
        in_specs=placed,
        out_specs=(P(None, ("grp", "seq", "tile")), P(("grp", "seq", "tile"))),
        check_vma=False,
    )
```

```python
import functools
import math

import jax
import jax.numpy as jnp
import ml_dtypes
import numpy as np
from jax import lax
from jax.experimental import pallas as pl
from jax.experimental.pallas import tpu as pltpu
from jax.sharding import PartitionSpec as P

soft_cap = 5.0
token_axes = ("seq", "tile")
bf16 = jnp.bfloat16
f32 = jnp.float32
rim = 8
most_chunks = 1
mebibyte = 1 << 20


whole = pl.BlockSpec(memory_space=pltpu.VMEM)
outside = pl.BlockSpec(memory_space=pltpu.HBM)


def in_hbm(x):
    return pltpu.with_memory_space_constraint(x, pltpu.HBM)


def params(limit=48):
    return pltpu.CompilerParams(vmem_limit_bytes=limit * mebibyte)


def cost(flops, size):
    return pl.CostEstimate(flops=flops, bytes_accessed=size, transcendentals=0)


def dot(a, b, over):
    return lax.dot_general(a, b, ((over[0], over[1]), ((), ())), preferred_element_type=f32)


def passed_along(block, axis, distance):
    devices = range(lax.axis_size(axis))
    route = [(i - distance, i) for i in devices if i - distance in devices]
    return lax.ppermute(block, axis, route)


def c_mul(z, angle):
    re, im = z
    turns = angle / (math.pi / 4)
    nearest = round(turns)
    if abs(turns - nearest) < 1e-9:
        eighth = nearest % 8
        if eighth == 0:
            return (re, im)
        if eighth == 2:
            return (-im, re)
        if eighth == 4:
            return (-re, -im)
        if eighth == 6:
            return (im, -re)
        half = math.sqrt(0.5)
        if eighth == 1:
            return ((re - im) * half, (re + im) * half)
        if eighth == 3:
            return ((re + im) * -half, (re - im) * half)
        if eighth == 5:
            return ((im - re) * half, (re + im) * -half)
        return ((re + im) * half, (im - re) * half)
    c, s = math.cos(angle), math.sin(angle)
    return (re * c - im * s, re * s + im * c)


def c_add(a, b):
    return (a[0] + b[0], a[1] + b[1])


def c_sub(a, b):
    return (a[0] - b[0], a[1] - b[1])


def c_dft(z, sign):
    n = len(z)
    if n == 1:
        return list(z)
    even = c_dft(z[0::2], sign)
    odd = c_dft(z[1::2], sign)
    turned = [c_mul(o, sign * 2 * math.pi * p / n) for p, o in enumerate(odd)]
    return [c_add(e, o) for e, o in zip(even, turned)] + [c_sub(e, o) for e, o in zip(even, turned)]


def odd_dft(x):
    n = len(x)
    if n == 1:
        return [(x[0], None)]
    half = n // 2
    z = [c_mul((x[j], -x[j + half]), -math.pi * j / n) for j in range(half)]
    wide = c_dft(z, -1)
    out = []
    for m in range(half):
        if m % 2 == 0:
            out.append(wide[m // 2])
        else:
            re, im = wide[(n - 1 - m) // 2]
            out.append((re, -im))
    return out


def real_dft(x):
    n = len(x)
    if n == 1:
        return [(x[0], None)]
    half = n // 2
    even = real_dft([x[j] + x[j + half] for j in range(half)])
    odd = odd_dft([x[j] - x[j + half] for j in range(half)])
    out = [None] * (half + 1)
    out[0::2] = even if half > 1 else [even[0]]
    out[1::2] = odd
    return out


def padded_real_dft(x):
    n = len(x)
    out = [None] * (n + 1)
    out[0::2] = real_dft(x)
    out[1::2] = odd_dft(x)
    return out


def odd_dft_adjoint(y):
    half = len(y)
    if y[0][1] is None:
        return [y[0][0]]
    n = 2 * half
    wide = []
    for p in range(half):
        if 2 * p < half:
            wide.append(y[2 * p])
        else:
            re, im = y[n - 1 - 2 * p]
            wide.append((re, -im))
    z = c_dft(wide, 1)
    turned = [c_mul(value, math.pi * j / n) for j, value in enumerate(z)]
    return [u[0] for u in turned] + [-u[1] for u in turned]


def real_dft_adjoint(x):
    if len(x) == 1:
        return [x[0][0]]
    even = real_dft_adjoint(x[0::2])
    odd = odd_dft_adjoint(x[1::2])
    return [e + o for e, o in zip(even, odd)] + [e - o for e, o in zip(even, odd)]


def padded_real_dft_adjoint(x):
    even = real_dft_adjoint(x[0::2])
    odd = odd_dft_adjoint(x[1::2])
    return [e + o for e, o in zip(even, odd)]


tile = 128


def rim_picker(lanes):
    row = lax.broadcasted_iota(jnp.int32, (rim, lanes), 0)
    lane = lax.broadcasted_iota(jnp.int32, (rim, lanes), 1)
    return (lane == row + (lanes - rim)).astype(bf16)


def rim_kernel(k_ref, v_ref, out_ref, held_k, held_v, sems):
    pieces = sems.shape[1]
    channels, lanes = k_ref.shape
    rows = channels // pieces
    pairs = ((k_ref, held_k), (v_ref, held_v))
    parts = [slice(p * rows, (p + 1) * rows) for p in range(pieces)]
    copies = [
        [pltpu.make_async_copy(ref.at[part], held.at[part], sems.at[a, p]) for a, (ref, held) in enumerate(pairs)]
        for p, part in enumerate(parts)
    ]
    for group in copies:
        for copy in group:
            copy.start()
    picker = rim_picker(lanes)
    for part, group in zip(parts, copies):
        for copy in group:
            copy.wait()
        last = [dot(picker, held[part], ((1,), (1,))) for _, held in pairs]
        out_ref[:, part] = jnp.concatenate(last, axis=0).astype(bf16)


def rims(key_input, value_input):
    channels, tokens = key_input.shape
    pieces = 2
    return pl.pallas_call(
        rim_kernel,
        in_specs=[outside] * 2,
        out_specs=[whole] * 3,
        out_shape=[jax.ShapeDtypeStruct((2 * rim, channels), bf16)]
        + [pltpu.VMEM((channels, tokens), bf16)] * 2,
        scratch_shapes=[pltpu.SemaphoreType.DMA((2, pieces))],
        compiler_params=params(6),
        cost_estimate=cost(4 * channels * tokens * rim, 4 * channels * tokens),
        name="rims",
    )(in_hbm(key_input), in_hbm(value_input))


def short_conv(x, before, taps_ref, which, lanes, space):
    tokens = x.shape[1]
    space[:rim] = before
    space[rim:] = x.astype(f32).T
    width = taps_ref.shape[1]
    taps = [
        jnp.broadcast_to(taps_ref[which, offset : offset + 1, lanes], (8, tile)) for offset in range(width)
    ]
    out = []
    for begin in range(0, tokens, 8):
        total = taps[0] * space[rim + begin : rim + begin + 8]
        for offset in range(1, width):
            first = rim + begin - offset
            total = total + taps[offset] * space[first : first + 8]
        out.append(total)
    return out


def aligned(start, size):
    return pl.ds(pl.multiple_of(start, size), size)


def gated_kernel(chunk, k_ref, v_ref, before_ref, taps_out, out_ref, made, key_space, value_space, taps_ref, sems, taps_sem):
    owners, per, tokens = made.shape
    local = k_ref.shape[1]
    (groups,) = sems.shape
    size = owners // groups
    first = chunk * per
    taps_load = pltpu.make_async_copy(taps_out, taps_ref, taps_sem)
    taps_load.start()
    parts = [slice(g * size, (g + 1) * size) for g in range(groups)]
    stores = [pltpu.make_async_copy(made.at[part], out_ref.at[part], sems.at[g]) for g, part in enumerate(parts)]
    taps_load.wait()
    tiles = per // tile
    for g in range(groups):

        @pl.loop(0, size * tiles, unroll=gated_unroll)
        def _(at):
            owner = g * size + at // tiles
            row = at % tiles * tile
            rows = aligned(first + row, tile)
            lanes = aligned(owner * local + first + row, tile)
            before = before_ref[:, lanes].astype(f32)
            key_short = short_conv(k_ref[owner, rows], before[:rim], taps_ref, 1, lanes, key_space)
            value_short = short_conv(v_ref[owner, rows], before[rim:], taps_ref, 2, lanes, value_space)
            made[owner, aligned(row, tile)] = (
                jnp.concatenate([k * v for k, v in zip(key_short, value_short)], 0).T.astype(bf16)
            )

        stores[g].start()
    for copy in stores:
        copy.wait()


gated_unroll = 4


def gated_features(chunk, chunks, key_input, value_input, before, short_taps, owners):
    channels, tokens = key_input.shape
    if chunks == 1:
        owners = channels // tile
    local = channels // owners
    per = local // chunks
    groups = math.gcd(owners, 8)
    return pl.pallas_call(
        functools.partial(gated_kernel, chunk),
        in_specs=[whole, whole, whole, outside],
        out_specs=outside,
        out_shape=jax.ShapeDtypeStruct((owners, per, tokens), bf16),
        scratch_shapes=[
            pltpu.VMEM((owners, per, tokens), bf16),
            pltpu.VMEM((rim + tokens, tile), f32),
            pltpu.VMEM((rim + tokens, tile), f32),
            pltpu.VMEM(short_taps.shape, f32),
            pltpu.SemaphoreType.DMA((groups,)),
            pltpu.SemaphoreType.DMA,
        ],
        compiler_params=params(8),
        cost_estimate=cost(28 * channels * tokens // chunks, 6 * channels * tokens // chunks),
        name="gated",
    )(
        key_input.reshape(owners, local, tokens),
        value_input.reshape(owners, local, tokens),
        before,
        in_hbm(short_taps),
    )


step_rows = 16
long_parts = 2


def halves(x):
    high = x.astype(bf16)
    return high, (x - high.astype(f32)).astype(bf16)


def put_spectrum(spectrum, turn_ref, high_ref, low_ref, rows, lanes):
    for at, (re, im) in enumerate(spectrum):
        if at == 0:
            im = jnp.zeros_like(re)
        else:
            c, s = turn_ref[0, at : at + 1], turn_ref[1, at : at + 1]
            if im is None:
                re, im = re * c, -(re * s)
            else:
                re, im = re * c + im * s, im * c - re * s
        for value, part in ((re, slice(0, lanes)), (im, slice(lanes, 2 * lanes))):
            high, low = halves(value)
            high_ref[at, rows, part] = high
            low_ref[at, rows, part] = low


def three_pass(ah, al, wh, wl, over):
    return dot(ah, wh, over) + (dot(al, wh, over) + dot(ah, wl, over))


def over_frequencies(count, body):
    if count <= 33:
        for k in range(count):
            body(k)
    else:
        pl.loop(0, count)(body)


def filter_kernel(taps_ref, skip_ref, table_ref, q_ref, *rest):
    *spec_refs, last_ref, ah, al, turn_ref, held, sem = rest
    load = pltpu.make_async_copy(q_ref, held, sem)
    load.start()
    put_turns(turn_ref)
    channels = taps_ref.shape[0]
    lanes = turn_ref.shape[2]
    blocks = taps_ref.shape[1] // lanes
    skip = jnp.broadcast_to(skip_ref[...], (8, channels)).T
    lane = lax.broadcasted_iota(jnp.int32, (step_rows, lanes), 1)
    for step in range(channels // step_rows):
        rows = slice(step * step_rows, (step + 1) * step_rows)
        x = [taps_ref[rows, j * lanes : (j + 1) * lanes] for j in range(blocks)]
        x[0] = x[0] + jnp.where(lane == 0, skip[rows, 0:1], 0.0)
        put_spectrum(padded_real_dft(x), turn_ref, ah, al, rows, lanes)
    per = channels // len(spec_refs)

    def one(k):
        ends = (k == 0) | (k == blocks)
        scale = jnp.where(ends, 1.0, 2.0) / (2 * blocks * lanes)
        spec = three_pass(ah[k], al[k], table_ref[0], table_ref[1], ((1,), (0,))) * scale
        for at, ref in enumerate(spec_refs):
            ref[k] = spec[at * per : (at + 1) * per]

    over_frequencies(blocks + 1, one)
    load.wait()
    last_ref[...] = dot(rim_picker(held.shape[1]), held[...], ((1,), (1,))).astype(bf16)


def put_turns(turn_ref):
    _, count, lanes = turn_ref.shape
    period = 2 * (count - 1) * lanes
    k = lax.broadcasted_iota(jnp.int32, (count, lanes), 0)
    s = lax.broadcasted_iota(jnp.int32, (count, lanes), 1)
    turn = (k * s).astype(f32) * (2 * math.pi / period)
    turn_ref[0] = jnp.cos(turn)
    turn_ref[1] = jnp.sin(turn)


def table(lanes):
    s = np.arange(lanes)
    base = 2 * np.pi * (s[:, None] * s[None, :] % lanes) / lanes
    c, n = np.cos(base), np.sin(base)
    full = np.block([[c, -n], [n, c]]).astype(np.float32)
    high = full.astype(ml_dtypes.bfloat16)
    low = (full - high.astype(np.float32)).astype(ml_dtypes.bfloat16)
    return jnp.asarray(np.stack([high, low]))


def filter_spectrum(long_filter, skip_gain, table, query_input, chunks):
    channels, length = long_filter.shape
    lanes = table.shape[2] // 2
    count = length // lanes + 1
    return pl.pallas_call(
        filter_kernel,
        in_specs=[whole, whole, whole, outside],
        out_specs=[whole] * (chunks + 1),
        out_shape=[pltpu.HBM((count, channels // chunks, 2 * lanes), f32)] * chunks
        + [pltpu.HBM((rim, query_input.shape[0]), bf16)],
        scratch_shapes=[pltpu.VMEM((count, channels, 2 * lanes), bf16)] * 2
        + [
            pltpu.VMEM((2, count, lanes), f32),
            pltpu.VMEM(query_input.shape, bf16),
            pltpu.SemaphoreType.DMA,
        ],
        compiler_params=params(24),
        cost_estimate=cost(6 * count * channels * 4 * lanes * lanes, 12 * count * channels * lanes),
        name="filter_spectrum",
    )(long_filter, skip_gain.reshape(1, channels), table, in_hbm(query_input))


def long_kernel(x_ref, spec_out, table_out, out_hbm, ah, al, back, spec_ref, table_ref, turn_ref, out_ref, sems):
    blocks, channels, lanes = x_ref.shape
    count = blocks + 1
    table_load = pltpu.make_async_copy(table_out, table_ref, sems.at[0])
    split = channels % (long_parts * step_rows) == 0 and count <= 33
    share = channels // long_parts if split else channels
    parts = [slice(first, first + share) for first in range(0, channels, share)]
    loads = [
        pltpu.make_async_copy(spec_out.at[:, part], spec_ref.at[:, part], sems.at[1 + at])
        for at, part in enumerate(parts)
    ]
    table_load.start()
    for copy in loads[:2]:
        copy.start()
    put_turns(turn_ref)

    def forward(rows):
        x = [x_ref[j, rows].astype(f32) for j in range(blocks)]
        put_spectrum(padded_real_dft(x), turn_ref, ah, al, rows, lanes)

    def multiply(first, size, rows):
        def take(ref):
            part = ref[pl.ds(first, size), rows]
            return part.reshape(size * part.shape[1], 2 * lanes)

        x = three_pass(take(ah), take(al), table_ref[0], table_ref[1], ((1,), (0,)))
        spec = take(spec_ref)
        xr, xi = x[:, :lanes], x[:, lanes:]
        fr, fi = spec[:, :lanes], spec[:, lanes:]
        product = jnp.concatenate([xr * fr - xi * fi, xr * fi + xi * fr], axis=1)
        high, low = halves(product)
        y = three_pass(high, low, table_ref[0], table_ref[1], ((1,), (1,)))
        back[pl.ds(first, size), rows] = y.reshape(size, -1, 2 * lanes)

    def backward(rows):
        spectrum = [(back[0, rows, :lanes], None)]
        for k in range(1, count):
            re, im = back[k, rows, :lanes], back[k, rows, lanes:]
            c, s = turn_ref[0, k : k + 1], turn_ref[1, k : k + 1]
            spectrum.append((re * c - im * s, None if k == blocks else re * s + im * c))
        for j, y in enumerate(padded_real_dft_adjoint(spectrum)):
            out_ref[j, rows] = y.astype(bf16)

    def store(part, at):
        return pltpu.make_async_copy(out_ref.at[:, part], out_hbm.at[:, part], sems.at[1 + long_parts + at])

    if split:
        size = max(1, 256 // share)
        steps = [[slice(r, r + step_rows) for r in range(p.start, p.stop, step_rows)] for p in parts]
        groups = [(k, min(size, count - k)) for k in range(0, count, size)]

        def together(part, others):
            done = 0
            for at, (k, many) in enumerate(groups):
                multiply(k, many, part)
                upto = len(others) * (at + 1) // len(groups)
                for body, rows in others[done:upto]:
                    body(rows)
                done = upto

        ahead = 2
        for step in steps[:ahead]:
            for rows in step:
                forward(rows)
        table_load.wait()
        for at, part in enumerate(parts):
            loads[at].wait()
            if at + 2 < len(parts):
                loads[at + 2].start()
            others = [(forward, rows) for rows in (steps[at + ahead] if at + ahead < len(parts) else [])]
            others += [(backward, rows) for rows in (steps[at - 1] if at else [])]
            together(part, others)
            if at:
                store(parts[at - 1], at - 1).start()
        for rows in steps[-1]:
            backward(rows)
        store(parts[-1], len(parts) - 1).start()
        for at, part in enumerate(parts):
            store(part, at).wait()
    else:
        everything = slice(0, channels)

        @pl.loop(0, channels // step_rows)
        def _(step):
            forward(aligned(step * step_rows, step_rows))

        table_load.wait()
        loads[0].wait()
        over_frequencies(count, lambda k: multiply(k, 1, everything))

        @pl.loop(0, channels // step_rows)
        def _(step):
            backward(aligned(step * step_rows, step_rows))

        store(everything, 0).start()
        store(everything, 0).wait()


def long_convolution(arrived, spec, table):
    blocks, channels, lanes = arrived.shape
    count = blocks + 1
    return pl.pallas_call(
        long_kernel,
        in_specs=[whole, outside, outside],
        out_specs=outside,
        out_shape=jax.ShapeDtypeStruct(arrived.shape, bf16),
        scratch_shapes=[
            pltpu.VMEM((count, channels, 2 * lanes), bf16),
            pltpu.VMEM((count, channels, 2 * lanes), bf16),
            pltpu.VMEM((count, channels, 2 * lanes), f32),
            pltpu.VMEM((count, channels, 2 * lanes), f32),
            pltpu.VMEM(table.shape, bf16),
            pltpu.VMEM((2, count, lanes), f32),
            pltpu.VMEM(arrived.shape, bf16),
            pltpu.SemaphoreType.DMA((1 + 2 * long_parts,)),
        ],
        compiler_params=params(24),
        cost_estimate=cost(12 * count * channels * 4 * lanes * lanes, 12 * count * channels * lanes),
        name="long_convolution",
    )(arrived, in_hbm(spec), in_hbm(table))


def query_kernel(q_ref, before_ref, taps_ref, unembed_ref, targets_ref, ranks_ref, qs_ref, picked_ref, after_ref, space):
    rows, tokens = q_ref.shape

    @pl.loop(0, rows // tile, unroll=min(4, rows // tile))
    def _(at):
        part = aligned(at * tile, tile)
        before = before_ref[:, part].astype(f32)
        query_short = short_conv(q_ref[part], before[:rim], taps_ref, 0, part, space.at[at % 2])
        qs_ref[part] = jnp.concatenate(query_short, 0).T

    vocabulary = unembed_ref.shape[1]
    word = lax.broadcasted_iota(jnp.int32, (vocabulary, tokens), 0)
    chosen = (word == targets_ref[...]).astype(bf16)
    picked_ref[...] = dot(unembed_ref[...], chosen, ((1,), (0,))).astype(bf16)

    @pl.when(pl.program_id(0) == 0)
    def _():
        lists, size = ranks_ref.shape
        token = lax.broadcasted_iota(jnp.int32, (size, size), 0)
        rank = lax.broadcasted_iota(jnp.int32, (size, size), 1).astype(f32)
        at = [
            jnp.sum(jnp.where(token == ranks_ref[b : b + 1, :], rank, 0.0), axis=1, keepdims=True)
            for b in range(lists)
        ]
        column = jnp.concatenate(at, axis=0)
        row_of = lax.broadcasted_iota(jnp.int32, (tokens, tokens), 0)
        col_of = lax.broadcasted_iota(jnp.int32, (tokens, tokens), 1)
        row = jnp.sum(jnp.where(row_of == col_of, column, 0.0), axis=0, keepdims=True)
        same = row_of // size == col_of // size
        after_ref[...] = jnp.where(same & (row >= column), 1.0, 0.0)


def query_side(query_input, before, short_taps, unembed, targets, rankings):
    channels, tokens = query_input.shape
    width = short_taps.shape[1]
    vocabulary = unembed.shape[1]
    rows = channels // 4
    block = pl.BlockSpec((rows, tokens), lambda i: (i, 0))
    return pl.pallas_call(
        query_kernel,
        grid=(channels // rows,),
        in_specs=[
            block,
            pl.BlockSpec((rim, rows), lambda i: (0, i)),
            pl.BlockSpec((1, width, rows), lambda i: (0, 0, i)),
            pl.BlockSpec((rows, vocabulary), lambda i: (i, 0)),
            pl.BlockSpec((1, tokens), lambda i: (0, 0)),
            pl.BlockSpec(rankings.shape, lambda i: (0, 0)),
        ],
        out_specs=[block, block, pl.BlockSpec((tokens, tokens), lambda i: (0, 0))],
        out_shape=[
            pltpu.HBM((channels, tokens), f32),
            pltpu.HBM((channels, tokens), bf16),
            pltpu.HBM((tokens, tokens), f32),
        ],
        scratch_shapes=[pltpu.VMEM((2, rim + tokens, tile), f32)],
        compiler_params=params(12),
        cost_estimate=cost(2 * channels * tokens * (vocabulary + 7), channels * (8 * tokens + 2 * vocabulary)),
        name="query_side",
    )(in_hbm(query_input), before, short_taps, in_hbm(unembed), targets.reshape(1, tokens), rankings)


def result_kernel(
    size, last, first, carried_ref, qs_out, picked_out, after_out, total_ref, _, out_hbm, next_ref, loss_ref,
    qs_ref, picked_ref, out_ref, after_ref, sems, after_sem,
):
    owners, per, tokens = carried_ref.shape
    groups = sems.shape[1]
    share = owners // groups
    loads, stores = [], []
    for g in range(groups):
        part = slice(g * share, (g + 1) * share)
        rows = slice(first, first + per)
        loads.append(
            [
                pltpu.make_async_copy(qs_out.at[part, rows], qs_ref.at[part], sems.at[0, g]),
                pltpu.make_async_copy(picked_out.at[part, rows], picked_ref.at[part], sems.at[1, g]),
            ]
        )
        stores.append(pltpu.make_async_copy(out_ref.at[part], out_hbm.at[part, rows], sems.at[2, g]))
    for pair in loads:
        for copy in pair:
            copy.start()
    after_load = pltpu.make_async_copy(after_out, after_ref, after_sem)
    after_load.start()
    total = total_ref[...]
    for g in range(groups):
        for copy in loads[g]:
            copy.wait()
        part = slice(g * share, (g + 1) * share)
        out = (qs_ref[part] * carried_ref[part].astype(f32)).astype(bf16)
        out_ref[part] = out
        stores[g].start()
        terms = out.astype(f32) * picked_ref[part].astype(f32)
        total = total + jnp.sum(terms.reshape(share * per // 8, 8, tokens), axis=0)
    next_ref[...] = total
    after_load.wait()
    if last:
        logit = jnp.sum(total, axis=0, keepdims=True)
        score = soft_cap * jnp.tanh(logit / soft_cap)
        mass = jnp.sum(after_ref[...] * jnp.exp(score), axis=1, keepdims=True)
        level = jnp.log(mass)
        lists = tokens // size
        lane = lax.broadcasted_iota(jnp.int32, (1, lists), 1)
        losses = jnp.zeros((1, lists), f32)
        for b in range(lists):
            part = slice(b * size, (b + 1) * size)
            own = jnp.sum(level[part]) - jnp.sum(score[:, part])
            losses = jnp.where(lane == b, own / size, losses)
        loss_ref[...] = losses
    for copy in stores:
        copy.wait()


def result(chunk, chunks, carried, query_short, picked, after, lists, total, out):
    owners, per, tokens = carried.shape
    local = per * chunks
    groups = math.gcd(owners, 8)
    start = out is None
    if start:
        total, out = jnp.zeros((8, tokens), f32), jnp.zeros((8, tokens), bf16)
    return pl.pallas_call(
        functools.partial(result_kernel, tokens // lists, chunk == chunks - 1, chunk * per),
        in_specs=[whole, outside, outside, outside, whole, outside],
        out_specs=[outside, whole, whole],
        out_shape=[
            jax.ShapeDtypeStruct((owners, local, tokens), bf16),
            jax.ShapeDtypeStruct((8, tokens), f32),
            jax.ShapeDtypeStruct((1, lists), f32),
        ],
        scratch_shapes=[
            pltpu.VMEM((owners, per, tokens), f32),
            pltpu.VMEM((owners, per, tokens), bf16),
            pltpu.VMEM((owners, per, tokens), bf16),
            pltpu.VMEM((tokens, tokens), f32),
            pltpu.SemaphoreType.DMA((3, groups)),
            pltpu.SemaphoreType.DMA,
        ],
        input_output_aliases={} if start else {5: 0},
        compiler_params=params(8),
        cost_estimate=cost(4 * owners * per * tokens, 10 * owners * per * tokens),
        name="result",
    )(
        carried,
        in_hbm(query_short.reshape(owners, local, tokens)),
        in_hbm(picked.reshape(owners, local, tokens)),
        in_hbm(after),
        total,
        out,
    )


def per_device(
    query_input,
    key_input,
    value_input,
    short_taps,
    long_filter,
    skip_gain,
    unembed,
    targets,
    rankings,
):
    channels, tokens = query_input.shape
    owners = lax.axis_size(token_axes)
    local = channels // owners
    lists = rankings.shape[0]
    chunks = most_chunks if local % (most_chunks * tile) == 0 else 1
    last, held_key, held_value = rims(key_input, value_input)
    before = passed_along(last, token_axes, 1)
    arrived = []
    for chunk in range(chunks):
        gated = gated_features(chunk, chunks, held_key, held_value, before, short_taps, owners)
        arrived.append(
            lax.all_to_all(gated.reshape(owners, local // chunks, tokens), token_axes, 0, 0, tiled=True)
        )
    transform = table(tokens)
    *specs, last_query = filter_spectrum(long_filter, skip_gain, transform, query_input, chunks)
    before_query = passed_along(last_query, token_axes, 1)
    arrived, before_query = lax.optimization_barrier((arrived, before_query))
    query_short, picked, after = query_side(query_input, before_query, short_taps, unembed, targets, rankings)
    returned = []
    for chunk in range(chunks):
        carried = long_convolution(arrived[chunk], specs[chunk], transform)
        returned.append(lax.all_to_all(carried, token_axes, 0, 0, tiled=True))
    total = out = None
    for chunk in range(chunks):
        out, total, losses = result(
            chunk, chunks, returned[chunk], query_short, picked, after, lists, total, out
        )
    return out.reshape(channels, tokens), losses.reshape(lists)


def solution(mesh):
    placed = (
        P(None, ("grp", "seq", "tile")),
        P(None, ("grp", "seq", "tile")),
        P(None, ("grp", "seq", "tile")),
        P(),
        P(("seq", "tile"), None),
        P(("seq", "tile")),
        P(),
        P(("grp", "seq", "tile")),
        P(("grp", "seq", "tile"), None),
    )
    return jax.shard_map(
        per_device,
        mesh=mesh,
        in_specs=placed,
        out_specs=(P(None, ("grp", "seq", "tile")), P(("grp", "seq", "tile"))),
        check_vma=False,
    )
```

```python
import functools
import math

import jax
import jax.numpy as jnp
import ml_dtypes
import numpy as np
from jax import lax
from jax.experimental import pallas as pl
from jax.experimental.pallas import tpu as pltpu
from jax.sharding import PartitionSpec as P

soft_cap = 5.0
token_axes = ("seq", "tile")
bf16 = jnp.bfloat16
f32 = jnp.float32
rim = 8
most_chunks = 1
mebibyte = 1 << 20


whole = pl.BlockSpec(memory_space=pltpu.VMEM)
outside = pl.BlockSpec(memory_space=pltpu.HBM)


def in_hbm(x):
    return pltpu.with_memory_space_constraint(x, pltpu.HBM)


def params(limit=48):
    return pltpu.CompilerParams(vmem_limit_bytes=limit * mebibyte)


def cost(flops, size):
    return pl.CostEstimate(flops=flops, bytes_accessed=size, transcendentals=0)


def dot(a, b, over):
    return lax.dot_general(a, b, ((over[0], over[1]), ((), ())), preferred_element_type=f32)


def passed_along(block, axis, distance):
    devices = range(lax.axis_size(axis))
    route = [(i - distance, i) for i in devices if i - distance in devices]
    return lax.ppermute(block, axis, route)


def c_mul(z, angle):
    re, im = z
    turns = angle / (math.pi / 4)
    nearest = round(turns)
    if abs(turns - nearest) < 1e-9:
        eighth = nearest % 8
        if eighth == 0:
            return (re, im)
        if eighth == 2:
            return (-im, re)
        if eighth == 4:
            return (-re, -im)
        if eighth == 6:
            return (im, -re)
        half = math.sqrt(0.5)
        if eighth == 1:
            return ((re - im) * half, (re + im) * half)
        if eighth == 3:
            return ((re + im) * -half, (re - im) * half)
        if eighth == 5:
            return ((im - re) * half, (re + im) * -half)
        return ((re + im) * half, (im - re) * half)
    c, s = math.cos(angle), math.sin(angle)
    return (re * c - im * s, re * s + im * c)


def c_add(a, b):
    return (a[0] + b[0], a[1] + b[1])


def c_sub(a, b):
    return (a[0] - b[0], a[1] - b[1])


def c_dft(z, sign):
    n = len(z)
    if n == 1:
        return list(z)
    even = c_dft(z[0::2], sign)
    odd = c_dft(z[1::2], sign)
    turned = [c_mul(o, sign * 2 * math.pi * p / n) for p, o in enumerate(odd)]
    return [c_add(e, o) for e, o in zip(even, turned)] + [c_sub(e, o) for e, o in zip(even, turned)]


def odd_dft(x):
    n = len(x)
    if n == 1:
        return [(x[0], None)]
    half = n // 2
    z = [c_mul((x[j], -x[j + half]), -math.pi * j / n) for j in range(half)]
    wide = c_dft(z, -1)
    out = []
    for m in range(half):
        if m % 2 == 0:
            out.append(wide[m // 2])
        else:
            re, im = wide[(n - 1 - m) // 2]
            out.append((re, -im))
    return out


def real_dft(x):
    n = len(x)
    if n == 1:
        return [(x[0], None)]
    half = n // 2
    even = real_dft([x[j] + x[j + half] for j in range(half)])
    odd = odd_dft([x[j] - x[j + half] for j in range(half)])
    out = [None] * (half + 1)
    out[0::2] = even if half > 1 else [even[0]]
    out[1::2] = odd
    return out


def padded_real_dft(x):
    n = len(x)
    out = [None] * (n + 1)
    out[0::2] = real_dft(x)
    out[1::2] = odd_dft(x)
    return out


def odd_dft_adjoint(y):
    half = len(y)
    if y[0][1] is None:
        return [y[0][0]]
    n = 2 * half
    wide = []
    for p in range(half):
        if 2 * p < half:
            wide.append(y[2 * p])
        else:
            re, im = y[n - 1 - 2 * p]
            wide.append((re, -im))
    z = c_dft(wide, 1)
    turned = [c_mul(value, math.pi * j / n) for j, value in enumerate(z)]
    return [u[0] for u in turned] + [-u[1] for u in turned]


def real_dft_adjoint(x):
    if len(x) == 1:
        return [x[0][0]]
    even = real_dft_adjoint(x[0::2])
    odd = odd_dft_adjoint(x[1::2])
    return [e + o for e, o in zip(even, odd)] + [e - o for e, o in zip(even, odd)]


def padded_real_dft_adjoint(x):
    even = real_dft_adjoint(x[0::2])
    odd = odd_dft_adjoint(x[1::2])
    return [e + o for e, o in zip(even, odd)]


tile = 128


def rim_picker(lanes):
    row = lax.broadcasted_iota(jnp.int32, (rim, lanes), 0)
    lane = lax.broadcasted_iota(jnp.int32, (rim, lanes), 1)
    return (lane == row + (lanes - rim)).astype(bf16)


def rim_kernel(k_ref, v_ref, out_ref, held_k, held_v, sems):
    pieces = sems.shape[1]
    channels, lanes = k_ref.shape
    rows = channels // pieces
    pairs = ((k_ref, held_k), (v_ref, held_v))
    parts = [slice(p * rows, (p + 1) * rows) for p in range(pieces)]
    copies = [
        [pltpu.make_async_copy(ref.at[part], held.at[part], sems.at[a, p]) for a, (ref, held) in enumerate(pairs)]
        for p, part in enumerate(parts)
    ]
    for group in copies:
        for copy in group:
            copy.start()
    picker = rim_picker(lanes)
    for part, group in zip(parts, copies):
        for copy in group:
            copy.wait()
        last = [dot(picker, held[part], ((1,), (1,))) for _, held in pairs]
        out_ref[:, part] = jnp.concatenate(last, axis=0).astype(bf16)


def rims(key_input, value_input):
    channels, tokens = key_input.shape
    pieces = 2
    return pl.pallas_call(
        rim_kernel,
        in_specs=[outside] * 2,
        out_specs=[whole] * 3,
        out_shape=[jax.ShapeDtypeStruct((2 * rim, channels), bf16)]
        + [pltpu.VMEM((channels, tokens), bf16)] * 2,
        scratch_shapes=[pltpu.SemaphoreType.DMA((2, pieces))],
        compiler_params=params(6),
        cost_estimate=cost(4 * channels * tokens * rim, 4 * channels * tokens),
        name="rims",
    )(in_hbm(key_input), in_hbm(value_input))


def short_conv(x, before, taps_ref, which, lanes, space):
    tokens = x.shape[1]
    space[:rim] = before
    space[rim:] = x.astype(f32).T
    width = taps_ref.shape[1]
    taps = [
        jnp.broadcast_to(taps_ref[which, offset : offset + 1, lanes], (8, tile)) for offset in range(width)
    ]
    out = []
    for begin in range(0, tokens, 8):
        total = taps[0] * space[rim + begin : rim + begin + 8]
        for offset in range(1, width):
            first = rim + begin - offset
            total = total + taps[offset] * space[first : first + 8]
        out.append(total)
    return out


def aligned(start, size):
    return pl.ds(pl.multiple_of(start, size), size)


def filtered(space, taps, begin):
    total = taps[0] * space[rim + begin : rim + begin + 8]
    for offset in range(1, len(taps)):
        first = rim + begin - offset
        total = total + taps[offset] * space[first : first + 8]
    return total


def tap_rows(taps_ref, which, lanes):
    return [
        jnp.broadcast_to(taps_ref[which, offset : offset + 1, lanes], (8, tile))
        for offset in range(taps_ref.shape[1])
    ]


def inner_kernel(k_ref, v_ref, taps_out, part_ref, first_ref, taps_ref, key_space, value_space, sem):
    tiles, tokens, _ = part_ref.shape
    load = pltpu.make_async_copy(taps_out, taps_ref, sem)
    load.start()
    load.wait()
    unroll = math.gcd(tiles, 4)
    for group in range(tiles // unroll):

        @pl.loop(0, unroll, unroll=unroll)
        def _(step):
            at = group * unroll + step
            lanes = aligned(at * tile, tile)
            for a, (ref, space) in enumerate(((k_ref, key_space), (v_ref, value_space))):
                turned = ref[lanes].astype(f32).T
                space[rim:] = turned
                first_ref[a, at] = turned[:rim]
            key_taps, value_taps = tap_rows(taps_ref, 1, lanes), tap_rows(taps_ref, 2, lanes)
            for begin in range(rim, tokens, 8):
                k = filtered(key_space, key_taps, begin)
                part_ref[at, begin : begin + 8] = k * filtered(value_space, value_taps, begin)


def inner_features(key_input, value_input, short_taps):
    channels, tokens = key_input.shape
    tiles = channels // tile
    return pl.pallas_call(
        inner_kernel,
        in_specs=[whole, whole, outside],
        out_specs=[whole] * 3,
        out_shape=[
            pltpu.VMEM((tiles, tokens, tile), f32),
            pltpu.VMEM((2, tiles, rim, tile), f32),
            pltpu.VMEM(short_taps.shape, f32),
        ],
        scratch_shapes=[
            pltpu.VMEM((rim + tokens, tile), f32),
            pltpu.VMEM((rim + tokens, tile), f32),
            pltpu.SemaphoreType.DMA,
        ],
        compiler_params=params(8),
        cost_estimate=cost(28 * channels * tokens, 8 * channels * tokens),
        name="inner",
    )(key_input, value_input, in_hbm(short_taps))


def gated_kernel(part_ref, first_ref, taps_ref, before_ref, out_ref, made, key_space, value_space, sems):
    tiles, tokens, _ = part_ref.shape
    (groups,) = sems.shape
    size = tiles // groups
    for g in range(groups):

        @pl.loop(0, size, unroll=size)
        def _(step):
            at = g * size + step
            lanes = aligned(at * tile, tile)
            before = before_ref[:, lanes].astype(f32)
            for a, space in enumerate((key_space, value_space)):
                space[:rim] = before[a * rim : (a + 1) * rim]
                space[rim:] = first_ref[a, at]
            k = filtered(key_space, tap_rows(taps_ref, 1, lanes), 0)
            v = filtered(value_space, tap_rows(taps_ref, 2, lanes), 0)
            made[at] = jnp.concatenate([k * v, part_ref[at, rim:]], 0).T.astype(bf16)

        here = slice(g * size, (g + 1) * size)
        pltpu.make_async_copy(made.at[here], out_ref.at[here], sems.at[g]).start()
    for g in range(groups):
        here = slice(g * size, (g + 1) * size)
        pltpu.make_async_copy(made.at[here], out_ref.at[here], sems.at[g]).wait()


def gated_features(part, first, taps, before):
    tiles, tokens, _ = part.shape
    groups = math.gcd(tiles, 8)
    return pl.pallas_call(
        gated_kernel,
        in_specs=[whole] * 4,
        out_specs=outside,
        out_shape=jax.ShapeDtypeStruct((tiles, tile, tokens), bf16),
        scratch_shapes=[
            pltpu.VMEM((tiles, tile, tokens), bf16),
            pltpu.VMEM((2 * rim, tile), f32),
            pltpu.VMEM((2 * rim, tile), f32),
            pltpu.SemaphoreType.DMA((groups,)),
        ],
        compiler_params=params(6),
        cost_estimate=cost(4 * tiles * tile * tokens, 6 * tiles * tile * tokens),
        name="gated",
    )(part, first, taps, before)


step_rows = 16
long_parts = 2


def halves(x):
    high = x.astype(bf16)
    return high, (x - high.astype(f32)).astype(bf16)


def put_spectrum(spectrum, turn_ref, high_ref, low_ref, rows, lanes):
    for at, (re, im) in enumerate(spectrum):
        if at == 0:
            im = jnp.zeros_like(re)
        else:
            c, s = turn_ref[0, at : at + 1], turn_ref[1, at : at + 1]
            if im is None:
                re, im = re * c, -(re * s)
            else:
                re, im = re * c + im * s, im * c - re * s
        for value, part in ((re, slice(0, lanes)), (im, slice(lanes, 2 * lanes))):
            high, low = halves(value)
            high_ref[at, rows, part] = high
            low_ref[at, rows, part] = low


def three_pass(ah, al, wh, wl, over):
    return dot(ah, wh, over) + (dot(al, wh, over) + dot(ah, wl, over))


def over_frequencies(count, body):
    if count <= 33:
        for k in range(count):
            body(k)
    else:
        pl.loop(0, count)(body)


def filter_kernel(taps_ref, skip_ref, table_ref, q_ref, *rest):
    *spec_refs, last_ref, ah, al, turn_ref, held, sem = rest
    load = pltpu.make_async_copy(q_ref, held, sem)
    load.start()
    put_turns(turn_ref)
    channels = taps_ref.shape[0]
    lanes = turn_ref.shape[2]
    blocks = taps_ref.shape[1] // lanes
    skip = jnp.broadcast_to(skip_ref[...], (8, channels)).T
    lane = lax.broadcasted_iota(jnp.int32, (step_rows, lanes), 1)
    for step in range(channels // step_rows):
        rows = slice(step * step_rows, (step + 1) * step_rows)
        x = [taps_ref[rows, j * lanes : (j + 1) * lanes] for j in range(blocks)]
        x[0] = x[0] + jnp.where(lane == 0, skip[rows, 0:1], 0.0)
        put_spectrum(padded_real_dft(x), turn_ref, ah, al, rows, lanes)
    per = channels // len(spec_refs)

    def one(k):
        ends = (k == 0) | (k == blocks)
        scale = jnp.where(ends, 1.0, 2.0) / (2 * blocks * lanes)
        spec = three_pass(ah[k], al[k], table_ref[0], table_ref[1], ((1,), (0,))) * scale
        for at, ref in enumerate(spec_refs):
            ref[k] = spec[at * per : (at + 1) * per]

    over_frequencies(blocks + 1, one)
    load.wait()
    last_ref[...] = dot(rim_picker(held.shape[1]), held[...], ((1,), (1,))).astype(bf16)


def put_turns(turn_ref):
    _, count, lanes = turn_ref.shape
    period = 2 * (count - 1) * lanes
    k = lax.broadcasted_iota(jnp.int32, (count, lanes), 0)
    s = lax.broadcasted_iota(jnp.int32, (count, lanes), 1)
    turn = (k * s).astype(f32) * (2 * math.pi / period)
    turn_ref[0] = jnp.cos(turn)
    turn_ref[1] = jnp.sin(turn)


def table(lanes):
    s = np.arange(lanes)
    base = 2 * np.pi * (s[:, None] * s[None, :] % lanes) / lanes
    c, n = np.cos(base), np.sin(base)
    full = np.block([[c, -n], [n, c]]).astype(np.float32)
    high = full.astype(ml_dtypes.bfloat16)
    low = (full - high.astype(np.float32)).astype(ml_dtypes.bfloat16)
    return jnp.asarray(np.stack([high, low]))


def filter_spectrum(long_filter, skip_gain, table, query_input, chunks):
    channels, length = long_filter.shape
    lanes = table.shape[2] // 2
    count = length // lanes + 1
    return pl.pallas_call(
        filter_kernel,
        in_specs=[whole, whole, whole, outside],
        out_specs=[whole] * (chunks + 1),
        out_shape=[pltpu.HBM((count, channels // chunks, 2 * lanes), f32)] * chunks
        + [pltpu.HBM((rim, query_input.shape[0]), bf16)],
        scratch_shapes=[pltpu.VMEM((count, channels, 2 * lanes), bf16)] * 2
        + [
            pltpu.VMEM((2, count, lanes), f32),
            pltpu.VMEM(query_input.shape, bf16),
            pltpu.SemaphoreType.DMA,
        ],
        compiler_params=params(24),
        cost_estimate=cost(6 * count * channels * 4 * lanes * lanes, 12 * count * channels * lanes),
        name="filter_spectrum",
    )(long_filter, skip_gain.reshape(1, channels), table, in_hbm(query_input))


def long_kernel(x_ref, spec_out, table_out, out_hbm, ah, al, back, spec_ref, table_ref, turn_ref, out_ref, sems):
    blocks, channels, lanes = x_ref.shape
    count = blocks + 1
    table_load = pltpu.make_async_copy(table_out, table_ref, sems.at[0])
    split = channels % (long_parts * step_rows) == 0 and count <= 33
    share = channels // long_parts if split else channels
    parts = [slice(first, first + share) for first in range(0, channels, share)]
    loads = [
        pltpu.make_async_copy(spec_out.at[:, part], spec_ref.at[:, part], sems.at[1 + at])
        for at, part in enumerate(parts)
    ]
    table_load.start()
    for copy in loads[:2]:
        copy.start()
    put_turns(turn_ref)

    def forward(rows):
        x = [x_ref[j, rows].astype(f32) for j in range(blocks)]
        put_spectrum(padded_real_dft(x), turn_ref, ah, al, rows, lanes)

    def multiply(first, size, rows):
        def take(ref):
            part = ref[pl.ds(first, size), rows]
            return part.reshape(size * part.shape[1], 2 * lanes)

        x = three_pass(take(ah), take(al), table_ref[0], table_ref[1], ((1,), (0,)))
        spec = take(spec_ref)
        xr, xi = x[:, :lanes], x[:, lanes:]
        fr, fi = spec[:, :lanes], spec[:, lanes:]
        product = jnp.concatenate([xr * fr - xi * fi, xr * fi + xi * fr], axis=1)
        high, low = halves(product)
        y = three_pass(high, low, table_ref[0], table_ref[1], ((1,), (1,)))
        back[pl.ds(first, size), rows] = y.reshape(size, -1, 2 * lanes)

    def backward(rows):
        spectrum = [(back[0, rows, :lanes], None)]
        for k in range(1, count):
            re, im = back[k, rows, :lanes], back[k, rows, lanes:]
            c, s = turn_ref[0, k : k + 1], turn_ref[1, k : k + 1]
            spectrum.append((re * c - im * s, None if k == blocks else re * s + im * c))
        for j, y in enumerate(padded_real_dft_adjoint(spectrum)):
            out_ref[j, rows] = y.astype(bf16)

    def store(part, at):
        return pltpu.make_async_copy(out_ref.at[:, part], out_hbm.at[:, part], sems.at[1 + long_parts + at])

    if split:
        size = max(1, 256 // share)
        steps = [[slice(r, r + step_rows) for r in range(p.start, p.stop, step_rows)] for p in parts]
        groups = [(k, min(size, count - k)) for k in range(0, count, size)]

        def together(part, others):
            done = 0
            for at, (k, many) in enumerate(groups):
                multiply(k, many, part)
                upto = len(others) * (at + 1) // len(groups)
                for body, rows in others[done:upto]:
                    body(rows)
                done = upto

        ahead = 2
        for step in steps[:ahead]:
            for rows in step:
                forward(rows)
        table_load.wait()
        for at, part in enumerate(parts):
            loads[at].wait()
            if at + 2 < len(parts):
                loads[at + 2].start()
            others = [(forward, rows) for rows in (steps[at + ahead] if at + ahead < len(parts) else [])]
            others += [(backward, rows) for rows in (steps[at - 1] if at else [])]
            together(part, others)
            if at:
                store(parts[at - 1], at - 1).start()
        for rows in steps[-1]:
            backward(rows)
        store(parts[-1], len(parts) - 1).start()
        for at, part in enumerate(parts):
            store(part, at).wait()
    else:
        everything = slice(0, channels)

        @pl.loop(0, channels // step_rows)
        def _(step):
            forward(aligned(step * step_rows, step_rows))

        table_load.wait()
        loads[0].wait()
        over_frequencies(count, lambda k: multiply(k, 1, everything))

        @pl.loop(0, channels // step_rows)
        def _(step):
            backward(aligned(step * step_rows, step_rows))

        store(everything, 0).start()
        store(everything, 0).wait()


def long_convolution(arrived, spec, table):
    blocks, channels, lanes = arrived.shape
    count = blocks + 1
    return pl.pallas_call(
        long_kernel,
        in_specs=[whole, outside, outside],
        out_specs=outside,
        out_shape=jax.ShapeDtypeStruct(arrived.shape, bf16),
        scratch_shapes=[
            pltpu.VMEM((count, channels, 2 * lanes), bf16),
            pltpu.VMEM((count, channels, 2 * lanes), bf16),
            pltpu.VMEM((count, channels, 2 * lanes), f32),
            pltpu.VMEM((count, channels, 2 * lanes), f32),
            pltpu.VMEM(table.shape, bf16),
            pltpu.VMEM((2, count, lanes), f32),
            pltpu.VMEM(arrived.shape, bf16),
            pltpu.SemaphoreType.DMA((1 + 2 * long_parts,)),
        ],
        compiler_params=params(24),
        cost_estimate=cost(12 * count * channels * 4 * lanes * lanes, 12 * count * channels * lanes),
        name="long_convolution",
    )(arrived, in_hbm(spec), in_hbm(table))


def query_kernel(q_ref, before_ref, taps_ref, unembed_ref, targets_ref, ranks_ref, qs_ref, picked_ref, after_ref, space):
    rows, tokens = q_ref.shape

    @pl.loop(0, rows // tile, unroll=min(4, rows // tile))
    def _(at):
        part = aligned(at * tile, tile)
        before = before_ref[:, part].astype(f32)
        query_short = short_conv(q_ref[part], before[:rim], taps_ref, 0, part, space.at[at % 2])
        qs_ref[part] = jnp.concatenate(query_short, 0).T

    vocabulary = unembed_ref.shape[1]
    word = lax.broadcasted_iota(jnp.int32, (vocabulary, tokens), 0)
    chosen = (word == targets_ref[...]).astype(bf16)
    picked_ref[...] = dot(unembed_ref[...], chosen, ((1,), (0,))).astype(bf16)

    @pl.when(pl.program_id(0) == 0)
    def _():
        lists, size = ranks_ref.shape
        token = lax.broadcasted_iota(jnp.int32, (size, size), 0)
        rank = lax.broadcasted_iota(jnp.int32, (size, size), 1).astype(f32)
        at = [
            jnp.sum(jnp.where(token == ranks_ref[b : b + 1, :], rank, 0.0), axis=1, keepdims=True)
            for b in range(lists)
        ]
        column = jnp.concatenate(at, axis=0)
        row_of = lax.broadcasted_iota(jnp.int32, (tokens, tokens), 0)
        col_of = lax.broadcasted_iota(jnp.int32, (tokens, tokens), 1)
        row = jnp.sum(jnp.where(row_of == col_of, column, 0.0), axis=0, keepdims=True)
        same = row_of // size == col_of // size
        after_ref[...] = jnp.where(same & (row >= column), 1.0, 0.0)


def query_side(query_input, before, short_taps, unembed, targets, rankings):
    channels, tokens = query_input.shape
    width = short_taps.shape[1]
    vocabulary = unembed.shape[1]
    rows = channels // 4
    block = pl.BlockSpec((rows, tokens), lambda i: (i, 0))
    return pl.pallas_call(
        query_kernel,
        grid=(channels // rows,),
        in_specs=[
            block,
            pl.BlockSpec((rim, rows), lambda i: (0, i)),
            pl.BlockSpec((1, width, rows), lambda i: (0, 0, i)),
            pl.BlockSpec((rows, vocabulary), lambda i: (i, 0)),
            pl.BlockSpec((1, tokens), lambda i: (0, 0)),
            pl.BlockSpec(rankings.shape, lambda i: (0, 0)),
        ],
        out_specs=[block, block, pl.BlockSpec((tokens, tokens), lambda i: (0, 0))],
        out_shape=[
            pltpu.HBM((channels, tokens), f32),
            pltpu.HBM((channels, tokens), bf16),
            pltpu.HBM((tokens, tokens), f32),
        ],
        scratch_shapes=[pltpu.VMEM((2, rim + tokens, tile), f32)],
        compiler_params=params(12),
        cost_estimate=cost(2 * channels * tokens * (vocabulary + 7), channels * (8 * tokens + 2 * vocabulary)),
        name="query_side",
    )(in_hbm(query_input), before, short_taps, in_hbm(unembed), targets.reshape(1, tokens), rankings)


def result_kernel(
    size, last, first, carried_ref, qs_out, picked_out, after_out, total_ref, _, out_hbm, next_ref, loss_ref,
    qs_ref, picked_ref, out_ref, after_ref, sems, after_sem,
):
    owners, per, tokens = carried_ref.shape
    groups = sems.shape[1]
    share = owners // groups
    loads, stores = [], []
    for g in range(groups):
        part = slice(g * share, (g + 1) * share)
        rows = slice(first, first + per)
        loads.append(
            [
                pltpu.make_async_copy(qs_out.at[part, rows], qs_ref.at[part], sems.at[0, g]),
                pltpu.make_async_copy(picked_out.at[part, rows], picked_ref.at[part], sems.at[1, g]),
            ]
        )
        stores.append(pltpu.make_async_copy(out_ref.at[part], out_hbm.at[part, rows], sems.at[2, g]))
    for pair in loads:
        for copy in pair:
            copy.start()
    after_load = pltpu.make_async_copy(after_out, after_ref, after_sem)
    after_load.start()
    total = total_ref[...]
    for g in range(groups):
        for copy in loads[g]:
            copy.wait()
        part = slice(g * share, (g + 1) * share)
        out = (qs_ref[part] * carried_ref[part].astype(f32)).astype(bf16)
        out_ref[part] = out
        stores[g].start()
        terms = out.astype(f32) * picked_ref[part].astype(f32)
        total = total + jnp.sum(terms.reshape(share * per // 8, 8, tokens), axis=0)
    next_ref[...] = total
    after_load.wait()
    if last:
        logit = jnp.sum(total, axis=0, keepdims=True)
        score = soft_cap * jnp.tanh(logit / soft_cap)
        mass = jnp.sum(after_ref[...] * jnp.exp(score), axis=1, keepdims=True)
        level = jnp.log(mass)
        lists = tokens // size
        lane = lax.broadcasted_iota(jnp.int32, (1, lists), 1)
        losses = jnp.zeros((1, lists), f32)
        for b in range(lists):
            part = slice(b * size, (b + 1) * size)
            own = jnp.sum(level[part]) - jnp.sum(score[:, part])
            losses = jnp.where(lane == b, own / size, losses)
        loss_ref[...] = losses
    for copy in stores:
        copy.wait()


def result(chunk, chunks, carried, query_short, picked, after, lists, total, out):
    owners, per, tokens = carried.shape
    local = per * chunks
    groups = math.gcd(owners, 8)
    start = out is None
    if start:
        total, out = jnp.zeros((8, tokens), f32), jnp.zeros((8, tokens), bf16)
    return pl.pallas_call(
        functools.partial(result_kernel, tokens // lists, chunk == chunks - 1, chunk * per),
        in_specs=[whole, outside, outside, outside, whole, outside],
        out_specs=[outside, whole, whole],
        out_shape=[
            jax.ShapeDtypeStruct((owners, local, tokens), bf16),
            jax.ShapeDtypeStruct((8, tokens), f32),
            jax.ShapeDtypeStruct((1, lists), f32),
        ],
        scratch_shapes=[
            pltpu.VMEM((owners, per, tokens), f32),
            pltpu.VMEM((owners, per, tokens), bf16),
            pltpu.VMEM((owners, per, tokens), bf16),
            pltpu.VMEM((tokens, tokens), f32),
            pltpu.SemaphoreType.DMA((3, groups)),
            pltpu.SemaphoreType.DMA,
        ],
        input_output_aliases={} if start else {5: 0},
        compiler_params=params(8),
        cost_estimate=cost(4 * owners * per * tokens, 10 * owners * per * tokens),
        name="result",
    )(
        carried,
        in_hbm(query_short.reshape(owners, local, tokens)),
        in_hbm(picked.reshape(owners, local, tokens)),
        in_hbm(after),
        total,
        out,
    )


def per_device(
    query_input,
    key_input,
    value_input,
    short_taps,
    long_filter,
    skip_gain,
    unembed,
    targets,
    rankings,
):
    channels, tokens = query_input.shape
    owners = lax.axis_size(token_axes)
    local = channels // owners
    lists = rankings.shape[0]
    chunks = most_chunks if local % (most_chunks * tile) == 0 else 1
    last, held_key, held_value = rims(key_input, value_input)
    before = passed_along(last, token_axes, 1)
    inner = inner_features(held_key, held_value, short_taps)
    gated = gated_features(*inner, before).reshape(owners, chunks, local // chunks, tokens)
    arrived = [
        lax.all_to_all(gated[:, chunk], token_axes, 0, 0, tiled=True) for chunk in range(chunks)
    ]
    transform = table(tokens)
    *specs, last_query = filter_spectrum(long_filter, skip_gain, transform, query_input, chunks)
    before_query = passed_along(last_query, token_axes, 1)
    arrived, before_query = lax.optimization_barrier((arrived, before_query))
    query_short, picked, after = query_side(query_input, before_query, short_taps, unembed, targets, rankings)
    returned = []
    for chunk in range(chunks):
        carried = long_convolution(arrived[chunk], specs[chunk], transform)
        returned.append(lax.all_to_all(carried, token_axes, 0, 0, tiled=True))
    total = out = None
    for chunk in range(chunks):
        out, total, losses = result(
            chunk, chunks, returned[chunk], query_short, picked, after, lists, total, out
        )
    return out.reshape(channels, tokens), losses.reshape(lists)


def solution(mesh):
    placed = (
        P(None, ("grp", "seq", "tile")),
        P(None, ("grp", "seq", "tile")),
        P(None, ("grp", "seq", "tile")),
        P(),
        P(("seq", "tile"), None),
        P(("seq", "tile")),
        P(),
        P(("grp", "seq", "tile")),
        P(("grp", "seq", "tile"), None),
    )
    return jax.shard_map(
        per_device,
        mesh=mesh,
        in_specs=placed,
        out_specs=(P(None, ("grp", "seq", "tile")), P(("grp", "seq", "tile"))),
        check_vma=False,
    )
```

```python
import functools
import math

import jax
import jax.numpy as jnp
import ml_dtypes
import numpy as np
from jax import lax
from jax.experimental import pallas as pl
from jax.experimental.pallas import tpu as pltpu
from jax.sharding import PartitionSpec as P

soft_cap = 5.0
token_axes = ("seq", "tile")
bf16 = jnp.bfloat16
f32 = jnp.float32
rim = 8
most_chunks = 1
mebibyte = 1 << 20


whole = pl.BlockSpec(memory_space=pltpu.VMEM)
outside = pl.BlockSpec(memory_space=pltpu.HBM)


def in_hbm(x):
    return pltpu.with_memory_space_constraint(x, pltpu.HBM)


def params(limit=48):
    return pltpu.CompilerParams(vmem_limit_bytes=limit * mebibyte)


def cost(flops, size):
    return pl.CostEstimate(flops=flops, bytes_accessed=size, transcendentals=0)


def dot(a, b, over):
    return lax.dot_general(a, b, ((over[0], over[1]), ((), ())), preferred_element_type=f32)


def passed_along(block, axis, distance):
    devices = range(lax.axis_size(axis))
    route = [(i - distance, i) for i in devices if i - distance in devices]
    return lax.ppermute(block, axis, route)


def c_mul(z, angle):
    re, im = z
    turns = angle / (math.pi / 4)
    nearest = round(turns)
    if abs(turns - nearest) < 1e-9:
        eighth = nearest % 8
        if eighth == 0:
            return (re, im)
        if eighth == 2:
            return (-im, re)
        if eighth == 4:
            return (-re, -im)
        if eighth == 6:
            return (im, -re)
        half = math.sqrt(0.5)
        if eighth == 1:
            return ((re - im) * half, (re + im) * half)
        if eighth == 3:
            return ((re + im) * -half, (re - im) * half)
        if eighth == 5:
            return ((im - re) * half, (re + im) * -half)
        return ((re + im) * half, (im - re) * half)
    c, s = math.cos(angle), math.sin(angle)
    return (re * c - im * s, re * s + im * c)


def c_add(a, b):
    return (a[0] + b[0], a[1] + b[1])


def c_sub(a, b):
    return (a[0] - b[0], a[1] - b[1])


def c_dft(z, sign):
    n = len(z)
    if n == 1:
        return list(z)
    even = c_dft(z[0::2], sign)
    odd = c_dft(z[1::2], sign)
    turned = [c_mul(o, sign * 2 * math.pi * p / n) for p, o in enumerate(odd)]
    return [c_add(e, o) for e, o in zip(even, turned)] + [c_sub(e, o) for e, o in zip(even, turned)]


def odd_dft(x):
    n = len(x)
    if n == 1:
        return [(x[0], None)]
    half = n // 2
    z = [c_mul((x[j], -x[j + half]), -math.pi * j / n) for j in range(half)]
    wide = c_dft(z, -1)
    out = []
    for m in range(half):
        if m % 2 == 0:
            out.append(wide[m // 2])
        else:
            re, im = wide[(n - 1 - m) // 2]
            out.append((re, -im))
    return out


def real_dft(x):
    n = len(x)
    if n == 1:
        return [(x[0], None)]
    half = n // 2
    even = real_dft([x[j] + x[j + half] for j in range(half)])
    odd = odd_dft([x[j] - x[j + half] for j in range(half)])
    out = [None] * (half + 1)
    out[0::2] = even if half > 1 else [even[0]]
    out[1::2] = odd
    return out


def padded_real_dft(x):
    n = len(x)
    out = [None] * (n + 1)
    out[0::2] = real_dft(x)
    out[1::2] = odd_dft(x)
    return out


def odd_dft_adjoint(y):
    half = len(y)
    if y[0][1] is None:
        return [y[0][0]]
    n = 2 * half
    wide = []
    for p in range(half):
        if 2 * p < half:
            wide.append(y[2 * p])
        else:
            re, im = y[n - 1 - 2 * p]
            wide.append((re, -im))
    z = c_dft(wide, 1)
    turned = [c_mul(value, math.pi * j / n) for j, value in enumerate(z)]
    return [u[0] for u in turned] + [-u[1] for u in turned]


def real_dft_adjoint(x):
    if len(x) == 1:
        return [x[0][0]]
    even = real_dft_adjoint(x[0::2])
    odd = odd_dft_adjoint(x[1::2])
    return [e + o for e, o in zip(even, odd)] + [e - o for e, o in zip(even, odd)]


def padded_real_dft_adjoint(x):
    even = real_dft_adjoint(x[0::2])
    odd = odd_dft_adjoint(x[1::2])
    return [e + o for e, o in zip(even, odd)]


tile = 128


def rim_picker(lanes):
    row = lax.broadcasted_iota(jnp.int32, (rim, lanes), 0)
    lane = lax.broadcasted_iota(jnp.int32, (rim, lanes), 1)
    return (lane == row + (lanes - rim)).astype(bf16)


def rim_kernel(k_ref, v_ref, out_ref, held_k, held_v, sems):
    pieces = sems.shape[1]
    channels, lanes = k_ref.shape
    rows = channels // pieces
    pairs = ((k_ref, held_k), (v_ref, held_v))
    parts = [slice(p * rows, (p + 1) * rows) for p in range(pieces)]
    copies = [
        [pltpu.make_async_copy(ref.at[part], held.at[part], sems.at[a, p]) for a, (ref, held) in enumerate(pairs)]
        for p, part in enumerate(parts)
    ]
    for group in copies:
        for copy in group:
            copy.start()
    picker = rim_picker(lanes)
    for part, group in zip(parts, copies):
        for copy in group:
            copy.wait()
        last = [dot(picker, held[part], ((1,), (1,))) for _, held in pairs]
        out_ref[:, part] = jnp.concatenate(last, axis=0).astype(bf16)


def rims(key_input, value_input):
    channels, tokens = key_input.shape
    pieces = 2
    return pl.pallas_call(
        rim_kernel,
        in_specs=[outside] * 2,
        out_specs=[whole] * 3,
        out_shape=[jax.ShapeDtypeStruct((2 * rim, channels), bf16)]
        + [pltpu.VMEM((channels, tokens), bf16)] * 2,
        scratch_shapes=[pltpu.SemaphoreType.DMA((2, pieces))],
        compiler_params=params(6),
        cost_estimate=cost(4 * channels * tokens * rim, 4 * channels * tokens),
        name="rims",
    )(in_hbm(key_input), in_hbm(value_input))


def short_conv(x, before, taps_ref, which, lanes, space):
    tokens = x.shape[1]
    space[:rim] = before
    space[rim:] = x.astype(f32).T
    width = taps_ref.shape[1]
    taps = [
        jnp.broadcast_to(taps_ref[which, offset : offset + 1, lanes], (8, tile)) for offset in range(width)
    ]
    out = []
    for begin in range(0, tokens, 8):
        total = taps[0] * space[rim + begin : rim + begin + 8]
        for offset in range(1, width):
            first = rim + begin - offset
            total = total + taps[offset] * space[first : first + 8]
        out.append(total)
    return out


def aligned(start, size):
    return pl.ds(pl.multiple_of(start, size), size)


def filtered(space, taps, begin):
    total = taps[0] * space[rim + begin : rim + begin + 8]
    for offset in range(1, len(taps)):
        first = rim + begin - offset
        total = total + taps[offset] * space[first : first + 8]
    return total


def tap_rows(taps_ref, which, lanes):
    return [
        jnp.broadcast_to(taps_ref[which, offset : offset + 1, lanes], (8, tile))
        for offset in range(taps_ref.shape[1])
    ]


def inner_kernel(k_ref, v_ref, taps_out, part_ref, first_ref, taps_ref, key_space, value_space, sem):
    tiles, tokens, _ = part_ref.shape
    load = pltpu.make_async_copy(taps_out, taps_ref, sem)
    load.start()
    load.wait()
    unroll = math.gcd(tiles, 4)
    for group in range(tiles // unroll):

        @pl.loop(0, unroll, unroll=unroll)
        def _(step):
            at = group * unroll + step
            lanes = aligned(at * tile, tile)
            for a, (ref, space) in enumerate(((k_ref, key_space), (v_ref, value_space))):
                turned = ref[lanes].astype(f32).T
                space[rim:] = turned
                first_ref[a, at] = turned[:rim]
            key_taps, value_taps = tap_rows(taps_ref, 1, lanes), tap_rows(taps_ref, 2, lanes)
            for begin in range(rim, tokens, 8):
                k = filtered(key_space, key_taps, begin)
                part_ref[at, begin : begin + 8] = k * filtered(value_space, value_taps, begin)


def inner_features(key_input, value_input, short_taps):
    channels, tokens = key_input.shape
    tiles = channels // tile
    return pl.pallas_call(
        inner_kernel,
        in_specs=[whole, whole, outside],
        out_specs=[whole] * 3,
        out_shape=[
            pltpu.VMEM((tiles, tokens, tile), f32),
            pltpu.VMEM((2, tiles, rim, tile), f32),
            pltpu.VMEM(short_taps.shape, f32),
        ],
        scratch_shapes=[
            pltpu.VMEM((rim + tokens, tile), f32),
            pltpu.VMEM((rim + tokens, tile), f32),
            pltpu.SemaphoreType.DMA,
        ],
        compiler_params=params(8),
        cost_estimate=cost(28 * channels * tokens, 8 * channels * tokens),
        name="inner",
    )(key_input, value_input, in_hbm(short_taps))


def gated_kernel(part_ref, first_ref, taps_ref, before_ref, out_ref, made, key_space, value_space, sems):
    tiles, tokens, _ = part_ref.shape
    (groups,) = sems.shape
    size = tiles // groups
    for g in range(groups):

        @pl.loop(0, size, unroll=size)
        def _(step):
            at = g * size + step
            lanes = aligned(at * tile, tile)
            before = before_ref[:, lanes].astype(f32)
            for a, space in enumerate((key_space, value_space)):
                space[:rim] = before[a * rim : (a + 1) * rim]
                space[rim:] = first_ref[a, at]
            k = filtered(key_space, tap_rows(taps_ref, 1, lanes), 0)
            v = filtered(value_space, tap_rows(taps_ref, 2, lanes), 0)
            made[at] = jnp.concatenate([k * v, part_ref[at, rim:]], 0).T.astype(bf16)

        here = slice(g * size, (g + 1) * size)
        pltpu.make_async_copy(made.at[here], out_ref.at[here], sems.at[g]).start()
    for g in range(groups):
        here = slice(g * size, (g + 1) * size)
        pltpu.make_async_copy(made.at[here], out_ref.at[here], sems.at[g]).wait()


def gated_features(part, first, taps, before):
    tiles, tokens, _ = part.shape
    groups = math.gcd(tiles, 8)
    return pl.pallas_call(
        gated_kernel,
        in_specs=[whole] * 4,
        out_specs=outside,
        out_shape=jax.ShapeDtypeStruct((tiles, tile, tokens), bf16),
        scratch_shapes=[
            pltpu.VMEM((tiles, tile, tokens), bf16),
            pltpu.VMEM((2 * rim, tile), f32),
            pltpu.VMEM((2 * rim, tile), f32),
            pltpu.SemaphoreType.DMA((groups,)),
        ],
        compiler_params=params(6),
        cost_estimate=cost(4 * tiles * tile * tokens, 6 * tiles * tile * tokens),
        name="gated",
    )(part, first, taps, before)


step_rows = 16
long_parts = 2


def halves(x):
    high = x.astype(bf16)
    return high, (x - high.astype(f32)).astype(bf16)


def put_spectrum(spectrum, turn_ref, high_ref, low_ref, rows, lanes):
    for at, (re, im) in enumerate(spectrum):
        if at == 0:
            im = jnp.zeros_like(re)
        else:
            c, s = turn_ref[0, at : at + 1], turn_ref[1, at : at + 1]
            if im is None:
                re, im = re * c, -(re * s)
            else:
                re, im = re * c + im * s, im * c - re * s
        for value, part in ((re, slice(0, lanes)), (im, slice(lanes, 2 * lanes))):
            high, low = halves(value)
            high_ref[at, rows, part] = high
            if low_ref is not None:
                low_ref[at, rows, part] = low


def three_pass(ah, al, wh, wl, over):
    return dot(ah, wh, over) + (dot(al, wh, over) + dot(ah, wl, over))


def two_pass(a, wh, wl, over):
    return dot(a, wh, over) + dot(a, wl, over)


def over_frequencies(count, body):
    if count <= 33:
        for k in range(count):
            body(k)
    else:
        pl.loop(0, count)(body)


def filter_kernel(taps_ref, skip_ref, table_ref, q_ref, *rest):
    *spec_refs, last_ref, ah, al, turn_ref, held, sem = rest
    load = pltpu.make_async_copy(q_ref, held, sem)
    load.start()
    put_turns(turn_ref)
    channels = taps_ref.shape[0]
    lanes = turn_ref.shape[2]
    blocks = taps_ref.shape[1] // lanes
    skip = jnp.broadcast_to(skip_ref[...], (8, channels)).T
    lane = lax.broadcasted_iota(jnp.int32, (step_rows, lanes), 1)
    for step in range(channels // step_rows):
        rows = slice(step * step_rows, (step + 1) * step_rows)
        x = [taps_ref[rows, j * lanes : (j + 1) * lanes] for j in range(blocks)]
        x[0] = x[0] + jnp.where(lane == 0, skip[rows, 0:1], 0.0)
        put_spectrum(padded_real_dft(x), turn_ref, ah, al, rows, lanes)
    per = channels // len(spec_refs)

    def one(k):
        ends = (k == 0) | (k == blocks)
        scale = jnp.where(ends, 1.0, 2.0) / (2 * blocks * lanes)
        spec = three_pass(ah[k], al[k], table_ref[0], table_ref[1], ((1,), (0,))) * scale
        for at, ref in enumerate(spec_refs):
            ref[k] = spec[at * per : (at + 1) * per]

    over_frequencies(blocks + 1, one)
    load.wait()
    last_ref[...] = dot(rim_picker(held.shape[1]), held[...], ((1,), (1,))).astype(bf16)


def put_turns(turn_ref):
    _, count, lanes = turn_ref.shape
    period = 2 * (count - 1) * lanes
    k = lax.broadcasted_iota(jnp.int32, (count, lanes), 0)
    s = lax.broadcasted_iota(jnp.int32, (count, lanes), 1)
    turn = (k * s).astype(f32) * (2 * math.pi / period)
    turn_ref[0] = jnp.cos(turn)
    turn_ref[1] = jnp.sin(turn)


def table(lanes):
    s = np.arange(lanes)
    base = 2 * np.pi * (s[:, None] * s[None, :] % lanes) / lanes
    c, n = np.cos(base), np.sin(base)
    full = np.block([[c, -n], [n, c]]).astype(np.float32)
    high = full.astype(ml_dtypes.bfloat16)
    low = (full - high.astype(np.float32)).astype(ml_dtypes.bfloat16)
    return jnp.asarray(np.stack([high, low]))


def filter_spectrum(long_filter, skip_gain, table, query_input, chunks):
    channels, length = long_filter.shape
    lanes = table.shape[2] // 2
    count = length // lanes + 1
    return pl.pallas_call(
        filter_kernel,
        in_specs=[whole, whole, whole, outside],
        out_specs=[whole] * (chunks + 1),
        out_shape=[pltpu.HBM((count, channels // chunks, 2 * lanes), f32)] * chunks
        + [pltpu.HBM((rim, query_input.shape[0]), bf16)],
        scratch_shapes=[pltpu.VMEM((count, channels, 2 * lanes), bf16)] * 2
        + [
            pltpu.VMEM((2, count, lanes), f32),
            pltpu.VMEM(query_input.shape, bf16),
            pltpu.SemaphoreType.DMA,
        ],
        compiler_params=params(24),
        cost_estimate=cost(6 * count * channels * 4 * lanes * lanes, 12 * count * channels * lanes),
        name="filter_spectrum",
    )(long_filter, skip_gain.reshape(1, channels), table, in_hbm(query_input))


def long_kernel(x_ref, spec_out, table_out, out_hbm, ah, back, spec_ref, table_ref, turn_ref, out_ref, sems):
    blocks, channels, lanes = x_ref.shape
    count = blocks + 1
    table_load = pltpu.make_async_copy(table_out, table_ref, sems.at[0])
    split = channels % (long_parts * step_rows) == 0 and count <= 33
    share = channels // long_parts if split else channels
    parts = [slice(first, first + share) for first in range(0, channels, share)]
    loads = [
        pltpu.make_async_copy(spec_out.at[:, part], spec_ref.at[:, part], sems.at[1 + at])
        for at, part in enumerate(parts)
    ]
    table_load.start()
    for copy in loads[:2]:
        copy.start()
    put_turns(turn_ref)

    def forward(rows):
        x = [x_ref[j, rows].astype(f32) for j in range(blocks)]
        put_spectrum(padded_real_dft(x), turn_ref, ah, None, rows, lanes)

    def multiply(first, size, rows):
        def take(ref):
            part = ref[pl.ds(first, size), rows]
            return part.reshape(size * part.shape[1], 2 * lanes)

        x = two_pass(take(ah), table_ref[0], table_ref[1], ((1,), (0,)))
        spec = take(spec_ref)
        xr, xi = x[:, :lanes], x[:, lanes:]
        fr, fi = spec[:, :lanes], spec[:, lanes:]
        product = jnp.concatenate([xr * fr - xi * fi, xr * fi + xi * fr], axis=1)
        y = two_pass(product.astype(bf16), table_ref[0], table_ref[1], ((1,), (1,)))
        back[pl.ds(first, size), rows] = y.reshape(size, -1, 2 * lanes)

    def backward(rows):
        spectrum = [(back[0, rows, :lanes], None)]
        for k in range(1, count):
            re, im = back[k, rows, :lanes], back[k, rows, lanes:]
            c, s = turn_ref[0, k : k + 1], turn_ref[1, k : k + 1]
            spectrum.append((re * c - im * s, None if k == blocks else re * s + im * c))
        for j, y in enumerate(padded_real_dft_adjoint(spectrum)):
            out_ref[j, rows] = y.astype(bf16)

    def store(part, at):
        return pltpu.make_async_copy(out_ref.at[:, part], out_hbm.at[:, part], sems.at[1 + long_parts + at])

    if split:
        size = max(1, 256 // share)
        steps = [[slice(r, r + step_rows) for r in range(p.start, p.stop, step_rows)] for p in parts]
        groups = [(k, min(size, count - k)) for k in range(0, count, size)]

        def together(part, others):
            done = 0
            for at, (k, many) in enumerate(groups):
                multiply(k, many, part)
                upto = len(others) * (at + 1) // len(groups)
                for body, rows in others[done:upto]:
                    body(rows)
                done = upto

        ahead = 2
        for step in steps[:ahead]:
            for rows in step:
                forward(rows)
        table_load.wait()
        for at, part in enumerate(parts):
            loads[at].wait()
            if at + 2 < len(parts):
                loads[at + 2].start()
            others = [(forward, rows) for rows in (steps[at + ahead] if at + ahead < len(parts) else [])]
            others += [(backward, rows) for rows in (steps[at - 1] if at else [])]
            together(part, others)
            if at:
                store(parts[at - 1], at - 1).start()
        for rows in steps[-1]:
            backward(rows)
        store(parts[-1], len(parts) - 1).start()
        for at, part in enumerate(parts):
            store(part, at).wait()
    else:
        everything = slice(0, channels)

        @pl.loop(0, channels // step_rows)
        def _(step):
            forward(aligned(step * step_rows, step_rows))

        table_load.wait()
        loads[0].wait()
        over_frequencies(count, lambda k: multiply(k, 1, everything))

        @pl.loop(0, channels // step_rows)
        def _(step):
            backward(aligned(step * step_rows, step_rows))

        store(everything, 0).start()
        store(everything, 0).wait()


def long_convolution(arrived, spec, table):
    blocks, channels, lanes = arrived.shape
    count = blocks + 1
    return pl.pallas_call(
        long_kernel,
        in_specs=[whole, outside, outside],
        out_specs=outside,
        out_shape=jax.ShapeDtypeStruct(arrived.shape, bf16),
        scratch_shapes=[
            pltpu.VMEM((count, channels, 2 * lanes), bf16),
            pltpu.VMEM((count, channels, 2 * lanes), f32),
            pltpu.VMEM((count, channels, 2 * lanes), f32),
            pltpu.VMEM(table.shape, bf16),
            pltpu.VMEM((2, count, lanes), f32),
            pltpu.VMEM(arrived.shape, bf16),
            pltpu.SemaphoreType.DMA((1 + 2 * long_parts,)),
        ],
        compiler_params=params(24),
        cost_estimate=cost(12 * count * channels * 4 * lanes * lanes, 12 * count * channels * lanes),
        name="long_convolution",
    )(arrived, in_hbm(spec), in_hbm(table))


def query_kernel(q_ref, before_ref, taps_ref, unembed_ref, targets_ref, ranks_ref, qs_ref, picked_ref, after_ref, space):
    rows, tokens = q_ref.shape

    @pl.loop(0, rows // tile, unroll=min(4, rows // tile))
    def _(at):
        part = aligned(at * tile, tile)
        before = before_ref[:, part].astype(f32)
        query_short = short_conv(q_ref[part], before[:rim], taps_ref, 0, part, space.at[at % 2])
        qs_ref[part] = jnp.concatenate(query_short, 0).T

    vocabulary = unembed_ref.shape[1]
    word = lax.broadcasted_iota(jnp.int32, (vocabulary, tokens), 0)
    chosen = (word == targets_ref[...]).astype(bf16)
    picked_ref[...] = dot(unembed_ref[...], chosen, ((1,), (0,))).astype(bf16)

    @pl.when(pl.program_id(0) == 0)
    def _():
        lists, size = ranks_ref.shape
        token = lax.broadcasted_iota(jnp.int32, (size, size), 0)
        rank = lax.broadcasted_iota(jnp.int32, (size, size), 1).astype(f32)
        at = [
            jnp.sum(jnp.where(token == ranks_ref[b : b + 1, :], rank, 0.0), axis=1, keepdims=True)
            for b in range(lists)
        ]
        column = jnp.concatenate(at, axis=0)
        row_of = lax.broadcasted_iota(jnp.int32, (tokens, tokens), 0)
        col_of = lax.broadcasted_iota(jnp.int32, (tokens, tokens), 1)
        row = jnp.sum(jnp.where(row_of == col_of, column, 0.0), axis=0, keepdims=True)
        same = row_of // size == col_of // size
        after_ref[...] = jnp.where(same & (row >= column), 1.0, 0.0)


def query_side(query_input, before, short_taps, unembed, targets, rankings):
    channels, tokens = query_input.shape
    width = short_taps.shape[1]
    vocabulary = unembed.shape[1]
    rows = channels // 4
    block = pl.BlockSpec((rows, tokens), lambda i: (i, 0))
    return pl.pallas_call(
        query_kernel,
        grid=(channels // rows,),
        in_specs=[
            block,
            pl.BlockSpec((rim, rows), lambda i: (0, i)),
            pl.BlockSpec((1, width, rows), lambda i: (0, 0, i)),
            pl.BlockSpec((rows, vocabulary), lambda i: (i, 0)),
            pl.BlockSpec((1, tokens), lambda i: (0, 0)),
            pl.BlockSpec(rankings.shape, lambda i: (0, 0)),
        ],
        out_specs=[block, block, pl.BlockSpec((tokens, tokens), lambda i: (0, 0))],
        out_shape=[
            pltpu.HBM((channels, tokens), f32),
            pltpu.HBM((channels, tokens), bf16),
            pltpu.HBM((tokens, tokens), f32),
        ],
        scratch_shapes=[pltpu.VMEM((2, rim + tokens, tile), f32)],
        compiler_params=params(12),
        cost_estimate=cost(2 * channels * tokens * (vocabulary + 7), channels * (8 * tokens + 2 * vocabulary)),
        name="query_side",
    )(in_hbm(query_input), before, short_taps, in_hbm(unembed), targets.reshape(1, tokens), rankings)


def result_kernel(
    size, last, first, carried_ref, qs_out, picked_out, after_out, total_ref, _, out_hbm, next_ref, loss_ref,
    qs_ref, picked_ref, out_ref, after_ref, sems, after_sem,
):
    owners, per, tokens = carried_ref.shape
    groups = sems.shape[1]
    share = owners // groups
    loads, stores = [], []
    for g in range(groups):
        part = slice(g * share, (g + 1) * share)
        rows = slice(first, first + per)
        loads.append(
            [
                pltpu.make_async_copy(qs_out.at[part, rows], qs_ref.at[part], sems.at[0, g]),
                pltpu.make_async_copy(picked_out.at[part, rows], picked_ref.at[part], sems.at[1, g]),
            ]
        )
        stores.append(pltpu.make_async_copy(out_ref.at[part], out_hbm.at[part, rows], sems.at[2, g]))
    for pair in loads:
        for copy in pair:
            copy.start()
    after_load = pltpu.make_async_copy(after_out, after_ref, after_sem)
    after_load.start()
    total = total_ref[...]
    for g in range(groups):
        for copy in loads[g]:
            copy.wait()
        part = slice(g * share, (g + 1) * share)
        out = (qs_ref[part] * carried_ref[part].astype(f32)).astype(bf16)
        out_ref[part] = out
        stores[g].start()
        terms = out.astype(f32) * picked_ref[part].astype(f32)
        total = total + jnp.sum(terms.reshape(share * per // 8, 8, tokens), axis=0)
    next_ref[...] = total
    after_load.wait()
    if last:
        logit = jnp.sum(total, axis=0, keepdims=True)
        score = soft_cap * jnp.tanh(logit / soft_cap)
        mass = jnp.sum(after_ref[...] * jnp.exp(score), axis=1, keepdims=True)
        level = jnp.log(mass)
        lists = tokens // size
        lane = lax.broadcasted_iota(jnp.int32, (1, lists), 1)
        losses = jnp.zeros((1, lists), f32)
        for b in range(lists):
            part = slice(b * size, (b + 1) * size)
            own = jnp.sum(level[part]) - jnp.sum(score[:, part])
            losses = jnp.where(lane == b, own / size, losses)
        loss_ref[...] = losses
    for copy in stores:
        copy.wait()


def result(chunk, chunks, carried, query_short, picked, after, lists, total, out):
    owners, per, tokens = carried.shape
    local = per * chunks
    groups = math.gcd(owners, 8)
    start = out is None
    if start:
        total, out = jnp.zeros((8, tokens), f32), jnp.zeros((8, tokens), bf16)
    return pl.pallas_call(
        functools.partial(result_kernel, tokens // lists, chunk == chunks - 1, chunk * per),
        in_specs=[whole, outside, outside, outside, whole, outside],
        out_specs=[outside, whole, whole],
        out_shape=[
            jax.ShapeDtypeStruct((owners, local, tokens), bf16),
            jax.ShapeDtypeStruct((8, tokens), f32),
            jax.ShapeDtypeStruct((1, lists), f32),
        ],
        scratch_shapes=[
            pltpu.VMEM((owners, per, tokens), f32),
            pltpu.VMEM((owners, per, tokens), bf16),
            pltpu.VMEM((owners, per, tokens), bf16),
            pltpu.VMEM((tokens, tokens), f32),
            pltpu.SemaphoreType.DMA((3, groups)),
            pltpu.SemaphoreType.DMA,
        ],
        input_output_aliases={} if start else {5: 0},
        compiler_params=params(8),
        cost_estimate=cost(4 * owners * per * tokens, 10 * owners * per * tokens),
        name="result",
    )(
        carried,
        in_hbm(query_short.reshape(owners, local, tokens)),
        in_hbm(picked.reshape(owners, local, tokens)),
        in_hbm(after),
        total,
        out,
    )


def per_device(
    query_input,
    key_input,
    value_input,
    short_taps,
    long_filter,
    skip_gain,
    unembed,
    targets,
    rankings,
):
    channels, tokens = query_input.shape
    owners = lax.axis_size(token_axes)
    local = channels // owners
    lists = rankings.shape[0]
    chunks = most_chunks if local % (most_chunks * tile) == 0 else 1
    last, held_key, held_value = rims(key_input, value_input)
    before = passed_along(last, token_axes, 1)
    inner = inner_features(held_key, held_value, short_taps)
    gated = gated_features(*inner, before).reshape(owners, chunks, local // chunks, tokens)
    arrived = [
        lax.all_to_all(gated[:, chunk], token_axes, 0, 0, tiled=True) for chunk in range(chunks)
    ]
    transform = table(tokens)
    *specs, last_query = filter_spectrum(long_filter, skip_gain, transform, query_input, chunks)
    before_query = passed_along(last_query, token_axes, 1)
    arrived, before_query = lax.optimization_barrier((arrived, before_query))
    query_short, picked, after = query_side(query_input, before_query, short_taps, unembed, targets, rankings)
    returned = []
    for chunk in range(chunks):
        carried = long_convolution(arrived[chunk], specs[chunk], transform)
        returned.append(lax.all_to_all(carried, token_axes, 0, 0, tiled=True))
    total = out = None
    for chunk in range(chunks):
        out, total, losses = result(
            chunk, chunks, returned[chunk], query_short, picked, after, lists, total, out
        )
    return out.reshape(channels, tokens), losses.reshape(lists)


def solution(mesh):
    placed = (
        P(None, ("grp", "seq", "tile")),
        P(None, ("grp", "seq", "tile")),
        P(None, ("grp", "seq", "tile")),
        P(),
        P(("seq", "tile"), None),
        P(("seq", "tile")),
        P(),
        P(("grp", "seq", "tile")),
        P(("grp", "seq", "tile"), None),
    )
    return jax.shard_map(
        per_device,
        mesh=mesh,
        in_specs=placed,
        out_specs=(P(None, ("grp", "seq", "tile")), P(("grp", "seq", "tile"))),
        check_vma=False,
    )
```

```python
import functools
import math

import jax
import jax.numpy as jnp
import ml_dtypes
import numpy as np
from jax import lax
from jax.experimental import pallas as pl
from jax.experimental.pallas import tpu as pltpu
from jax.sharding import PartitionSpec as P

soft_cap = 5.0
token_axes = ("seq", "tile")
bf16 = jnp.bfloat16
f32 = jnp.float32
rim = 8
most_chunks = 1
mebibyte = 1 << 20


whole = pl.BlockSpec(memory_space=pltpu.VMEM)
outside = pl.BlockSpec(memory_space=pltpu.HBM)


def in_hbm(x):
    return pltpu.with_memory_space_constraint(x, pltpu.HBM)


def params(limit=48):
    return pltpu.CompilerParams(vmem_limit_bytes=limit * mebibyte)


def cost(flops, size):
    return pl.CostEstimate(flops=flops, bytes_accessed=size, transcendentals=0)


def dot(a, b, over):
    return lax.dot_general(a, b, ((over[0], over[1]), ((), ())), preferred_element_type=f32)


def passed_along(block, axis, distance):
    devices = range(lax.axis_size(axis))
    route = [(i - distance, i) for i in devices if i - distance in devices]
    return lax.ppermute(block, axis, route)


def c_mul(z, angle):
    re, im = z
    turns = angle / (math.pi / 4)
    nearest = round(turns)
    if abs(turns - nearest) < 1e-9:
        eighth = nearest % 8
        if eighth == 0:
            return (re, im)
        if eighth == 2:
            return (-im, re)
        if eighth == 4:
            return (-re, -im)
        if eighth == 6:
            return (im, -re)
        half = math.sqrt(0.5)
        if eighth == 1:
            return ((re - im) * half, (re + im) * half)
        if eighth == 3:
            return ((re + im) * -half, (re - im) * half)
        if eighth == 5:
            return ((im - re) * half, (re + im) * -half)
        return ((re + im) * half, (im - re) * half)
    c, s = math.cos(angle), math.sin(angle)
    return (re * c - im * s, re * s + im * c)


def c_add(a, b):
    return (a[0] + b[0], a[1] + b[1])


def c_sub(a, b):
    return (a[0] - b[0], a[1] - b[1])


def c_dft(z, sign):
    n = len(z)
    if n == 1:
        return list(z)
    even = c_dft(z[0::2], sign)
    odd = c_dft(z[1::2], sign)
    turned = [c_mul(o, sign * 2 * math.pi * p / n) for p, o in enumerate(odd)]
    return [c_add(e, o) for e, o in zip(even, turned)] + [c_sub(e, o) for e, o in zip(even, turned)]


def odd_dft(x):
    n = len(x)
    if n == 1:
        return [(x[0], None)]
    half = n // 2
    z = [c_mul((x[j], -x[j + half]), -math.pi * j / n) for j in range(half)]
    wide = c_dft(z, -1)
    out = []
    for m in range(half):
        if m % 2 == 0:
            out.append(wide[m // 2])
        else:
            re, im = wide[(n - 1 - m) // 2]
            out.append((re, -im))
    return out


def real_dft(x):
    n = len(x)
    if n == 1:
        return [(x[0], None)]
    half = n // 2
    even = real_dft([x[j] + x[j + half] for j in range(half)])
    odd = odd_dft([x[j] - x[j + half] for j in range(half)])
    out = [None] * (half + 1)
    out[0::2] = even if half > 1 else [even[0]]
    out[1::2] = odd
    return out


def padded_real_dft(x):
    n = len(x)
    out = [None] * (n + 1)
    out[0::2] = real_dft(x)
    out[1::2] = odd_dft(x)
    return out


def odd_dft_adjoint(y):
    half = len(y)
    if y[0][1] is None:
        return [y[0][0]]
    n = 2 * half
    wide = []
    for p in range(half):
        if 2 * p < half:
            wide.append(y[2 * p])
        else:
            re, im = y[n - 1 - 2 * p]
            wide.append((re, -im))
    z = c_dft(wide, 1)
    turned = [c_mul(value, math.pi * j / n) for j, value in enumerate(z)]
    return [u[0] for u in turned] + [-u[1] for u in turned]


def real_dft_adjoint(x):
    if len(x) == 1:
        return [x[0][0]]
    even = real_dft_adjoint(x[0::2])
    odd = odd_dft_adjoint(x[1::2])
    return [e + o for e, o in zip(even, odd)] + [e - o for e, o in zip(even, odd)]


def padded_real_dft_adjoint(x):
    even = real_dft_adjoint(x[0::2])
    odd = odd_dft_adjoint(x[1::2])
    return [e + o for e, o in zip(even, odd)]


tile = 128


def rim_picker(lanes):
    row = lax.broadcasted_iota(jnp.int32, (rim, lanes), 0)
    lane = lax.broadcasted_iota(jnp.int32, (rim, lanes), 1)
    return (lane == row + (lanes - rim)).astype(bf16)


def rim_kernel(k_ref, v_ref, out_ref, held_k, held_v, sems):
    pieces = sems.shape[1]
    channels, lanes = k_ref.shape
    rows = channels // pieces
    pairs = ((k_ref, held_k), (v_ref, held_v))
    parts = [slice(p * rows, (p + 1) * rows) for p in range(pieces)]
    copies = [
        [pltpu.make_async_copy(ref.at[part], held.at[part], sems.at[a, p]) for a, (ref, held) in enumerate(pairs)]
        for p, part in enumerate(parts)
    ]
    for group in copies:
        for copy in group:
            copy.start()
    picker = rim_picker(lanes)
    for part, group in zip(parts, copies):
        for copy in group:
            copy.wait()
        last = [dot(picker, held[part], ((1,), (1,))) for _, held in pairs]
        out_ref[:, part] = jnp.concatenate(last, axis=0).astype(bf16)


def rims(key_input, value_input):
    channels, tokens = key_input.shape
    pieces = 2
    return pl.pallas_call(
        rim_kernel,
        in_specs=[outside] * 2,
        out_specs=[whole] * 3,
        out_shape=[jax.ShapeDtypeStruct((2 * rim, channels), bf16)]
        + [pltpu.VMEM((channels, tokens), bf16)] * 2,
        scratch_shapes=[pltpu.SemaphoreType.DMA((2, pieces))],
        compiler_params=params(6),
        cost_estimate=cost(4 * channels * tokens * rim, 4 * channels * tokens),
        name="rims",
    )(in_hbm(key_input), in_hbm(value_input))


def short_conv(x, before, taps_ref, which, lanes, space):
    tokens = x.shape[1]
    space[:rim] = before
    space[rim:] = x.astype(f32).T
    width = taps_ref.shape[1]
    taps = [
        jnp.broadcast_to(taps_ref[which, offset : offset + 1, lanes], (8, tile)) for offset in range(width)
    ]
    out = []
    for begin in range(0, tokens, 8):
        total = taps[0] * space[rim + begin : rim + begin + 8]
        for offset in range(1, width):
            first = rim + begin - offset
            total = total + taps[offset] * space[first : first + 8]
        out.append(total)
    return out


def aligned(start, size):
    return pl.ds(pl.multiple_of(start, size), size)


def filtered(space, taps, begin):
    total = taps[0] * space[rim + begin : rim + begin + 8]
    for offset in range(1, len(taps)):
        first = rim + begin - offset
        total = total + taps[offset] * space[first : first + 8]
    return total


def tap_rows(taps_ref, which, lanes):
    return [
        jnp.broadcast_to(taps_ref[which, offset : offset + 1, lanes], (8, tile))
        for offset in range(taps_ref.shape[1])
    ]


def inner_kernel(k_ref, v_ref, taps_out, part_ref, first_ref, taps_ref, key_space, value_space, sem):
    tiles, tokens, _ = part_ref.shape
    load = pltpu.make_async_copy(taps_out, taps_ref, sem)
    load.start()
    load.wait()
    unroll = math.gcd(tiles, 4)
    for group in range(tiles // unroll):

        @pl.loop(0, unroll, unroll=unroll)
        def _(step):
            at = group * unroll + step
            lanes = aligned(at * tile, tile)
            for a, (ref, space) in enumerate(((k_ref, key_space), (v_ref, value_space))):
                turned = ref[lanes].astype(f32).T
                space[rim:] = turned
                first_ref[a, at] = turned[:rim]
            key_taps, value_taps = tap_rows(taps_ref, 1, lanes), tap_rows(taps_ref, 2, lanes)
            for begin in range(rim, tokens, 8):
                k = filtered(key_space, key_taps, begin)
                part_ref[at, begin : begin + 8] = k * filtered(value_space, value_taps, begin)


def inner_features(key_input, value_input, short_taps):
    channels, tokens = key_input.shape
    tiles = channels // tile
    return pl.pallas_call(
        inner_kernel,
        in_specs=[whole, whole, outside],
        out_specs=[whole] * 3,
        out_shape=[
            pltpu.VMEM((tiles, tokens, tile), f32),
            pltpu.VMEM((2, tiles, rim, tile), f32),
            pltpu.VMEM(short_taps.shape, f32),
        ],
        scratch_shapes=[
            pltpu.VMEM((rim + tokens, tile), f32),
            pltpu.VMEM((rim + tokens, tile), f32),
            pltpu.SemaphoreType.DMA,
        ],
        compiler_params=params(8),
        cost_estimate=cost(28 * channels * tokens, 8 * channels * tokens),
        name="inner",
    )(key_input, value_input, in_hbm(short_taps))


def gated_kernel(part_ref, first_ref, taps_ref, before_ref, out_ref, made, key_space, value_space, sems):
    tiles, tokens, _ = part_ref.shape
    (groups,) = sems.shape
    size = tiles // groups
    for g in range(groups):

        @pl.loop(0, size, unroll=size)
        def _(step):
            at = g * size + step
            lanes = aligned(at * tile, tile)
            before = before_ref[:, lanes].astype(f32)
            for a, space in enumerate((key_space, value_space)):
                space[:rim] = before[a * rim : (a + 1) * rim]
                space[rim:] = first_ref[a, at]
            k = filtered(key_space, tap_rows(taps_ref, 1, lanes), 0)
            v = filtered(value_space, tap_rows(taps_ref, 2, lanes), 0)
            made[at] = jnp.concatenate([k * v, part_ref[at, rim:]], 0).T.astype(bf16)

        here = slice(g * size, (g + 1) * size)
        pltpu.make_async_copy(made.at[here], out_ref.at[here], sems.at[g]).start()
    for g in range(groups):
        here = slice(g * size, (g + 1) * size)
        pltpu.make_async_copy(made.at[here], out_ref.at[here], sems.at[g]).wait()


def gated_features(part, first, taps, before):
    tiles, tokens, _ = part.shape
    groups = math.gcd(tiles, 8)
    return pl.pallas_call(
        gated_kernel,
        in_specs=[whole] * 4,
        out_specs=outside,
        out_shape=jax.ShapeDtypeStruct((tiles, tile, tokens), bf16),
        scratch_shapes=[
            pltpu.VMEM((tiles, tile, tokens), bf16),
            pltpu.VMEM((2 * rim, tile), f32),
            pltpu.VMEM((2 * rim, tile), f32),
            pltpu.SemaphoreType.DMA((groups,)),
        ],
        compiler_params=params(6),
        cost_estimate=cost(4 * tiles * tile * tokens, 6 * tiles * tile * tokens),
        name="gated",
    )(part, first, taps, before)


step_rows = 16
long_parts = 2


def halves(x):
    high = x.astype(bf16)
    return high, (x - high.astype(f32)).astype(bf16)


def put_spectrum(spectrum, turn_ref, high_ref, low_ref, rows, lanes):
    for at, (re, im) in enumerate(spectrum):
        if at == 0:
            im = jnp.zeros_like(re)
        else:
            c, s = turn_ref[0, at : at + 1], turn_ref[1, at : at + 1]
            if im is None:
                re, im = re * c, -(re * s)
            else:
                re, im = re * c + im * s, im * c - re * s
        for value, part in ((re, slice(0, lanes)), (im, slice(lanes, 2 * lanes))):
            high, low = halves(value)
            high_ref[at, rows, part] = high
            if low_ref is not None:
                low_ref[at, rows, part] = low


def three_pass(ah, al, wh, wl, over):
    return dot(ah, wh, over) + (dot(al, wh, over) + dot(ah, wl, over))


def over_frequencies(count, body):
    if count <= 33:
        for k in range(count):
            body(k)
    else:
        pl.loop(0, count)(body)


def filter_kernel(taps_ref, skip_ref, table_ref, q_ref, *rest):
    *spec_refs, last_ref, ah, al, turn_ref, held, sem = rest
    load = pltpu.make_async_copy(q_ref, held, sem)
    load.start()
    put_turns(turn_ref)
    channels = taps_ref.shape[0]
    lanes = turn_ref.shape[2]
    blocks = taps_ref.shape[1] // lanes
    skip = jnp.broadcast_to(skip_ref[...], (8, channels)).T
    lane = lax.broadcasted_iota(jnp.int32, (step_rows, lanes), 1)
    for step in range(channels // step_rows):
        rows = slice(step * step_rows, (step + 1) * step_rows)
        x = [taps_ref[rows, j * lanes : (j + 1) * lanes] for j in range(blocks)]
        x[0] = x[0] + jnp.where(lane == 0, skip[rows, 0:1], 0.0)
        put_spectrum(padded_real_dft(x), turn_ref, ah, al, rows, lanes)
    per = channels // len(spec_refs)

    def one(k):
        ends = (k == 0) | (k == blocks)
        scale = jnp.where(ends, 1.0, 2.0) / (2 * blocks * lanes)
        spec = three_pass(ah[k], al[k], table_ref[0], table_ref[1], ((1,), (0,))) * scale
        for at, ref in enumerate(spec_refs):
            ref[k] = spec[at * per : (at + 1) * per].astype(bf16)

    over_frequencies(blocks + 1, one)
    load.wait()
    last_ref[...] = dot(rim_picker(held.shape[1]), held[...], ((1,), (1,))).astype(bf16)


def put_turns(turn_ref):
    _, count, lanes = turn_ref.shape
    period = 2 * (count - 1) * lanes
    k = lax.broadcasted_iota(jnp.int32, (count, lanes), 0)
    s = lax.broadcasted_iota(jnp.int32, (count, lanes), 1)
    turn = (k * s).astype(f32) * (2 * math.pi / period)
    turn_ref[0] = jnp.cos(turn)
    turn_ref[1] = jnp.sin(turn)


def table(lanes):
    s = np.arange(lanes)
    base = 2 * np.pi * (s[:, None] * s[None, :] % lanes) / lanes
    c, n = np.cos(base), np.sin(base)
    full = np.block([[c, -n], [n, c]]).astype(np.float32)
    high = full.astype(ml_dtypes.bfloat16)
    low = (full - high.astype(np.float32)).astype(ml_dtypes.bfloat16)
    return jnp.asarray(np.stack([high, low]))


def filter_spectrum(long_filter, skip_gain, table, query_input, chunks):
    channels, length = long_filter.shape
    lanes = table.shape[2] // 2
    count = length // lanes + 1
    return pl.pallas_call(
        filter_kernel,
        in_specs=[whole, whole, whole, outside],
        out_specs=[whole] * (chunks + 1),
        out_shape=[pltpu.HBM((count, channels // chunks, 2 * lanes), bf16)] * chunks
        + [pltpu.HBM((rim, query_input.shape[0]), bf16)],
        scratch_shapes=[pltpu.VMEM((count, channels, 2 * lanes), bf16)] * 2
        + [
            pltpu.VMEM((2, count, lanes), f32),
            pltpu.VMEM(query_input.shape, bf16),
            pltpu.SemaphoreType.DMA,
        ],
        compiler_params=params(24),
        cost_estimate=cost(6 * count * channels * 4 * lanes * lanes, 12 * count * channels * lanes),
        name="filter_spectrum",
    )(long_filter, skip_gain.reshape(1, channels), table, in_hbm(query_input))


def long_kernel(x_ref, spec_out, table_out, out_hbm, ah, back, spec_ref, table_ref, turn_ref, out_ref, sems):
    blocks, channels, lanes = x_ref.shape
    count = blocks + 1
    table_load = pltpu.make_async_copy(table_out.at[0], table_ref, sems.at[0])
    split = channels % (long_parts * step_rows) == 0 and count <= 33
    share = channels // long_parts if split else channels
    parts = [slice(first, first + share) for first in range(0, channels, share)]
    loads = [
        pltpu.make_async_copy(spec_out.at[:, part], spec_ref.at[:, part], sems.at[1 + at])
        for at, part in enumerate(parts)
    ]
    table_load.start()
    for copy in loads[:2]:
        copy.start()
    put_turns(turn_ref)

    def forward(rows):
        x = [x_ref[j, rows].astype(f32) for j in range(blocks)]
        put_spectrum(padded_real_dft(x), turn_ref, ah, None, rows, lanes)

    def multiply(first, size, rows):
        def take(ref):
            part = ref[pl.ds(first, size), rows]
            return part.reshape(size * part.shape[1], 2 * lanes)

        x = dot(take(ah), table_ref[...], ((1,), (0,)))
        spec = take(spec_ref).astype(f32)
        xr, xi = x[:, :lanes], x[:, lanes:]
        fr, fi = spec[:, :lanes], spec[:, lanes:]
        product = jnp.concatenate([xr * fr - xi * fi, xr * fi + xi * fr], axis=1)
        y = dot(product.astype(bf16), table_ref[...], ((1,), (1,)))
        back[pl.ds(first, size), rows] = y.reshape(size, -1, 2 * lanes)

    def backward(rows):
        spectrum = [(back[0, rows, :lanes], None)]
        for k in range(1, count):
            re, im = back[k, rows, :lanes], back[k, rows, lanes:]
            c, s = turn_ref[0, k : k + 1], turn_ref[1, k : k + 1]
            spectrum.append((re * c - im * s, None if k == blocks else re * s + im * c))
        for j, y in enumerate(padded_real_dft_adjoint(spectrum)):
            out_ref[j, rows] = y.astype(bf16)

    def store(part, at):
        return pltpu.make_async_copy(out_ref.at[:, part], out_hbm.at[:, part], sems.at[1 + long_parts + at])

    if split:
        size = max(1, 256 // share)
        steps = [[slice(r, r + step_rows) for r in range(p.start, p.stop, step_rows)] for p in parts]
        groups = [(k, min(size, count - k)) for k in range(0, count, size)]

        def together(part, others):
            done = 0
            for at, (k, many) in enumerate(groups):
                multiply(k, many, part)
                upto = len(others) * (at + 1) // len(groups)
                for body, rows in others[done:upto]:
                    body(rows)
                done = upto

        ahead = 2
        for step in steps[:ahead]:
            for rows in step:
                forward(rows)
        table_load.wait()
        for at, part in enumerate(parts):
            loads[at].wait()
            if at + 2 < len(parts):
                loads[at + 2].start()
            others = [(forward, rows) for rows in (steps[at + ahead] if at + ahead < len(parts) else [])]
            others += [(backward, rows) for rows in (steps[at - 1] if at else [])]
            together(part, others)
            if at:
                store(parts[at - 1], at - 1).start()
        for rows in steps[-1]:
            backward(rows)
        store(parts[-1], len(parts) - 1).start()
        for at, part in enumerate(parts):
            store(part, at).wait()
    else:
        everything = slice(0, channels)

        @pl.loop(0, channels // step_rows)
        def _(step):
            forward(aligned(step * step_rows, step_rows))

        table_load.wait()
        loads[0].wait()
        over_frequencies(count, lambda k: multiply(k, 1, everything))

        @pl.loop(0, channels // step_rows)
        def _(step):
            backward(aligned(step * step_rows, step_rows))

        store(everything, 0).start()
        store(everything, 0).wait()


def long_convolution(arrived, spec, table):
    blocks, channels, lanes = arrived.shape
    count = blocks + 1
    return pl.pallas_call(
        long_kernel,
        in_specs=[whole, outside, outside],
        out_specs=outside,
        out_shape=jax.ShapeDtypeStruct(arrived.shape, bf16),
        scratch_shapes=[
            pltpu.VMEM((count, channels, 2 * lanes), bf16),
            pltpu.VMEM((count, channels, 2 * lanes), f32),
            pltpu.VMEM((count, channels, 2 * lanes), bf16),
            pltpu.VMEM(table.shape[1:], bf16),
            pltpu.VMEM((2, count, lanes), f32),
            pltpu.VMEM(arrived.shape, bf16),
            pltpu.SemaphoreType.DMA((1 + 2 * long_parts,)),
        ],
        compiler_params=params(24),
        cost_estimate=cost(12 * count * channels * 4 * lanes * lanes, 12 * count * channels * lanes),
        name="long_convolution",
    )(arrived, in_hbm(spec), in_hbm(table))


def query_kernel(q_ref, before_ref, taps_ref, unembed_ref, targets_ref, ranks_ref, qs_ref, picked_ref, after_ref, space):
    rows, tokens = q_ref.shape

    @pl.loop(0, rows // tile, unroll=min(4, rows // tile))
    def _(at):
        part = aligned(at * tile, tile)
        before = before_ref[:, part].astype(f32)
        query_short = short_conv(q_ref[part], before[:rim], taps_ref, 0, part, space.at[at % 2])
        qs_ref[part] = jnp.concatenate(query_short, 0).T

    vocabulary = unembed_ref.shape[1]
    word = lax.broadcasted_iota(jnp.int32, (vocabulary, tokens), 0)
    chosen = (word == targets_ref[...]).astype(bf16)
    picked_ref[...] = dot(unembed_ref[...], chosen, ((1,), (0,))).astype(bf16)

    @pl.when(pl.program_id(0) == 0)
    def _():
        lists, size = ranks_ref.shape
        token = lax.broadcasted_iota(jnp.int32, (size, size), 0)
        rank = lax.broadcasted_iota(jnp.int32, (size, size), 1).astype(f32)
        at = [
            jnp.sum(jnp.where(token == ranks_ref[b : b + 1, :], rank, 0.0), axis=1, keepdims=True)
            for b in range(lists)
        ]
        column = jnp.concatenate(at, axis=0)
        row_of = lax.broadcasted_iota(jnp.int32, (tokens, tokens), 0)
        col_of = lax.broadcasted_iota(jnp.int32, (tokens, tokens), 1)
        row = jnp.sum(jnp.where(row_of == col_of, column, 0.0), axis=0, keepdims=True)
        same = row_of // size == col_of // size
        after_ref[...] = jnp.where(same & (row >= column), 1.0, 0.0)


def query_side(query_input, before, short_taps, unembed, targets, rankings):
    channels, tokens = query_input.shape
    width = short_taps.shape[1]
    vocabulary = unembed.shape[1]
    rows = channels // 4
    block = pl.BlockSpec((rows, tokens), lambda i: (i, 0))
    return pl.pallas_call(
        query_kernel,
        grid=(channels // rows,),
        in_specs=[
            block,
            pl.BlockSpec((rim, rows), lambda i: (0, i)),
            pl.BlockSpec((1, width, rows), lambda i: (0, 0, i)),
            pl.BlockSpec((rows, vocabulary), lambda i: (i, 0)),
            pl.BlockSpec((1, tokens), lambda i: (0, 0)),
            pl.BlockSpec(rankings.shape, lambda i: (0, 0)),
        ],
        out_specs=[block, block, pl.BlockSpec((tokens, tokens), lambda i: (0, 0))],
        out_shape=[
            pltpu.HBM((channels, tokens), f32),
            pltpu.HBM((channels, tokens), bf16),
            pltpu.HBM((tokens, tokens), f32),
        ],
        scratch_shapes=[pltpu.VMEM((2, rim + tokens, tile), f32)],
        compiler_params=params(12),
        cost_estimate=cost(2 * channels * tokens * (vocabulary + 7), channels * (8 * tokens + 2 * vocabulary)),
        name="query_side",
    )(in_hbm(query_input), before, short_taps, in_hbm(unembed), targets.reshape(1, tokens), rankings)


def result_kernel(
    size, last, first, carried_ref, qs_out, picked_out, after_out, total_ref, _, out_hbm, next_ref, loss_ref,
    qs_ref, picked_ref, out_ref, after_ref, sems, after_sem,
):
    owners, per, tokens = carried_ref.shape
    groups = sems.shape[1]
    share = owners // groups
    loads, stores = [], []
    for g in range(groups):
        part = slice(g * share, (g + 1) * share)
        rows = slice(first, first + per)
        loads.append(
            [
                pltpu.make_async_copy(qs_out.at[part, rows], qs_ref.at[part], sems.at[0, g]),
                pltpu.make_async_copy(picked_out.at[part, rows], picked_ref.at[part], sems.at[1, g]),
            ]
        )
        stores.append(pltpu.make_async_copy(out_ref.at[part], out_hbm.at[part, rows], sems.at[2, g]))
    for pair in loads:
        for copy in pair:
            copy.start()
    after_load = pltpu.make_async_copy(after_out, after_ref, after_sem)
    after_load.start()
    total = total_ref[...]
    for g in range(groups):
        for copy in loads[g]:
            copy.wait()
        part = slice(g * share, (g + 1) * share)
        out = (qs_ref[part] * carried_ref[part].astype(f32)).astype(bf16)
        out_ref[part] = out
        stores[g].start()
        terms = out.astype(f32) * picked_ref[part].astype(f32)
        total = total + jnp.sum(terms.reshape(share * per // 8, 8, tokens), axis=0)
    next_ref[...] = total
    after_load.wait()
    if last:
        logit = jnp.sum(total, axis=0, keepdims=True)
        score = soft_cap * jnp.tanh(logit / soft_cap)
        mass = jnp.sum(after_ref[...] * jnp.exp(score), axis=1, keepdims=True)
        level = jnp.log(mass)
        lists = tokens // size
        lane = lax.broadcasted_iota(jnp.int32, (1, lists), 1)
        losses = jnp.zeros((1, lists), f32)
        for b in range(lists):
            part = slice(b * size, (b + 1) * size)
            own = jnp.sum(level[part]) - jnp.sum(score[:, part])
            losses = jnp.where(lane == b, own / size, losses)
        loss_ref[...] = losses
    for copy in stores:
        copy.wait()


def result(chunk, chunks, carried, query_short, picked, after, lists, total, out):
    owners, per, tokens = carried.shape
    local = per * chunks
    groups = math.gcd(owners, 8)
    start = out is None
    if start:
        total, out = jnp.zeros((8, tokens), f32), jnp.zeros((8, tokens), bf16)
    return pl.pallas_call(
        functools.partial(result_kernel, tokens // lists, chunk == chunks - 1, chunk * per),
        in_specs=[whole, outside, outside, outside, whole, outside],
        out_specs=[outside, whole, whole],
        out_shape=[
            jax.ShapeDtypeStruct((owners, local, tokens), bf16),
            jax.ShapeDtypeStruct((8, tokens), f32),
            jax.ShapeDtypeStruct((1, lists), f32),
        ],
        scratch_shapes=[
            pltpu.VMEM((owners, per, tokens), f32),
            pltpu.VMEM((owners, per, tokens), bf16),
            pltpu.VMEM((owners, per, tokens), bf16),
            pltpu.VMEM((tokens, tokens), f32),
            pltpu.SemaphoreType.DMA((3, groups)),
            pltpu.SemaphoreType.DMA,
        ],
        input_output_aliases={} if start else {5: 0},
        compiler_params=params(8),
        cost_estimate=cost(4 * owners * per * tokens, 10 * owners * per * tokens),
        name="result",
    )(
        carried,
        in_hbm(query_short.reshape(owners, local, tokens)),
        in_hbm(picked.reshape(owners, local, tokens)),
        in_hbm(after),
        total,
        out,
    )


def per_device(
    query_input,
    key_input,
    value_input,
    short_taps,
    long_filter,
    skip_gain,
    unembed,
    targets,
    rankings,
):
    channels, tokens = query_input.shape
    owners = lax.axis_size(token_axes)
    local = channels // owners
    lists = rankings.shape[0]
    chunks = most_chunks if local % (most_chunks * tile) == 0 else 1
    last, held_key, held_value = rims(key_input, value_input)
    before = passed_along(last, token_axes, 1)
    inner = inner_features(held_key, held_value, short_taps)
    gated = gated_features(*inner, before).reshape(owners, chunks, local // chunks, tokens)
    arrived = [
        lax.all_to_all(gated[:, chunk], token_axes, 0, 0, tiled=True) for chunk in range(chunks)
    ]
    transform = table(tokens)
    *specs, last_query = filter_spectrum(long_filter, skip_gain, transform, query_input, chunks)
    before_query = passed_along(last_query, token_axes, 1)
    arrived, before_query = lax.optimization_barrier((arrived, before_query))
    query_short, picked, after = query_side(query_input, before_query, short_taps, unembed, targets, rankings)
    returned = []
    for chunk in range(chunks):
        carried = long_convolution(arrived[chunk], specs[chunk], transform)
        returned.append(lax.all_to_all(carried, token_axes, 0, 0, tiled=True))
    total = out = None
    for chunk in range(chunks):
        out, total, losses = result(
            chunk, chunks, returned[chunk], query_short, picked, after, lists, total, out
        )
    return out.reshape(channels, tokens), losses.reshape(lists)


def solution(mesh):
    placed = (
        P(None, ("grp", "seq", "tile")),
        P(None, ("grp", "seq", "tile")),
        P(None, ("grp", "seq", "tile")),
        P(),
        P(("seq", "tile"), None),
        P(("seq", "tile")),
        P(),
        P(("grp", "seq", "tile")),
        P(("grp", "seq", "tile"), None),
    )
    return jax.shard_map(
        per_device,
        mesh=mesh,
        in_specs=placed,
        out_specs=(P(None, ("grp", "seq", "tile")), P(("grp", "seq", "tile"))),
        check_vma=False,
    )
```

```python
import functools
import math

import jax
import jax.numpy as jnp
import ml_dtypes
import numpy as np
from jax import lax
from jax.experimental import pallas as pl
from jax.experimental.pallas import tpu as pltpu
from jax.sharding import PartitionSpec as P

soft_cap = 5.0
token_axes = ("seq", "tile")
bf16 = jnp.bfloat16
f32 = jnp.float32
rim = 8
most_chunks = 1
mebibyte = 1 << 20


whole = pl.BlockSpec(memory_space=pltpu.VMEM)
outside = pl.BlockSpec(memory_space=pltpu.HBM)


def in_hbm(x):
    return pltpu.with_memory_space_constraint(x, pltpu.HBM)


def params(limit=48):
    return pltpu.CompilerParams(vmem_limit_bytes=limit * mebibyte)


def cost(flops, size):
    return pl.CostEstimate(flops=flops, bytes_accessed=size, transcendentals=0)


def dot(a, b, over):
    return lax.dot_general(a, b, ((over[0], over[1]), ((), ())), preferred_element_type=f32)


def passed_along(block, axis, distance):
    devices = range(lax.axis_size(axis))
    route = [(i - distance, i) for i in devices if i - distance in devices]
    return lax.ppermute(block, axis, route)


def c_mul(z, angle):
    re, im = z
    turns = angle / (math.pi / 4)
    nearest = round(turns)
    if abs(turns - nearest) < 1e-9:
        eighth = nearest % 8
        if eighth == 0:
            return (re, im)
        if eighth == 2:
            return (-im, re)
        if eighth == 4:
            return (-re, -im)
        if eighth == 6:
            return (im, -re)
        half = math.sqrt(0.5)
        if eighth == 1:
            return ((re - im) * half, (re + im) * half)
        if eighth == 3:
            return ((re + im) * -half, (re - im) * half)
        if eighth == 5:
            return ((im - re) * half, (re + im) * -half)
        return ((re + im) * half, (im - re) * half)
    c, s = math.cos(angle), math.sin(angle)
    return (re * c - im * s, re * s + im * c)


def c_add(a, b):
    return (a[0] + b[0], a[1] + b[1])


def c_sub(a, b):
    return (a[0] - b[0], a[1] - b[1])


def c_dft(z, sign):
    n = len(z)
    if n == 1:
        return list(z)
    even = c_dft(z[0::2], sign)
    odd = c_dft(z[1::2], sign)
    turned = [c_mul(o, sign * 2 * math.pi * p / n) for p, o in enumerate(odd)]
    return [c_add(e, o) for e, o in zip(even, turned)] + [c_sub(e, o) for e, o in zip(even, turned)]


def odd_dft(x):
    n = len(x)
    if n == 1:
        return [(x[0], None)]
    half = n // 2
    z = [c_mul((x[j], -x[j + half]), -math.pi * j / n) for j in range(half)]
    wide = c_dft(z, -1)
    out = []
    for m in range(half):
        if m % 2 == 0:
            out.append(wide[m // 2])
        else:
            re, im = wide[(n - 1 - m) // 2]
            out.append((re, -im))
    return out


def real_dft(x):
    n = len(x)
    if n == 1:
        return [(x[0], None)]
    half = n // 2
    even = real_dft([x[j] + x[j + half] for j in range(half)])
    odd = odd_dft([x[j] - x[j + half] for j in range(half)])
    out = [None] * (half + 1)
    out[0::2] = even if half > 1 else [even[0]]
    out[1::2] = odd
    return out


def padded_real_dft(x):
    n = len(x)
    out = [None] * (n + 1)
    out[0::2] = real_dft(x)
    out[1::2] = odd_dft(x)
    return out


def odd_dft_adjoint(y):
    half = len(y)
    if y[0][1] is None:
        return [y[0][0]]
    n = 2 * half
    wide = []
    for p in range(half):
        if 2 * p < half:
            wide.append(y[2 * p])
        else:
            re, im = y[n - 1 - 2 * p]
            wide.append((re, -im))
    z = c_dft(wide, 1)
    turned = [c_mul(value, math.pi * j / n) for j, value in enumerate(z)]
    return [u[0] for u in turned] + [-u[1] for u in turned]


def real_dft_adjoint(x):
    if len(x) == 1:
        return [x[0][0]]
    even = real_dft_adjoint(x[0::2])
    odd = odd_dft_adjoint(x[1::2])
    return [e + o for e, o in zip(even, odd)] + [e - o for e, o in zip(even, odd)]


def padded_real_dft_adjoint(x):
    even = real_dft_adjoint(x[0::2])
    odd = odd_dft_adjoint(x[1::2])
    return [e + o for e, o in zip(even, odd)]


tile = 128


def rim_picker(lanes):
    row = lax.broadcasted_iota(jnp.int32, (rim, lanes), 0)
    lane = lax.broadcasted_iota(jnp.int32, (rim, lanes), 1)
    return (lane == row + (lanes - rim)).astype(bf16)


def rim_kernel(k_ref, v_ref, taps_out, out_ref, held_k, held_v, taps_ref, sems, taps_sem):
    pieces = sems.shape[1]
    channels, lanes = k_ref.shape
    rows = channels // pieces
    pairs = ((k_ref, held_k), (v_ref, held_v))
    parts = [slice(p * rows, (p + 1) * rows) for p in range(pieces)]
    copies = [
        [pltpu.make_async_copy(ref.at[part], held.at[part], sems.at[a, p]) for a, (ref, held) in enumerate(pairs)]
        for p, part in enumerate(parts)
    ]
    for group in copies:
        for copy in group:
            copy.start()
    taps_load = pltpu.make_async_copy(taps_out, taps_ref, taps_sem)
    taps_load.start()
    picker = rim_picker(lanes)
    for part, group in zip(parts, copies):
        for copy in group:
            copy.wait()
        last = [dot(picker, held[part], ((1,), (1,))) for _, held in pairs]
        out_ref[:, part] = jnp.concatenate(last, axis=0).astype(bf16)
    taps_load.wait()


def rims(key_input, value_input, short_taps):
    channels, tokens = key_input.shape
    pieces = 2
    return pl.pallas_call(
        rim_kernel,
        in_specs=[outside] * 3,
        out_specs=[whole] * 4,
        out_shape=[jax.ShapeDtypeStruct((2 * rim, channels), bf16)]
        + [pltpu.VMEM((channels, tokens), bf16)] * 2
        + [pltpu.VMEM(short_taps.shape, f32)],
        scratch_shapes=[pltpu.SemaphoreType.DMA((2, pieces)), pltpu.SemaphoreType.DMA],
        compiler_params=params(6),
        cost_estimate=cost(4 * channels * tokens * rim, 4 * channels * tokens),
        name="rims",
    )(in_hbm(key_input), in_hbm(value_input), in_hbm(short_taps))


def short_conv(x, before, taps_ref, which, lanes, space):
    tokens = x.shape[1]
    space[:rim] = before
    space[rim:] = x.astype(f32).T
    width = taps_ref.shape[1]
    taps = [
        jnp.broadcast_to(taps_ref[which, offset : offset + 1, lanes], (8, tile)) for offset in range(width)
    ]
    out = []
    for begin in range(0, tokens, 8):
        total = taps[0] * space[rim + begin : rim + begin + 8]
        for offset in range(1, width):
            first = rim + begin - offset
            total = total + taps[offset] * space[first : first + 8]
        out.append(total)
    return out


def aligned(start, size):
    return pl.ds(pl.multiple_of(start, size), size)


def filtered(space, taps, begin):
    total = taps[0] * space[rim + begin : rim + begin + 8]
    for offset in range(1, len(taps)):
        first = rim + begin - offset
        total = total + taps[offset] * space[first : first + 8]
    return total


def tap_rows(taps_ref, which, lanes):
    return [
        jnp.broadcast_to(taps_ref[which, offset : offset + 1, lanes], (8, tile))
        for offset in range(taps_ref.shape[1])
    ]


def inner_kernel(k_ref, v_ref, taps_ref, part_ref, first_ref, key_space, value_space):
    tiles, tokens, _ = part_ref.shape
    unroll = math.gcd(tiles, 4)
    for group in range(tiles // unroll):

        @pl.loop(0, unroll, unroll=unroll)
        def _(step):
            at = group * unroll + step
            lanes = aligned(at * tile, tile)
            for a, (ref, space) in enumerate(((k_ref, key_space), (v_ref, value_space))):
                turned = ref[lanes].astype(f32).T
                space[rim:] = turned
                first_ref[a, at] = turned[:rim]
            key_taps, value_taps = tap_rows(taps_ref, 1, lanes), tap_rows(taps_ref, 2, lanes)
            for begin in range(rim, tokens, 8):
                k = filtered(key_space, key_taps, begin)
                part_ref[at, begin : begin + 8] = k * filtered(value_space, value_taps, begin)


def inner_features(key_input, value_input, short_taps):
    channels, tokens = key_input.shape
    tiles = channels // tile
    return pl.pallas_call(
        inner_kernel,
        in_specs=[whole] * 3,
        out_specs=[whole] * 2,
        out_shape=[
            pltpu.VMEM((tiles, tokens, tile), f32),
            pltpu.VMEM((2, tiles, rim, tile), f32),
        ],
        scratch_shapes=[
            pltpu.VMEM((rim + tokens, tile), f32),
            pltpu.VMEM((rim + tokens, tile), f32),
        ],
        compiler_params=params(8),
        cost_estimate=cost(28 * channels * tokens, 8 * channels * tokens),
        name="inner",
    )(key_input, value_input, short_taps)


def gated_kernel(part_ref, first_ref, taps_ref, before_ref, out_ref, made, key_space, value_space, sems):
    tiles, tokens, _ = part_ref.shape
    (groups,) = sems.shape
    size = tiles // groups
    for g in range(groups):

        @pl.loop(0, size, unroll=size)
        def _(step):
            at = g * size + step
            lanes = aligned(at * tile, tile)
            before = before_ref[:, lanes].astype(f32)
            for a, space in enumerate((key_space, value_space)):
                space[:rim] = before[a * rim : (a + 1) * rim]
                space[rim:] = first_ref[a, at]
            k = filtered(key_space, tap_rows(taps_ref, 1, lanes), 0)
            v = filtered(value_space, tap_rows(taps_ref, 2, lanes), 0)
            made[at] = jnp.concatenate([k * v, part_ref[at, rim:]], 0).T.astype(bf16)

        here = slice(g * size, (g + 1) * size)
        pltpu.make_async_copy(made.at[here], out_ref.at[here], sems.at[g]).start()
    for g in range(groups):
        here = slice(g * size, (g + 1) * size)
        pltpu.make_async_copy(made.at[here], out_ref.at[here], sems.at[g]).wait()


def gated_features(part, first, taps, before):
    tiles, tokens, _ = part.shape
    groups = math.gcd(tiles, 8)
    return pl.pallas_call(
        gated_kernel,
        in_specs=[whole] * 4,
        out_specs=outside,
        out_shape=jax.ShapeDtypeStruct((tiles, tile, tokens), bf16),
        scratch_shapes=[
            pltpu.VMEM((tiles, tile, tokens), bf16),
            pltpu.VMEM((2 * rim, tile), f32),
            pltpu.VMEM((2 * rim, tile), f32),
            pltpu.SemaphoreType.DMA((groups,)),
        ],
        compiler_params=params(6),
        cost_estimate=cost(4 * tiles * tile * tokens, 6 * tiles * tile * tokens),
        name="gated",
    )(part, first, taps, before)


step_rows = 16
long_parts = 2


def halves(x):
    high = x.astype(bf16)
    return high, (x - high.astype(f32)).astype(bf16)


def put_spectrum(spectrum, turn_ref, high_ref, low_ref, rows, lanes):
    for at, (re, im) in enumerate(spectrum):
        if at == 0:
            im = jnp.zeros_like(re)
        else:
            c, s = turn_ref[0, at : at + 1], turn_ref[1, at : at + 1]
            if im is None:
                re, im = re * c, -(re * s)
            else:
                re, im = re * c + im * s, im * c - re * s
        for value, part in ((re, slice(0, lanes)), (im, slice(lanes, 2 * lanes))):
            high, low = halves(value)
            high_ref[at, rows, part] = high
            if low_ref is not None:
                low_ref[at, rows, part] = low


def three_pass(ah, al, wh, wl, over):
    return dot(ah, wh, over) + (dot(al, wh, over) + dot(ah, wl, over))


def over_frequencies(count, body):
    if count <= 33:
        for k in range(count):
            body(k)
    else:
        pl.loop(0, count)(body)


def filter_kernel(taps_ref, skip_ref, table_ref, q_ref, *rest):
    *spec_refs, last_ref, ah, al, turn_ref, held, sem = rest
    load = pltpu.make_async_copy(q_ref, held, sem)
    load.start()
    put_turns(turn_ref)
    channels = taps_ref.shape[0]
    lanes = turn_ref.shape[2]
    blocks = taps_ref.shape[1] // lanes
    skip = jnp.broadcast_to(skip_ref[...], (8, channels)).T
    lane = lax.broadcasted_iota(jnp.int32, (step_rows, lanes), 1)
    for step in range(channels // step_rows):
        rows = slice(step * step_rows, (step + 1) * step_rows)
        x = [taps_ref[rows, j * lanes : (j + 1) * lanes] for j in range(blocks)]
        x[0] = x[0] + jnp.where(lane == 0, skip[rows, 0:1], 0.0)
        put_spectrum(padded_real_dft(x), turn_ref, ah, al, rows, lanes)
    per = channels // len(spec_refs)

    def one(k):
        ends = (k == 0) | (k == blocks)
        scale = jnp.where(ends, 1.0, 2.0) / (2 * blocks * lanes)
        spec = three_pass(ah[k], al[k], table_ref[0], table_ref[1], ((1,), (0,))) * scale
        for at, ref in enumerate(spec_refs):
            ref[k] = spec[at * per : (at + 1) * per].astype(bf16)

    over_frequencies(blocks + 1, one)
    load.wait()
    last_ref[...] = dot(rim_picker(held.shape[1]), held[...], ((1,), (1,))).astype(bf16)


def put_turns(turn_ref):
    _, count, lanes = turn_ref.shape
    period = 2 * (count - 1) * lanes
    k = lax.broadcasted_iota(jnp.int32, (count, lanes), 0)
    s = lax.broadcasted_iota(jnp.int32, (count, lanes), 1)
    turn = (k * s).astype(f32) * (2 * math.pi / period)
    turn_ref[0] = jnp.cos(turn)
    turn_ref[1] = jnp.sin(turn)


def table(lanes):
    s = np.arange(lanes)
    base = 2 * np.pi * (s[:, None] * s[None, :] % lanes) / lanes
    c, n = np.cos(base), np.sin(base)
    full = np.block([[c, -n], [n, c]]).astype(np.float32)
    high = full.astype(ml_dtypes.bfloat16)
    low = (full - high.astype(np.float32)).astype(ml_dtypes.bfloat16)
    return jnp.asarray(np.stack([high, low]))


def filter_spectrum(long_filter, skip_gain, table, query_input, chunks):
    channels, length = long_filter.shape
    lanes = table.shape[2] // 2
    count = length // lanes + 1
    return pl.pallas_call(
        filter_kernel,
        in_specs=[whole, whole, whole, outside],
        out_specs=[whole] * (chunks + 1),
        out_shape=[pltpu.HBM((count, channels // chunks, 2 * lanes), bf16)] * chunks
        + [pltpu.HBM((rim, query_input.shape[0]), bf16)],
        scratch_shapes=[pltpu.VMEM((count, channels, 2 * lanes), bf16)] * 2
        + [
            pltpu.VMEM((2, count, lanes), f32),
            pltpu.VMEM(query_input.shape, bf16),
            pltpu.SemaphoreType.DMA,
        ],
        compiler_params=params(24),
        cost_estimate=cost(6 * count * channels * 4 * lanes * lanes, 12 * count * channels * lanes),
        name="filter_spectrum",
    )(long_filter, skip_gain.reshape(1, channels), table, in_hbm(query_input))


def long_kernel(x_ref, spec_out, table_out, out_hbm, ah, back, spec_ref, table_ref, turn_ref, out_ref, sems):
    blocks, channels, lanes = x_ref.shape
    count = blocks + 1
    table_load = pltpu.make_async_copy(table_out.at[0], table_ref, sems.at[0])
    split = channels % (long_parts * step_rows) == 0 and count <= 33
    share = channels // long_parts if split else channels
    parts = [slice(first, first + share) for first in range(0, channels, share)]
    loads = [
        pltpu.make_async_copy(spec_out.at[:, part], spec_ref.at[:, part], sems.at[1 + at])
        for at, part in enumerate(parts)
    ]
    table_load.start()
    for copy in loads[:2]:
        copy.start()
    put_turns(turn_ref)

    def forward(rows):
        x = [x_ref[j, rows].astype(f32) for j in range(blocks)]
        put_spectrum(padded_real_dft(x), turn_ref, ah, None, rows, lanes)

    def multiply(first, size, rows):
        def take(ref):
            part = ref[pl.ds(first, size), rows]
            return part.reshape(size * part.shape[1], 2 * lanes)

        x = dot(take(ah), table_ref[...], ((1,), (0,)))
        spec = take(spec_ref).astype(f32)
        xr, xi = x[:, :lanes], x[:, lanes:]
        fr, fi = spec[:, :lanes], spec[:, lanes:]
        product = jnp.concatenate([xr * fr - xi * fi, xr * fi + xi * fr], axis=1)
        y = dot(product.astype(bf16), table_ref[...], ((1,), (1,)))
        back[pl.ds(first, size), rows] = y.reshape(size, -1, 2 * lanes)

    def backward(rows):
        spectrum = [(back[0, rows, :lanes], None)]
        for k in range(1, count):
            re, im = back[k, rows, :lanes], back[k, rows, lanes:]
            c, s = turn_ref[0, k : k + 1], turn_ref[1, k : k + 1]
            spectrum.append((re * c - im * s, None if k == blocks else re * s + im * c))
        for j, y in enumerate(padded_real_dft_adjoint(spectrum)):
            out_ref[j, rows] = y.astype(bf16)

    def store(part, at):
        return pltpu.make_async_copy(out_ref.at[:, part], out_hbm.at[:, part], sems.at[1 + long_parts + at])

    if split:
        size = max(1, 256 // share)
        steps = [[slice(r, r + step_rows) for r in range(p.start, p.stop, step_rows)] for p in parts]
        groups = [(k, min(size, count - k)) for k in range(0, count, size)]

        def together(part, others):
            done = 0
            for at, (k, many) in enumerate(groups):
                multiply(k, many, part)
                upto = len(others) * (at + 1) // len(groups)
                for body, rows in others[done:upto]:
                    body(rows)
                done = upto

        ahead = 2
        for step in steps[:ahead]:
            for rows in step:
                forward(rows)
        table_load.wait()
        for at, part in enumerate(parts):
            loads[at].wait()
            if at + 2 < len(parts):
                loads[at + 2].start()
            others = [(forward, rows) for rows in (steps[at + ahead] if at + ahead < len(parts) else [])]
            others += [(backward, rows) for rows in (steps[at - 1] if at else [])]
            together(part, others)
            if at:
                store(parts[at - 1], at - 1).start()
        for rows in steps[-1]:
            backward(rows)
        store(parts[-1], len(parts) - 1).start()
        for at, part in enumerate(parts):
            store(part, at).wait()
    else:
        everything = slice(0, channels)

        @pl.loop(0, channels // step_rows)
        def _(step):
            forward(aligned(step * step_rows, step_rows))

        table_load.wait()
        loads[0].wait()
        over_frequencies(count, lambda k: multiply(k, 1, everything))

        @pl.loop(0, channels // step_rows)
        def _(step):
            backward(aligned(step * step_rows, step_rows))

        store(everything, 0).start()
        store(everything, 0).wait()


def long_convolution(arrived, spec, table):
    blocks, channels, lanes = arrived.shape
    count = blocks + 1
    return pl.pallas_call(
        long_kernel,
        in_specs=[whole, outside, outside],
        out_specs=outside,
        out_shape=jax.ShapeDtypeStruct(arrived.shape, bf16),
        scratch_shapes=[
            pltpu.VMEM((count, channels, 2 * lanes), bf16),
            pltpu.VMEM((count, channels, 2 * lanes), f32),
            pltpu.VMEM((count, channels, 2 * lanes), bf16),
            pltpu.VMEM(table.shape[1:], bf16),
            pltpu.VMEM((2, count, lanes), f32),
            pltpu.VMEM(arrived.shape, bf16),
            pltpu.SemaphoreType.DMA((1 + 2 * long_parts,)),
        ],
        compiler_params=params(24),
        cost_estimate=cost(12 * count * channels * 4 * lanes * lanes, 12 * count * channels * lanes),
        name="long_convolution",
    )(arrived, in_hbm(spec), in_hbm(table))


def query_kernel(q_ref, before_ref, taps_ref, unembed_ref, targets_ref, ranks_ref, qs_ref, picked_ref, after_ref, space):
    rows, tokens = q_ref.shape

    @pl.loop(0, rows // tile, unroll=min(4, rows // tile))
    def _(at):
        part = aligned(at * tile, tile)
        before = before_ref[:, part].astype(f32)
        query_short = short_conv(q_ref[part], before[:rim], taps_ref, 0, part, space.at[at % 2])
        qs_ref[part] = jnp.concatenate(query_short, 0).T

    vocabulary = unembed_ref.shape[1]
    word = lax.broadcasted_iota(jnp.int32, (vocabulary, tokens), 0)
    chosen = (word == targets_ref[...]).astype(bf16)
    picked_ref[...] = dot(unembed_ref[...], chosen, ((1,), (0,))).astype(bf16)

    @pl.when(pl.program_id(0) == 0)
    def _():
        lists, size = ranks_ref.shape
        token = lax.broadcasted_iota(jnp.int32, (size, size), 0)
        rank = lax.broadcasted_iota(jnp.int32, (size, size), 1).astype(f32)
        at = [
            jnp.sum(jnp.where(token == ranks_ref[b : b + 1, :], rank, 0.0), axis=1, keepdims=True)
            for b in range(lists)
        ]
        column = jnp.concatenate(at, axis=0)
        row_of = lax.broadcasted_iota(jnp.int32, (tokens, tokens), 0)
        col_of = lax.broadcasted_iota(jnp.int32, (tokens, tokens), 1)
        row = jnp.sum(jnp.where(row_of == col_of, column, 0.0), axis=0, keepdims=True)
        same = row_of // size == col_of // size
        after_ref[...] = jnp.where(same & (row >= column), 1.0, 0.0)


def query_side(query_input, before, short_taps, unembed, targets, rankings):
    channels, tokens = query_input.shape
    width = short_taps.shape[1]
    vocabulary = unembed.shape[1]
    rows = channels // 4
    block = pl.BlockSpec((rows, tokens), lambda i: (i, 0))
    return pl.pallas_call(
        query_kernel,
        grid=(channels // rows,),
        in_specs=[
            block,
            pl.BlockSpec((rim, rows), lambda i: (0, i)),
            pl.BlockSpec((1, width, rows), lambda i: (0, 0, i)),
            pl.BlockSpec((rows, vocabulary), lambda i: (i, 0)),
            pl.BlockSpec((1, tokens), lambda i: (0, 0)),
            pl.BlockSpec(rankings.shape, lambda i: (0, 0)),
        ],
        out_specs=[block, block, pl.BlockSpec((tokens, tokens), lambda i: (0, 0))],
        out_shape=[
            pltpu.HBM((channels, tokens), f32),
            pltpu.HBM((channels, tokens), bf16),
            pltpu.HBM((tokens, tokens), f32),
        ],
        scratch_shapes=[pltpu.VMEM((2, rim + tokens, tile), f32)],
        compiler_params=params(12),
        cost_estimate=cost(2 * channels * tokens * (vocabulary + 7), channels * (8 * tokens + 2 * vocabulary)),
        name="query_side",
    )(in_hbm(query_input), before, short_taps, in_hbm(unembed), targets.reshape(1, tokens), rankings)


def result_kernel(
    size, last, first, carried_ref, qs_out, picked_out, after_out, total_ref, _, out_hbm, next_ref, loss_ref,
    qs_ref, picked_ref, out_ref, after_ref, sems, after_sem,
):
    owners, per, tokens = carried_ref.shape
    groups = sems.shape[1]
    share = owners // groups
    loads, stores = [], []
    for g in range(groups):
        part = slice(g * share, (g + 1) * share)
        rows = slice(first, first + per)
        loads.append(
            [
                pltpu.make_async_copy(qs_out.at[part, rows], qs_ref.at[part], sems.at[0, g]),
                pltpu.make_async_copy(picked_out.at[part, rows], picked_ref.at[part], sems.at[1, g]),
            ]
        )
        stores.append(pltpu.make_async_copy(out_ref.at[part], out_hbm.at[part, rows], sems.at[2, g]))
    for pair in loads:
        for copy in pair:
            copy.start()
    after_load = pltpu.make_async_copy(after_out, after_ref, after_sem)
    after_load.start()
    total = total_ref[...]
    for g in range(groups):
        for copy in loads[g]:
            copy.wait()
        part = slice(g * share, (g + 1) * share)
        out = (qs_ref[part] * carried_ref[part].astype(f32)).astype(bf16)
        out_ref[part] = out
        stores[g].start()
        terms = out.astype(f32) * picked_ref[part].astype(f32)
        total = total + jnp.sum(terms.reshape(share * per // 8, 8, tokens), axis=0)
    next_ref[...] = total
    after_load.wait()
    if last:
        logit = jnp.sum(total, axis=0, keepdims=True)
        score = soft_cap * jnp.tanh(logit / soft_cap)
        mass = jnp.sum(after_ref[...] * jnp.exp(score), axis=1, keepdims=True)
        level = jnp.log(mass)
        lists = tokens // size
        lane = lax.broadcasted_iota(jnp.int32, (1, lists), 1)
        losses = jnp.zeros((1, lists), f32)
        for b in range(lists):
            part = slice(b * size, (b + 1) * size)
            own = jnp.sum(level[part]) - jnp.sum(score[:, part])
            losses = jnp.where(lane == b, own / size, losses)
        loss_ref[...] = losses
    for copy in stores:
        copy.wait()


def result(chunk, chunks, carried, query_short, picked, after, lists, total, out):
    owners, per, tokens = carried.shape
    local = per * chunks
    groups = math.gcd(owners, 4)
    start = out is None
    if start:
        total, out = jnp.zeros((8, tokens), f32), jnp.zeros((8, tokens), bf16)
    return pl.pallas_call(
        functools.partial(result_kernel, tokens // lists, chunk == chunks - 1, chunk * per),
        in_specs=[whole, outside, outside, outside, whole, outside],
        out_specs=[outside, whole, whole],
        out_shape=[
            jax.ShapeDtypeStruct((owners, local, tokens), bf16),
            jax.ShapeDtypeStruct((8, tokens), f32),
            jax.ShapeDtypeStruct((1, lists), f32),
        ],
        scratch_shapes=[
            pltpu.VMEM((owners, per, tokens), f32),
            pltpu.VMEM((owners, per, tokens), bf16),
            pltpu.VMEM((owners, per, tokens), bf16),
            pltpu.VMEM((tokens, tokens), f32),
            pltpu.SemaphoreType.DMA((3, groups)),
            pltpu.SemaphoreType.DMA,
        ],
        input_output_aliases={} if start else {5: 0},
        compiler_params=params(8),
        cost_estimate=cost(4 * owners * per * tokens, 10 * owners * per * tokens),
        name="result",
    )(
        carried,
        in_hbm(query_short.reshape(owners, local, tokens)),
        in_hbm(picked.reshape(owners, local, tokens)),
        in_hbm(after),
        total,
        out,
    )


def per_device(
    query_input,
    key_input,
    value_input,
    short_taps,
    long_filter,
    skip_gain,
    unembed,
    targets,
    rankings,
):
    channels, tokens = query_input.shape
    owners = lax.axis_size(token_axes)
    local = channels // owners
    lists = rankings.shape[0]
    chunks = most_chunks if local % (most_chunks * tile) == 0 else 1
    last, held_key, held_value, held_taps = rims(key_input, value_input, short_taps)
    before = passed_along(last, token_axes, 1)
    inner = inner_features(held_key, held_value, held_taps)
    gated = gated_features(*inner, held_taps, before).reshape(owners, chunks, local // chunks, tokens)
    arrived = [
        lax.all_to_all(gated[:, chunk], token_axes, 0, 0, tiled=True) for chunk in range(chunks)
    ]
    transform = table(tokens)
    *specs, last_query = filter_spectrum(long_filter, skip_gain, transform, query_input, chunks)
    before_query = passed_along(last_query, token_axes, 1)
    arrived, before_query = lax.optimization_barrier((arrived, before_query))
    query_short, picked, after = query_side(query_input, before_query, short_taps, unembed, targets, rankings)
    returned = []
    for chunk in range(chunks):
        carried = long_convolution(arrived[chunk], specs[chunk], transform)
        returned.append(lax.all_to_all(carried, token_axes, 0, 0, tiled=True))
    total = out = None
    for chunk in range(chunks):
        out, total, losses = result(
            chunk, chunks, returned[chunk], query_short, picked, after, lists, total, out
        )
    return out.reshape(channels, tokens), losses.reshape(lists)


def solution(mesh):
    placed = (
        P(None, ("grp", "seq", "tile")),
        P(None, ("grp", "seq", "tile")),
        P(None, ("grp", "seq", "tile")),
        P(),
        P(("seq", "tile"), None),
        P(("seq", "tile")),
        P(),
        P(("grp", "seq", "tile")),
        P(("grp", "seq", "tile"), None),
    )
    return jax.shard_map(
        per_device,
        mesh=mesh,
        in_specs=placed,
        out_specs=(P(None, ("grp", "seq", "tile")), P(("grp", "seq", "tile"))),
        check_vma=False,
    )
```
